128 devices in a mesh: member: 8 (over y, z_hi), lat: 16 (over z_lo, x, core).
Axes of the slice: x: 4, y: 4, z: 4 (z_hi: 2, z_lo: 2; z = z_hi * 2 + z_lo), core: 2. Of those that a mesh axis runs over, the one named last changes fastest.
Arguments:
- initial_states: float32 [8, 32, 80, 128], P('member', 'lat'), may hold values from -6 to 6
- targets: float32 [2, 32, 80, 128], P(None, 'lat'), may hold values from -6 to 6
- lat_weight: float32 [32], P('lat'), may hold values from 0.3 to 3
- weight_in: float32 [256, 720], replicated, may hold values from -0.21875 to 0.21875
- weight_out: float32 [80, 2304], replicated, may hold values from -0.125 to 0.125
- hidden_bias: float32 [256], replicated, may hold values from -4 to 4
Outputs:
- state_grad: float32 [8, 32, 80, 128], P('member', 'lat')
- loss: float32 [], replicated
The draws below stay inside these ranges and needn't reach their ends.
All inputs are finite; a program needn't handle non-finite values.
Results may differ from the reference program's by a relative error of at most 0.00023.
Values sent between devices are 32-bit elements; how exact they have to be, the bound alone decides.
No kernel may reach another device: no remote copies, remote signals or barrier semaphores. Data moves between devices by JAX's collectives and lax.ppermute only.
A program may use at most 64 MiB of HBM per device.

```python
import math
import jax
import jax.numpy as jnp
from jax import lax

VARS = 80
CH = 256
LON = 128
STEPS = 2
MEMBERS = 8
NLAT = 32


def shard_levels(stream_key, extent, pieces, low, high):
    level, own = 1.0, jax.random.fold_in(stream_key, 6)
    for axis_at, parts in pieces:
        steps = jnp.exp(jax.random.uniform(jax.random.fold_in(own, axis_at), (parts,), jnp.float32, low / len(pieces), high / len(pieces)))
        level = level * jnp.repeat(steps, extent[axis_at] // parts).reshape([-1 if axis == axis_at else 1 for axis in range(len(extent))])
    return level


def gaussian(stream_key, extent, width, bound, split=(), kind=jnp.bfloat16):
    loudness = shard_levels(stream_key, extent, split, -0.22, 0.18) if split else 1.0
    array = jax.random.normal(stream_key, extent, jnp.float32) * width * loudness
    return jnp.minimum(jnp.maximum(array, -bound), bound).astype(kind)


def setup_inputs(seed: int = 0) -> dict:
    key_of = jax.random.split(jax.random.key(seed), 7)
    initial_states = gaussian(key_of[0], (MEMBERS, NLAT, VARS, LON), 1.0, 6.0, ((0, 8), (1, 16)), jnp.float32)
    targets = gaussian(key_of[1], (STEPS, NLAT, VARS, LON), 1.0, 6.0, ((1, 16),), jnp.float32)
    lat_weight = jnp.clip(jnp.exp(math.log(3.0) - 2.3025851 * jax.random.uniform(key_of[2], (NLAT,), jnp.float32) ** shard_levels(key_of[2], (NLAT,), ((0, 16),), -0.2, 0.2)), 0.3, 3.0)
    weight_in = gaussian(key_of[3], (CH, 9 * VARS), (9 * VARS) ** -0.5, 0.21875, (), jnp.float32)
    weight_out = gaussian(key_of[4], (VARS, 9 * CH), (9 * CH) ** -0.5, 0.125, (), jnp.float32)
    hidden_bias = gaussian(key_of[5], (CH,), 1.0, 4.0, (), jnp.float32)
    return dict(initial_states=initial_states, targets=targets, lat_weight=lat_weight, weight_in=weight_in, weight_out=weight_out, hidden_bias=hidden_bias)


smooth_width = 0.1

def smooth(spread):
    return jnp.sqrt(spread * spread + smooth_width * smooth_width)

def convolve(field, matrix):
    height, channels, columns = field.shape
    padded = jnp.pad(field, ((1, 1), (0, 0), (1, 1)))
    blocks = matrix.reshape(matrix.shape[0], 9, channels)
    result = jnp.zeros((height, matrix.shape[0], columns), jnp.float32)
    for across in range(3):
        for along in range(3):
            result = result + jnp.einsum('oc,rcl->rol', blocks[:, 3 * across + along], padded[across:across + height, :, along:along + columns], precision=lax.Precision.HIGHEST)
    return result

def summed_loss(initial_states, targets, lat_weight, weight_in, weight_out, hidden_bias):

    def advance(member_field):
        before = convolve(member_field, weight_in) + hidden_bias[None, :, None]
        return member_field + convolve(jax.nn.gelu(before), weight_out)
    field = initial_states
    result = jnp.zeros((), jnp.float32)
    weights = lat_weight[:, None, None]
    for rollout in range(STEPS):
        field = lax.map(advance, field)
        direct = lax.optimization_barrier(jnp.sum(smooth(field - targets[rollout][None]), axis=0))

        def pair_row(single, field=field):
            return lax.optimization_barrier(jnp.sum(smooth(single[None] - field), axis=0))
        pairs = lax.optimization_barrier(jnp.sum(lax.map(pair_row, field), axis=0))
        result = result + jnp.sum(weights * (direct - pairs / (2.0 * (MEMBERS - 1))))
    return result

def reference(initial_states, targets, lat_weight, weight_in, weight_out, hidden_bias):
    result, gradient = jax.value_and_grad(summed_loss)(initial_states, targets, lat_weight, weight_in, weight_out, hidden_bias)
    loss = result / (MEMBERS * STEPS * NLAT * VARS * LON)
    return (gradient, loss)
```

```python
import functools

import jax
import jax.numpy as jnp
from jax import lax
from jax.experimental import pallas as pl
from jax.experimental.pallas import tpu as pltpu
from jax.sharding import Mesh
from jax.sharding import PartitionSpec as P

MEMBER = ("member_0", "member_1")
LAT = ("lat_0", "lat_1", "lat_2")

smooth_width = 0.1
gelu_scale = 0.7978845608028654
gelu_cubic = 0.044715

f32 = jnp.float32
bf16 = jnp.bfloat16
params = pltpu.CompilerParams(vmem_limit_bytes=40 * 1024 * 1024)


def split(value):
    high = value.astype(bf16)
    return high, (value - high.astype(f32)).astype(bf16)


def product(left, right):
    dot = functools.partial(jnp.dot, preferred_element_type=f32)
    return dot(left[0], right[0]) + (dot(left[0], right[1]) + dot(left[1], right[0]))


def from_left(row):
    lane = lax.broadcasted_iota(jnp.int32, row.shape, 1)
    return jnp.where(lane == 0, 0.0, pltpu.roll(row, 1, 1))


def from_right(row):
    lane = lax.broadcasted_iota(jnp.int32, row.shape, 1)
    return jnp.where(lane == row.shape[1] - 1, 0.0, pltpu.roll(row, row.shape[1] - 1, 1))


def put_twice(refs, index, height, part, values):
    width = values[0].shape[1]
    size = values[0].shape[0]
    for ref, value in zip(refs, values):
        base = index * height + part * size
        if base + size <= ref.shape[0]:
            ref[base : base + size, :width] = value
        if index:
            ref[base - height : base - height + size, width:] = value


def put_windows(refs, index, row):
    height = 3 * row.shape[0]
    for part, shifted in enumerate((from_left(row), row, from_right(row))):
        put_twice(refs, index, height, part, split(shifted))


def read(refs, start, size):
    return tuple(ref[start : start + size, :] for ref in refs)


def to_channels(weights, windows, pair, channels):
    return product(weights, read(windows, pair * 3 * channels, 9 * channels))


def from_channels(weights, hidden, pair, channels, outer):
    mixed = product(weights, read(hidden, pair * channels, 3 * channels))
    width = mixed.shape[1] // 2
    rows = []
    for half in range(2):
        part = mixed[:, half * width : (half + 1) * width]
        rows.append(
            from_left(part[:outer])
            + part[outer : 2 * outer]
            + from_right(part[2 * outer :])
        )
    return rows


def gelu(x):
    return 0.5 * x * (1.0 + jnp.tanh(gelu_scale * (x + gelu_cubic * x * x * x)))


def gelu_slope(x):
    t = jnp.tanh(gelu_scale * (x + gelu_cubic * x * x * x))
    inner = gelu_scale * (1.0 + 3.0 * gelu_cubic * x * x)
    return 0.5 * (1.0 + t) + 0.5 * x * (1.0 - t * t) * inner


def prepare_kernel(win_ref, wout_ref, in_hi, in_lo, out_hi, out_lo, outb_hi, outb_lo, inb_hi, inb_lo, stack):
    outer, width = wout_ref.shape
    hidden = width // 9
    inner = win_ref.shape[1] // 9
    high, low = split(win_ref[...])
    in_hi[...] = high
    in_lo[...] = low
    for a in range(3):
        for b in range(3):
            tap = 3 * a + b
            block = wout_ref[:, tap * hidden : (tap + 1) * hidden]
            high, low = split(block)
            out_hi[b * outer : (b + 1) * outer, a * hidden : (a + 1) * hidden] = high
            out_lo[b * outer : (b + 1) * outer, a * hidden : (a + 1) * hidden] = low
            stack[(8 - tap) * outer : (9 - tap) * outer, :] = block
    high, low = split(stack[...].T)
    outb_hi[...] = high
    outb_lo[...] = low
    turned = win_ref[...].T
    for a in range(3):
        for b in range(3):
            tap = 3 * a + b
            high, low = split(turned[tap * inner : (tap + 1) * inner, :])
            j, k = 2 - a, 2 - b
            inb_hi[k * inner : (k + 1) * inner, j * hidden : (j + 1) * hidden] = high
            inb_lo[k * inner : (k + 1) * inner, j * hidden : (j + 1) * hidden] = low


def prepare(weight_in, weight_out):
    hidden, taps_in = weight_in.shape
    outer = weight_out.shape[0]
    inner = taps_in // 9
    shapes = [(hidden, 9 * inner)] * 2 + [(3 * outer, 3 * hidden)] * 2
    shapes = shapes + [(hidden, 9 * outer)] * 2 + [(3 * inner, 3 * hidden)] * 2
    return pl.pallas_call(
        prepare_kernel,
        out_shape=[jax.ShapeDtypeStruct(shape, bf16) for shape in shapes],
        scratch_shapes=[pltpu.VMEM((9 * outer, hidden), f32)],
        compiler_params=params,
        name="prepare",
    )(weight_in, weight_out)


def inside(at_ref, row, rows):
    index = at_ref[0] + row
    return (index >= 0) & (index < rows)


def forward_kernel(rows, at_ref, own_ref, near_ref, across_ref, far_across_ref, far_near_ref, bias_ref,
                   in_hi, in_lo, out_hi, out_lo, before_ref, fields_ref, wide_hi, wide_lo, hid_hi, hid_lo):
    channels, width = own_ref.shape[1:]
    hidden = in_hi.shape[0]
    even = at_ref[1] == 0
    wide = (wide_hi, wide_lo)
    hid = (hid_hi, hid_lo)
    w_in = (in_hi[...], in_lo[...])
    w_out = (out_hi[...], out_lo[...])
    bias = bias_ref[...]

    def initial(index):
        slab, row = index // 2, index % 2
        if slab == 2:
            return own_ref[row]
        first, second = {
            0: (far_across_ref, far_near_ref),
            1: (across_ref, near_ref),
            3: (near_ref, across_ref),
            4: (far_near_ref, far_across_ref),
        }[slab]
        return jnp.where(even, first[row], second[row])

    def advance(field, first, count, keep, step):
        for index in range(count):
            put_windows(wide, index, field(index))
        for pair in range(0, count - 2, 2):
            before = to_channels(w_in, wide, pair, channels) + bias
            if pair in keep:
                before_ref[step, keep.index(pair)] = before
            active = gelu(before)
            for half in range(2):
                row = active[:, half * width : (half + 1) * width]
                row = jnp.where(inside(at_ref, first + 1 + pair + half, rows), row, 0.0)
                put_twice(hid, pair + half, hidden, 0, split(row))
        result = []
        for pair in range(0, count - 4, 2):
            moved = from_channels(w_out, hid, pair, hidden, channels)
            for half in range(2):
                row = field(pair + 2 + half) + moved[half]
                result.append(jnp.where(inside(at_ref, first + 2 + pair + half, rows), row, 0.0))
        return result

    first = advance(initial, -4, 10, (2, 4), 0)
    for half in range(2):
        fields_ref[half * channels : (half + 1) * channels, :] = first[2 + half]
    second = advance(lambda index: first[index], -2, 6, (0, 2), 1)
    for half in range(2):
        fields_ref[(2 + half) * channels : (3 + half) * channels, :] = second[half]


def forward(rows, at, own, near, across, far_across, far_near, bias, w_in, w_out):
    channels, width = own.shape[1:]
    hidden = w_in[0].shape[0]
    vmem = pl.BlockSpec(memory_space=pltpu.VMEM)
    return pl.pallas_call(
        functools.partial(forward_kernel, rows),
        in_specs=[pl.BlockSpec(memory_space=pltpu.SMEM)] + [vmem] * 10,
        out_shape=[
            jax.ShapeDtypeStruct((2, 2, hidden, 2 * width), f32),
            jax.ShapeDtypeStruct((4 * channels, width), f32),
        ],
        scratch_shapes=[pltpu.VMEM((30 * channels, 2 * width), bf16)] * 2
        + [pltpu.VMEM((8 * hidden, 2 * width), bf16)] * 2,
        compiler_params=params,
        name="forward",
    )(at, own, near, across, far_across, far_near, bias, *w_in, *w_out)


def crps_kernel(at_ref, weight_ref, fields_ref, targets_ref, out_ref):
    members, height, width = fields_ref.shape
    mine = at_ref[2]
    weight = jnp.where((lax.rem(mine, 4) // 2) == 0, weight_ref[0], weight_ref[1])
    softness = smooth_width * smooth_width
    loss = jnp.zeros((8, width), f32)
    for tile in range(0, height, 8):
        values = [fields_ref[m, tile : tile + 8, :] for m in range(members)]
        truth = targets_ref[mine, tile : tile + 8, :]
        direct = jnp.zeros((8, width), f32)
        pairs = jnp.full((8, width), members * smooth_width, f32)
        slopes = [jnp.zeros((8, width), f32) for m in range(members)]
        grads = []
        for m in range(members):
            error = values[m] - truth
            spread = jnp.sqrt(error * error + softness)
            direct = direct + spread
            grads.append(error / spread)
            for other in range(m + 1, members):
                gap = values[m] - values[other]
                spread = jnp.sqrt(gap * gap + softness)
                pairs = pairs + 2.0 * spread
                slope = gap / spread
                slopes[m] = slopes[m] + slope
                slopes[other] = slopes[other] - slope
        loss = loss + weight * (direct - pairs / (2.0 * (members - 1)))
        for m in range(members):
            out_ref[m, tile : tile + 8, :] = weight * (grads[m] - slopes[m] / (members - 1))
    for m in range(members):
        out_ref[m, height : height + 8, :] = loss


def crps(at, weights, fields, targets):
    members, height, width = fields.shape
    smem = pl.BlockSpec(memory_space=pltpu.SMEM)
    vmem = pl.BlockSpec(memory_space=pltpu.VMEM)
    return pl.pallas_call(
        crps_kernel,
        in_specs=[smem, smem, vmem, vmem],
        out_shape=jax.ShapeDtypeStruct((members, height + 8, width), f32),
        compiler_params=params,
        name="crps",
    )(at, weights, fields, targets)


def backward_kernel(rows, step, at_ref, own_ref, near_ref, across_ref, before_ref, outb_hi, outb_lo, inb_hi, inb_lo,
                    *rest):
    added = rest[:-5]
    out_ref, wide_hi, wide_lo, hid_hi, hid_lo = rest[-5:]
    channels, width = own_ref.shape[1:]
    hidden = outb_hi.shape[0]
    even = at_ref[1] == 0
    wide = (wide_hi, wide_lo)
    hid = (hid_hi, hid_lo)
    w_out = (outb_hi[...], outb_lo[...])
    w_in = (inb_hi[...], inb_lo[...])
    for row in range(2):
        put_windows(wide, row, jnp.where(even, across_ref[row], near_ref[row]))
        put_windows(wide, 2 + row, own_ref[row])
    for row in range(2):
        put_windows(wide, 4 + row, jnp.where(even, near_ref[row], across_ref[row]))
    for pair in (0, 2):
        grads = to_channels(w_out, wide, pair, channels) * gelu_slope(before_ref[step, pair // 2])
        for half in range(2):
            row = grads[:, half * width : (half + 1) * width]
            row = jnp.where(inside(at_ref, pair + half - 1, rows), row, 0.0)
            put_twice(hid, pair + half, hidden, 0, split(row))
    moved = from_channels(w_in, hid, 0, hidden, channels)
    for row in range(2):
        total = own_ref[row] + moved[row]
        for extra in added:
            total = total + extra[row]
        out_ref[row] = total


def backward(rows, step, at, own, near, across, before, w_out, w_in, *added):
    channels, width = own.shape[1:]
    hidden = w_out[0].shape[0]
    vmem = pl.BlockSpec(memory_space=pltpu.VMEM)
    return pl.pallas_call(
        functools.partial(backward_kernel, rows, step),
        in_specs=[pl.BlockSpec(memory_space=pltpu.SMEM)] + [vmem] * (8 + len(added)),
        out_shape=jax.ShapeDtypeStruct((2, channels, width), f32),
        scratch_shapes=[pltpu.VMEM((18 * channels, 2 * width), bf16)] * 2
        + [pltpu.VMEM((4 * hidden, 2 * width), bf16)] * 2,
        compiler_params=params,
        name="backward",
    )(at, own, near, across, before, *w_out, *w_in, *added)


def on_device(initial_states, targets, lat_weight, weight_in, weight_out, hidden_bias):
    members = lax.axis_size(MEMBER)
    slabs = lax.axis_size(LAT)
    steps, slab_rows, channels, width = targets.shape
    rows = slabs * slab_rows
    near = [(i, i ^ 1) for i in range(slabs)]
    across = [(i, i + 1 if i % 2 else i - 1) for i in range(1, slabs - 1)]

    slab = lax.axis_index(LAT)
    at = jnp.stack([slab * slab_rows, lax.rem(slab, 2), lax.axis_index(MEMBER)]).astype(jnp.int32)
    own = initial_states[0]
    beside = lax.ppermute(own, LAT, near)
    crossed = lax.ppermute(own, LAT, across)
    far_crossed = lax.ppermute(beside, LAT, across)
    far_beside = lax.ppermute(crossed, LAT, near)
    ready = prepare(weight_in, weight_out)
    w_in, w_out, w_out_back, w_in_back = (ready[2 * i : 2 * i + 2] for i in range(4))
    bias = hidden_bias[:, None]
    before, fields = forward(
        rows, at, own, beside, crossed, far_crossed, far_beside, bias, w_in, w_out
    )
    height = steps * slab_rows * channels // members
    chunks = lax.all_to_all(
        fields.reshape(members, height, width), MEMBER, split_axis=0, concat_axis=0, tiled=True
    )
    grads = crps(at, lat_weight, chunks, targets.reshape(members, height, width))
    grads = lax.all_to_all(grads, MEMBER, split_axis=0, concat_axis=0, tiled=True)
    partial = jnp.sum(grads[:, height:, :], axis=0)
    loss_grads = grads[:, :height, :].reshape(steps, slab_rows, channels, width)

    total = partial
    total = total + lax.ppermute(total, LAT, near)
    for turn in (2, 6, 8):
        total = total + lax.ppermute(total, LAT, [(i, i ^ turn) for i in range(slabs)])
    loss = jnp.sum(total) / (members * steps * rows * channels * width)

    gradient = loss_grads[1]
    beside = lax.ppermute(gradient, LAT, near)
    crossed = lax.ppermute(gradient, LAT, across)
    gradient = backward(
        rows, 1, at, gradient, beside, crossed, before, w_out_back, w_in_back, loss_grads[0]
    )
    beside = lax.ppermute(gradient, LAT, near)
    crossed = lax.ppermute(gradient, LAT, across)
    gradient = backward(rows, 0, at, gradient, beside, crossed, before, w_out_back, w_in_back)
    return gradient[None], loss


def solution(mesh):
    torus = Mesh(
        mesh.devices.reshape(4, 2, 2, 4, 2), ("member_0", "member_1", "lat_0", "lat_1", "lat_2")
    )
    placed = (P(MEMBER, LAT, None, None), P(None, LAT, None, None), P(LAT), P(), P(), P())
    return jax.shard_map(
        on_device,
        mesh=torus,
        in_specs=placed,
        out_specs=(P(MEMBER, LAT, None, None), P()),
        check_vma=False,
    )
```

```python
import functools

import jax
import jax.numpy as jnp
from jax import lax
from jax.experimental import pallas as pl
from jax.experimental.pallas import tpu as pltpu
from jax.sharding import Mesh
from jax.sharding import PartitionSpec as P

MEMBER = ("member_0", "member_1")
LAT = ("lat_0", "lat_1", "lat_2")

smooth_width = 0.1
gelu_scale = 0.7978845608028654
gelu_cubic = 0.044715
slab_count = 16

f32 = jnp.float32
bf16 = jnp.bfloat16
params = pltpu.CompilerParams(vmem_limit_bytes=16 * 1024 * 1024)


def split(value):
    high = value.astype(bf16)
    return high, (value - high.astype(f32)).astype(bf16)


def product(left, right):
    dot = functools.partial(jnp.dot, preferred_element_type=f32)
    return dot(left[0], right[0]) + (dot(left[0], right[1]) + dot(left[1], right[0]))


def from_left(row):
    lane = lax.broadcasted_iota(jnp.int32, row.shape, 1)
    return jnp.where(lane == 0, 0.0, pltpu.roll(row, 1, 1))


def from_right(row):
    lane = lax.broadcasted_iota(jnp.int32, row.shape, 1)
    return jnp.where(lane == row.shape[1] - 1, 0.0, pltpu.roll(row, row.shape[1] - 1, 1))


def put_twice(refs, index, height, part, values):
    width = values[0].shape[1]
    size = values[0].shape[0]
    for ref, value in zip(refs, values):
        base = index * height + part * size
        if base + size <= ref.shape[0]:
            ref[base : base + size, :width] = value
        if index:
            ref[base - height : base - height + size, width:] = value


def put_windows(refs, index, row):
    height = 3 * row.shape[0]
    for part, shifted in enumerate((from_left(row), row, from_right(row))):
        put_twice(refs, index, height, part, split(shifted))


def read(refs, start, size):
    return tuple(ref[start : start + size, :] for ref in refs)


def to_channels(weights, windows, pair, channels):
    return product(weights, read(windows, pair * 3 * channels, 9 * channels))


def from_channels(weights, hidden, pair, channels, outer):
    mixed = product(weights, read(hidden, pair * channels, 3 * channels))
    width = mixed.shape[1] // 2
    rows = []
    for half in range(2):
        part = mixed[:, half * width : (half + 1) * width]
        rows.append(
            from_left(part[:outer])
            + part[outer : 2 * outer]
            + from_right(part[2 * outer :])
        )
    return rows


def gelu(x):
    return 0.5 * x * (1.0 + jnp.tanh(gelu_scale * (x + gelu_cubic * x * x * x)))


def gelu_slope(x):
    t = jnp.tanh(gelu_scale * (x + gelu_cubic * x * x * x))
    inner = gelu_scale * (1.0 + 3.0 * gelu_cubic * x * x)
    return 0.5 * (1.0 + t) + 0.5 * x * (1.0 - t * t) * inner


def prepare_kernel(win_hbm, wout_hbm, bias_hbm, in_hi, in_lo, out_hi, out_lo, outb_hi, outb_lo, inb_hi, inb_lo,
                   wide_bias_ref, stack, win_ref, wout_ref, bias_ref, arrived):
    pairs = ((win_hbm, win_ref), (wout_hbm, wout_ref), (bias_hbm, bias_ref))
    copies = [pltpu.make_async_copy(*pair, arrived.at[i]) for i, pair in enumerate(pairs)]
    for copy in copies:
        copy.start()
    for copy in copies:
        copy.wait()
    outer, width = wout_ref.shape
    hidden = width // 9
    inner = win_ref.shape[0] // 9
    high, low = split(win_ref[...].T)
    in_hi[...] = high
    in_lo[...] = low
    for a in range(3):
        for b in range(3):
            tap = 3 * a + b
            block = wout_ref[:, tap * hidden : (tap + 1) * hidden]
            high, low = split(block)
            out_hi[b * outer : (b + 1) * outer, a * hidden : (a + 1) * hidden] = high
            out_lo[b * outer : (b + 1) * outer, a * hidden : (a + 1) * hidden] = low
            stack[(8 - tap) * outer : (9 - tap) * outer, :] = block
            high, low = split(win_ref[tap * inner : (tap + 1) * inner, :])
            j, k = 2 - a, 2 - b
            inb_hi[k * inner : (k + 1) * inner, j * hidden : (j + 1) * hidden] = high
            inb_lo[k * inner : (k + 1) * inner, j * hidden : (j + 1) * hidden] = low
    high, low = split(stack[...].T)
    outb_hi[...] = high
    outb_lo[...] = low
    wide_bias_ref[...] = jnp.broadcast_to(bias_ref[...], wide_bias_ref.shape[::-1]).T


def prepare(weight_in, weight_out, bias, width):
    taps_in, hidden = weight_in.shape
    outer = weight_out.shape[0]
    inner = taps_in // 9
    shapes = [(hidden, 9 * inner)] * 2 + [(3 * outer, 3 * hidden)] * 2
    shapes = shapes + [(hidden, 9 * outer)] * 2 + [(3 * inner, 3 * hidden)] * 2
    return pl.pallas_call(
        prepare_kernel,
        out_shape=[jax.ShapeDtypeStruct(shape, bf16) for shape in shapes]
        + [jax.ShapeDtypeStruct((hidden, width), f32)],
        in_specs=[pl.BlockSpec(memory_space=pltpu.HBM)] * 3,
        scratch_shapes=[
            pltpu.VMEM((9 * outer, hidden), f32),
            pltpu.VMEM(weight_in.shape, f32),
            pltpu.VMEM(weight_out.shape, f32),
            pltpu.VMEM(bias.shape, f32),
            pltpu.SemaphoreType.DMA((3,)),
        ],
        compiler_params=params,
        name="prepare",
    )(weight_in, weight_out, bias)


def inside(at_ref, row, rows):
    index = at_ref[0] + row
    return (index >= 0) & (index < rows)


def forward_kernel(rows, at_ref, own_ref, near_ref, across_ref, far_across_ref, far_near_ref, bias_ref,
                   in_hi, in_lo, out_hi, out_lo, before_ref, fields_ref, wide_hi, wide_lo, hid_hi, hid_lo):
    channels, width = own_ref.shape[1:]
    hidden = in_hi.shape[0]
    even = at_ref[1] == 0
    wide = (wide_hi, wide_lo)
    hid = (hid_hi, hid_lo)
    w_in = (in_hi[...], in_lo[...])
    w_out = (out_hi[...], out_lo[...])
    bias = jnp.concatenate([bias_ref[...]] * 2, axis=1)

    def initial(index):
        slab, row = index // 2, index % 2
        if slab == 2:
            return own_ref[row]
        first, second = {
            0: (far_across_ref, far_near_ref),
            1: (across_ref, near_ref),
            3: (near_ref, across_ref),
            4: (far_near_ref, far_across_ref),
        }[slab]
        value = jnp.where(even, first[row], second[row])
        return jnp.where(inside(at_ref, index - 4, rows), value, 0.0)

    def advance(field, first, count, keep, step):
        for index in range(count):
            put_windows(wide, index, field(index))
        for pair in range(0, count - 2, 2):
            before = to_channels(w_in, wide, pair, channels) + bias
            if pair in keep:
                before_ref[step, keep.index(pair)] = before
            active = gelu(before)
            for half in range(2):
                row = active[:, half * width : (half + 1) * width]
                row = jnp.where(inside(at_ref, first + 1 + pair + half, rows), row, 0.0)
                put_twice(hid, pair + half, hidden, 0, split(row))
        result = []
        for pair in range(0, count - 4, 2):
            moved = from_channels(w_out, hid, pair, hidden, channels)
            for half in range(2):
                row = field(pair + 2 + half) + moved[half]
                result.append(jnp.where(inside(at_ref, first + 2 + pair + half, rows), row, 0.0))
        return result

    first = advance(initial, -4, 10, (2, 4), 0)
    for half in range(2):
        fields_ref[half * channels : (half + 1) * channels, :] = first[2 + half]
    second = advance(lambda index: first[index], -2, 6, (0, 2), 1)
    for half in range(2):
        fields_ref[(2 + half) * channels : (3 + half) * channels, :] = second[half]


def forward(rows, at, own, near, across, far_across, far_near, bias, w_in, w_out):
    channels, width = own.shape[1:]
    hidden = w_in[0].shape[0]
    vmem = pl.BlockSpec(memory_space=pltpu.VMEM)
    return pl.pallas_call(
        functools.partial(forward_kernel, rows),
        in_specs=[pl.BlockSpec(memory_space=pltpu.SMEM)] + [vmem] * 10,
        out_shape=[
            jax.ShapeDtypeStruct((2, 2, hidden, 2 * width), f32),
            jax.ShapeDtypeStruct((4 * channels, width), f32),
        ],
        scratch_shapes=[pltpu.VMEM((30 * channels, 2 * width), bf16)] * 2
        + [pltpu.VMEM((8 * hidden, 2 * width), bf16)] * 2,
        compiler_params=params,
        name="forward",
    )(at, own, near, across, far_across, far_near, bias, *w_in, *w_out)


def crps_kernel(at_ref, weight_ref, fields_ref, targets_ref, out_ref):
    members, height, width = fields_ref.shape
    mine = at_ref[2]
    weight = jnp.where((lax.rem(mine, 4) // 2) == 0, weight_ref[0], weight_ref[1])
    softness = smooth_width * smooth_width
    loss = jnp.zeros((8, width), f32)
    for tile in range(0, height, 8):
        values = [fields_ref[m, tile : tile + 8, :] for m in range(members)]
        truth = targets_ref[mine, tile : tile + 8, :]
        direct = jnp.zeros((8, width), f32)
        pairs = jnp.full((8, width), members * smooth_width, f32)
        slopes = [jnp.zeros((8, width), f32) for m in range(members)]
        grads = []
        for m in range(members):
            error = values[m] - truth
            spread = jnp.sqrt(error * error + softness)
            direct = direct + spread
            grads.append(error / spread)
            for other in range(m + 1, members):
                gap = values[m] - values[other]
                spread = jnp.sqrt(gap * gap + softness)
                pairs = pairs + 2.0 * spread
                slope = gap / spread
                slopes[m] = slopes[m] + slope
                slopes[other] = slopes[other] - slope
        loss = loss + weight * (direct - pairs / (2.0 * (members - 1)))
        for m in range(members):
            out_ref[m, tile : tile + 8, :] = weight * (grads[m] - slopes[m] / (members - 1))
    for m in range(members):
        out_ref[m, height : height + 8, :] = loss


def crps(at, weights, fields, targets):
    members, height, width = fields.shape
    smem = pl.BlockSpec(memory_space=pltpu.SMEM)
    vmem = pl.BlockSpec(memory_space=pltpu.VMEM)
    return pl.pallas_call(
        crps_kernel,
        in_specs=[smem, smem, vmem, vmem],
        out_shape=jax.ShapeDtypeStruct((members, height + 8, width), f32),
        compiler_params=params,
        name="crps",
    )(at, weights, fields, targets)


def collect_kernel(at_ref, grads_ref, first_ref, second_ref):
    chunks, height, width = grads_ref.shape
    height = height - 8
    half = chunks // 2
    total = grads_ref[0, height : height + 8, :]
    for chunk in range(1, chunks):
        total = total + grads_ref[chunk, height : height + 8, :]
    for chunk in range(half):
        first_ref[chunk * height : (chunk + 1) * height, :] = grads_ref[chunk, :height, :]
        second_ref[chunk * height : (chunk + 1) * height, :] = grads_ref[half + chunk, :height, :]
    known = jnp.broadcast_to(jnp.sum(total, axis=0, keepdims=True), (slab_count, width))
    slab = lax.broadcasted_iota(jnp.int32, known.shape, 0)
    second_ref[half * height :, :] = jnp.where(slab == at_ref[3], known, 0.0)


def collect(at, grads):
    chunks, height, width = grads.shape
    count = chunks // 2 * (height - 8)
    vmem = pl.BlockSpec(memory_space=pltpu.VMEM)
    return pl.pallas_call(
        collect_kernel,
        in_specs=[pl.BlockSpec(memory_space=pltpu.SMEM), vmem],
        out_shape=[
            jax.ShapeDtypeStruct((count, width), f32),
            jax.ShapeDtypeStruct((count + slab_count, width), f32),
        ],
        compiler_params=params,
        name="collect",
    )(at, grads)


def merged(*known):
    result = known[0]
    for other in known[1:]:
        result = jnp.where(result != 0.0, result, other)
    return result


def merge_kernel(own_ref, near_ref, across_ref, far_ref, out_ref):
    count = own_ref.shape[0] - slab_count
    out_ref[...] = merged(own_ref[count:, :], near_ref[count:, :], across_ref[count:, :], far_ref[...])


def merge(own, near, across, far):
    return pl.pallas_call(
        merge_kernel,
        out_shape=jax.ShapeDtypeStruct(far.shape, f32),
        compiler_params=params,
        name="merge",
    )(own, near, across, far)


def slopes_kernel(before_ref, out_ref):
    for step in range(2):
        for pair in range(2):
            out_ref[step, pair] = gelu_slope(before_ref[step, pair])


def slopes_of(before):
    return pl.pallas_call(
        slopes_kernel,
        out_shape=jax.ShapeDtypeStruct(before.shape, f32),
        compiler_params=params,
        name="slopes",
    )(before)


def backward_kernel(rows, step, at_ref, own_ref, near_ref, across_ref, slope_ref, outb_hi, outb_lo, inb_hi, inb_lo,
                    *rest):
    outs = 1 + step
    added = rest[: -4 - outs]
    out_ref, *known_ref = rest[-4 - outs : -4]
    wide_hi, wide_lo, hid_hi, hid_lo = rest[-4:]
    width = own_ref.shape[1]
    channels = (own_ref.shape[0] - slab_count) // 2
    hidden = outb_hi.shape[0]
    even = at_ref[1] == 0
    wide = (wide_hi, wide_lo)
    hid = (hid_hi, hid_lo)
    w_out = (outb_hi[...], outb_lo[...])
    w_in = (inb_hi[...], inb_lo[...])

    def take(ref, row):
        return ref[row * channels : (row + 1) * channels, :]

    def put_beside(index, first, second, row):
        value = jnp.where(even, take(first, row), take(second, row))
        value = jnp.where(inside(at_ref, index - 2, rows), value, 0.0)
        put_windows(wide, index, value)

    for row in range(2):
        put_windows(wide, 2 + row, take(own_ref, row))
    for row in range(2):
        put_beside(row, across_ref, near_ref, row)
        put_beside(4 + row, near_ref, across_ref, row)
    for pair in (0, 2):
        grads = to_channels(w_out, wide, pair, channels) * slope_ref[step, pair // 2]
        for half in range(2):
            row = grads[:, half * width : (half + 1) * width]
            row = jnp.where(inside(at_ref, pair + half - 1, rows), row, 0.0)
            put_twice(hid, pair + half, hidden, 0, split(row))
    moved = from_channels(w_in, hid, 0, hidden, channels)
    for row in range(2):
        total = take(own_ref, row) + moved[row]
        for extra in added:
            total = total + take(extra, row)
        out_ref[row * channels : (row + 1) * channels, :] = total
    if known_ref:
        last = 2 * channels
        known = merged(own_ref[last:, :], near_ref[last:, :], across_ref[last:, :])
        out_ref[last:, :] = known
        known_ref[0][...] = known


def backward(rows, step, at, own, near, across, slopes, w_out, w_in, *added):
    count, width = own.shape
    channels = (count - slab_count) // 2
    hidden = w_out[0].shape[0]
    vmem = pl.BlockSpec(memory_space=pltpu.VMEM)
    return pl.pallas_call(
        functools.partial(backward_kernel, rows, step),
        in_specs=[pl.BlockSpec(memory_space=pltpu.SMEM)] + [vmem] * (8 + len(added)),
        out_shape=[jax.ShapeDtypeStruct((count if step else 2 * channels, width), f32)]
        + [jax.ShapeDtypeStruct((slab_count, width), f32)] * step,
        scratch_shapes=[pltpu.VMEM((18 * channels, 2 * width), bf16)] * 2
        + [pltpu.VMEM((4 * hidden, 2 * width), bf16)] * 2,
        compiler_params=params,
        name="backward",
    )(at, own, near, across, slopes, *w_out, *w_in, *added)


def on_device(initial_states, targets, lat_weight, weight_in, weight_out, hidden_bias):
    members = lax.axis_size(MEMBER)
    slabs = lax.axis_size(LAT)
    steps, slab_rows, channels, width = targets.shape
    rows = slabs * slab_rows
    near = [(i, i ^ 1) for i in range(slabs)]
    across = [(i, (i + 1 if i % 2 else i - 1) % slabs) for i in range(slabs)]

    slab = lax.axis_index(LAT)
    at = [slab * slab_rows, lax.rem(slab, 2), lax.axis_index(MEMBER), slab]
    at = jnp.stack(at).astype(jnp.int32)
    own = initial_states[0]
    beside = lax.ppermute(own, LAT, near)
    crossed = lax.ppermute(own, LAT, across)
    far_crossed = lax.ppermute(beside, LAT, across)
    crossed, beside = lax.optimization_barrier((crossed, beside))
    far_beside = lax.ppermute(crossed, LAT, near)
    far_beside, weight_out = lax.optimization_barrier((far_beside, weight_out))
    ready = prepare(weight_in.T, weight_out, hidden_bias[None, :], width)
    w_in, w_out, w_out_back, w_in_back = (ready[2 * i : 2 * i + 2] for i in range(4))
    before, fields = forward(
        rows, at, own, beside, crossed, far_crossed, far_beside, ready[8], w_in, w_out
    )
    height = steps * slab_rows * channels // members
    chunks = lax.all_to_all(
        fields.reshape(members, height, width), MEMBER, split_axis=0, concat_axis=0, tiled=True
    )
    grads = crps(at, lat_weight, chunks, targets.reshape(members, height, width))
    grads = lax.all_to_all(grads, MEMBER, split_axis=0, concat_axis=0, tiled=True)
    grads, before = lax.optimization_barrier((grads, before))
    slopes = slopes_of(before)
    first_grads, message = collect(at, grads)

    beside = lax.ppermute(message, LAT, near)
    crossed = lax.ppermute(message, LAT, across)
    message, known = backward(
        rows, 1, at, message, beside, crossed, slopes, w_out_back, w_in_back, first_grads
    )
    beside = lax.ppermute(message, LAT, near)
    crossed = lax.ppermute(message, LAT, across)
    far = lax.ppermute(known, LAT, [(i, i ^ 4) for i in range(slabs)])
    known = merge(message, beside, crossed, far)
    (gradient,) = backward(rows, 0, at, message, beside, crossed, slopes, w_out_back, w_in_back)
    opposite = lax.ppermute(known, LAT, [(i, i ^ 8) for i in range(slabs)])
    total = jnp.sum(jnp.where(known != 0.0, known, opposite))
    loss = total / (members * steps * rows * channels * width)
    return gradient.reshape(initial_states.shape), loss


def solution(mesh):
    torus = Mesh(
        mesh.devices.reshape(4, 2, 2, 4, 2), ("member_0", "member_1", "lat_0", "lat_1", "lat_2")
    )
    placed = (P(MEMBER, LAT, None, None), P(None, LAT, None, None), P(LAT), P(), P(), P())
    return jax.shard_map(
        on_device,
        mesh=torus,
        in_specs=placed,
        out_specs=(P(MEMBER, LAT, None, None), P()),
        check_vma=False,
    )
```

```python
import functools

import jax
import jax.numpy as jnp
from jax import lax
from jax.experimental import pallas as pl
from jax.experimental.pallas import tpu as pltpu
from jax.sharding import Mesh
from jax.sharding import PartitionSpec as P

MEMBER = ("member_0", "member_1")
LAT = ("lat_0", "lat_1", "lat_2")

smooth_width = 0.1
gelu_scale = 0.7978845608028654
gelu_cubic = 0.044715
slab_count = 16

f32 = jnp.float32
bf16 = jnp.bfloat16
params = pltpu.CompilerParams(vmem_limit_bytes=16 * 1024 * 1024)


def split(value):
    high = value.astype(bf16)
    return high, (value - high.astype(f32)).astype(bf16)


def product(left, right):
    dot = functools.partial(jnp.dot, preferred_element_type=f32)
    return dot(left[0], right[0]) + (dot(left[0], right[1]) + dot(left[1], right[0]))


def from_left(row):
    lane = lax.broadcasted_iota(jnp.int32, row.shape, 1)
    return jnp.where(lane == 0, 0.0, pltpu.roll(row, 1, 1))


def from_right(row):
    lane = lax.broadcasted_iota(jnp.int32, row.shape, 1)
    return jnp.where(lane == row.shape[1] - 1, 0.0, pltpu.roll(row, row.shape[1] - 1, 1))


def put_twice(refs, index, height, part, values):
    width = values[0].shape[1]
    size = values[0].shape[0]
    for ref, value in zip(refs, values):
        base = index * height + part * size
        if base + size <= ref.shape[0]:
            ref[base : base + size, :width] = value
        if index:
            ref[base - height : base - height + size, width:] = value


def put_windows(refs, index, row):
    height = 3 * row.shape[0]
    for part, shifted in enumerate((from_left(row), row, from_right(row))):
        put_twice(refs, index, height, part, split(shifted))


def read(refs, start, size):
    return tuple(ref[start : start + size, :] for ref in refs)


def to_channels(weights, windows, pair, channels):
    return product(weights, read(windows, pair * 3 * channels, 9 * channels))


def from_channels(weights, hidden, pair, channels, outer):
    mixed = product(weights, read(hidden, pair * channels, 3 * channels))
    width = mixed.shape[1] // 2
    rows = []
    for half in range(2):
        part = mixed[:, half * width : (half + 1) * width]
        rows.append(
            from_left(part[:outer])
            + part[outer : 2 * outer]
            + from_right(part[2 * outer :])
        )
    return rows


def gelu(x):
    return 0.5 * x * (1.0 + jnp.tanh(gelu_scale * (x + gelu_cubic * x * x * x)))


def gelu_slope(x):
    t = jnp.tanh(gelu_scale * (x + gelu_cubic * x * x * x))
    inner = gelu_scale * (1.0 + 3.0 * gelu_cubic * x * x)
    return 0.5 * (1.0 + t) + 0.5 * x * (1.0 - t * t) * inner


def fetch(pairs, arrived):
    copies = [pltpu.make_async_copy(*pair, arrived.at[i]) for i, pair in enumerate(pairs)]
    for copy in copies:
        copy.start()
    for copy in copies:
        copy.wait()


def prepare_kernel(win_hbm, wout_hbm, bias_hbm, lat_hbm, in_hi, in_lo, out_hi, out_lo, wide_bias_ref, wide_lat_ref,
                   win_ref, wout_ref, bias_ref, lat_ref, arrived):
    fetch(((win_hbm, win_ref), (wout_hbm, wout_ref), (bias_hbm, bias_ref), (lat_hbm, lat_ref)), arrived)
    outer, width = wout_ref.shape
    hidden = width // 9
    high, low = split(win_ref[...].T)
    in_hi[...] = high
    in_lo[...] = low
    for a in range(3):
        for b in range(3):
            tap = 3 * a + b
            high, low = split(wout_ref[:, tap * hidden : (tap + 1) * hidden])
            out_hi[b * outer : (b + 1) * outer, a * hidden : (a + 1) * hidden] = high
            out_lo[b * outer : (b + 1) * outer, a * hidden : (a + 1) * hidden] = low
    wide_bias_ref[...] = jnp.broadcast_to(bias_ref[...], wide_bias_ref.shape[::-1]).T
    for row in range(2):
        one = jnp.broadcast_to(lat_ref[:, row : row + 1], (8, wide_lat_ref.shape[1]))
        wide_lat_ref[8 * row : 8 * (row + 1), :] = one


def prepare(weight_in, weight_out, bias, lat_weight, width):
    taps_in, hidden = weight_in.shape
    outer = weight_out.shape[0]
    arrays = (weight_in, weight_out, bias, lat_weight)
    shapes = [(hidden, taps_in)] * 2 + [(3 * outer, 3 * hidden)] * 2
    return pl.pallas_call(
        prepare_kernel,
        out_shape=[jax.ShapeDtypeStruct(shape, bf16) for shape in shapes]
        + [jax.ShapeDtypeStruct((hidden, width), f32), jax.ShapeDtypeStruct((16, width), f32)],
        in_specs=[pl.BlockSpec(memory_space=pltpu.HBM)] * 4,
        scratch_shapes=[pltpu.VMEM(array.shape, f32) for array in arrays] + [pltpu.SemaphoreType.DMA((4,))],
        compiler_params=params,
        name="prepare",
    )(*(pltpu.with_memory_space_constraint(array, pltpu.HBM) for array in arrays))


def prepare_back_kernel(win_hbm, wout_hbm, before_ref, outb_hi, outb_lo, inb_hi, inb_lo, slope_ref,
                        stack, win_ref, wout_ref, arrived):
    pairs = ((win_hbm, win_ref), (wout_hbm, wout_ref))
    copies = [pltpu.make_async_copy(*pair, arrived.at[i]) for i, pair in enumerate(pairs)]
    for copy in copies:
        copy.start()
    for step in range(2):
        for pair in range(2):
            slope_ref[step, pair] = gelu_slope(before_ref[step, pair])
    for copy in copies:
        copy.wait()
    outer, width = wout_ref.shape
    hidden = width // 9
    inner = win_ref.shape[0] // 9
    for a in range(3):
        for b in range(3):
            tap = 3 * a + b
            stack[(8 - tap) * outer : (9 - tap) * outer, :] = wout_ref[:, tap * hidden : (tap + 1) * hidden]
            high, low = split(win_ref[tap * inner : (tap + 1) * inner, :])
            j, k = 2 - a, 2 - b
            inb_hi[k * inner : (k + 1) * inner, j * hidden : (j + 1) * hidden] = high
            inb_lo[k * inner : (k + 1) * inner, j * hidden : (j + 1) * hidden] = low
    high, low = split(stack[...].T)
    outb_hi[...] = high
    outb_lo[...] = low


def prepare_back(weight_in, weight_out, before):
    taps_in, hidden = weight_in.shape
    outer = weight_out.shape[0]
    inner = taps_in // 9
    arrays = (weight_in, weight_out)
    shapes = [(hidden, 9 * outer)] * 2 + [(3 * inner, 3 * hidden)] * 2
    hbm = pl.BlockSpec(memory_space=pltpu.HBM)
    return pl.pallas_call(
        prepare_back_kernel,
        out_shape=[jax.ShapeDtypeStruct(shape, bf16) for shape in shapes]
        + [jax.ShapeDtypeStruct(before.shape, f32)],
        in_specs=[hbm, hbm, pl.BlockSpec(memory_space=pltpu.VMEM)],
        scratch_shapes=[pltpu.VMEM((9 * outer, hidden), f32)]
        + [pltpu.VMEM(array.shape, f32) for array in arrays]
        + [pltpu.SemaphoreType.DMA((2,))],
        compiler_params=params,
        name="prepare_back",
    )(*(pltpu.with_memory_space_constraint(array, pltpu.HBM) for array in arrays), before)


def inside(row):
    index = lax.axis_index(LAT) * 2 + row
    return (index >= 0) & (index < 2 * slab_count)


def is_even():
    return lax.rem(lax.axis_index(LAT), 2) == 0


def forward_kernel(own_ref, near_ref, across_ref, far_across_ref, far_near_ref, bias_ref,
                   in_hi, in_lo, out_hi, out_lo, before_ref, fields_ref, wide_hi, wide_lo, hid_hi, hid_lo):
    channels, width = own_ref.shape[1:]
    hidden = in_hi.shape[0]
    even = is_even()
    wide = (wide_hi, wide_lo)
    hid = (hid_hi, hid_lo)
    w_in = (in_hi[...], in_lo[...])
    w_out = (out_hi[...], out_lo[...])
    bias = jnp.concatenate([bias_ref[...]] * 2, axis=1)

    def initial(index):
        slab, row = index // 2, index % 2
        if slab == 2:
            return own_ref[row]
        first, second = {
            0: (far_across_ref, far_near_ref),
            1: (across_ref, near_ref),
            3: (near_ref, across_ref),
            4: (far_near_ref, far_across_ref),
        }[slab]
        value = jnp.where(even, first[row], second[row])
        return jnp.where(inside(index - 4), value, 0.0)

    def advance(field, first, count, keep, step):
        for index in range(count):
            put_windows(wide, index, field(index))
        for pair in range(0, count - 2, 2):
            before = to_channels(w_in, wide, pair, channels) + bias
            if pair in keep:
                before_ref[step, keep.index(pair)] = before
            active = gelu(before)
            for half in range(2):
                row = active[:, half * width : (half + 1) * width]
                row = jnp.where(inside(first + 1 + pair + half), row, 0.0)
                put_twice(hid, pair + half, hidden, 0, split(row))
        result = []
        for pair in range(0, count - 4, 2):
            moved = from_channels(w_out, hid, pair, hidden, channels)
            for half in range(2):
                row = field(pair + 2 + half) + moved[half]
                result.append(jnp.where(inside(first + 2 + pair + half), row, 0.0))
        return result

    first = advance(initial, -4, 10, (2, 4), 0)
    for half in range(2):
        fields_ref[half * channels : (half + 1) * channels, :] = first[2 + half]
    second = advance(lambda index: first[index], -2, 6, (0, 2), 1)
    for half in range(2):
        fields_ref[(2 + half) * channels : (3 + half) * channels, :] = second[half]


def forward(own, near, across, far_across, far_near, bias, w_in, w_out):
    channels, width = own.shape[1:]
    hidden = w_in[0].shape[0]
    vmem = pl.BlockSpec(memory_space=pltpu.VMEM)
    return pl.pallas_call(
        forward_kernel,
        in_specs=[vmem] * 10,
        out_shape=[
            jax.ShapeDtypeStruct((2, 2, hidden, 2 * width), f32),
            jax.ShapeDtypeStruct((4 * channels, width), f32),
        ],
        scratch_shapes=[pltpu.VMEM((30 * channels, 2 * width), bf16)] * 2
        + [pltpu.VMEM((8 * hidden, 2 * width), bf16)] * 2,
        compiler_params=params,
        name="forward",
    )(own, near, across, far_across, far_near, bias, *w_in, *w_out)


def crps_kernel(weight_ref, fields_ref, targets_ref, out_ref):
    members, height, width = fields_ref.shape
    mine = lax.axis_index(MEMBER)
    weight = jnp.where(lax.rem(lax.div(mine, 2), 2) == 0, weight_ref[:8, :], weight_ref[8:, :])
    softness = smooth_width * smooth_width
    loss = jnp.zeros((8, width), f32)
    for tile in range(0, height, 8):
        values = [fields_ref[m, tile : tile + 8, :] for m in range(members)]
        truth = targets_ref[mine, tile : tile + 8, :]
        direct = jnp.zeros((8, width), f32)
        pairs = jnp.full((8, width), members * smooth_width, f32)
        slopes = [jnp.zeros((8, width), f32) for m in range(members)]
        grads = []
        for m in range(members):
            error = values[m] - truth
            square = error * error + softness
            inverse = lax.rsqrt(square)
            direct = direct + square * inverse
            grads.append(error * inverse)
            for other in range(m + 1, members):
                gap = values[m] - values[other]
                square = gap * gap + softness
                inverse = lax.rsqrt(square)
                pairs = pairs + 2.0 * square * inverse
                slope = gap * inverse
                slopes[m] = slopes[m] + slope
                slopes[other] = slopes[other] - slope
        loss = loss + weight * (direct - pairs / (2.0 * (members - 1)))
        for m in range(members):
            out_ref[m, tile : tile + 8, :] = weight * (grads[m] - slopes[m] / (members - 1))
    for m in range(members):
        out_ref[m, height : height + 8, :] = loss


def crps(weights, fields, targets):
    members, height, width = fields.shape
    return pl.pallas_call(
        crps_kernel,
        out_shape=jax.ShapeDtypeStruct((members, height + 8, width), f32),
        compiler_params=params,
        name="crps",
    )(weights, fields, targets)


def collect_kernel(grads_ref, first_ref, second_ref):
    chunks, height, width = grads_ref.shape
    height = height - 8
    half = chunks // 2
    total = grads_ref[0, height : height + 8, :]
    for chunk in range(1, chunks):
        total = total + grads_ref[chunk, height : height + 8, :]
    for chunk in range(half):
        first_ref[chunk * height : (chunk + 1) * height, :] = grads_ref[chunk, :height, :]
        second_ref[chunk * height : (chunk + 1) * height, :] = grads_ref[half + chunk, :height, :]
    known = jnp.broadcast_to(jnp.sum(total, axis=0, keepdims=True), (slab_count, width))
    slab = lax.broadcasted_iota(jnp.int32, known.shape, 0)
    second_ref[half * height :, :] = jnp.where(slab == lax.axis_index(LAT), known, 0.0)


def collect(grads):
    chunks, height, width = grads.shape
    count = chunks // 2 * (height - 8)
    return pl.pallas_call(
        collect_kernel,
        out_shape=[
            jax.ShapeDtypeStruct((count, width), f32),
            jax.ShapeDtypeStruct((count + slab_count, width), f32),
        ],
        compiler_params=params,
        name="collect",
    )(grads)


def merged(*known):
    result = known[0]
    for other in known[1:]:
        result = jnp.where(result != 0.0, result, other)
    return result


def merge_kernel(own_ref, near_ref, across_ref, *rest):
    count = own_ref.shape[0] - slab_count
    tables = [ref[count:, :] for ref in (own_ref, near_ref, across_ref)]
    rest[-1][...] = merged(*tables, *(ref[...] for ref in rest[:-1]))


def merge(own, near, across, *far):
    return pl.pallas_call(
        merge_kernel,
        out_shape=jax.ShapeDtypeStruct((slab_count, own.shape[1]), f32),
        compiler_params=params,
        name="merge",
    )(own, near, across, *far)


def backward_kernel(step, own_ref, near_ref, across_ref, slope_ref, outb_hi, outb_lo, inb_hi, inb_lo,
                    *rest):
    added, known_ref = rest[:-5][:1], rest[:-5][1:]
    out_ref, wide_hi, wide_lo, hid_hi, hid_lo = rest[-5:]
    width = own_ref.shape[1]
    channels = (own_ref.shape[0] - slab_count) // 2
    hidden = outb_hi.shape[0]
    even = is_even()
    wide = (wide_hi, wide_lo)
    hid = (hid_hi, hid_lo)
    w_out = (outb_hi[...], outb_lo[...])
    w_in = (inb_hi[...], inb_lo[...])

    def take(ref, row):
        return ref[row * channels : (row + 1) * channels, :]

    def put_beside(index, first, second, row):
        value = jnp.where(even, take(first, row), take(second, row))
        value = jnp.where(inside(index - 2), value, 0.0)
        put_windows(wide, index, value)

    for row in range(2):
        put_windows(wide, 2 + row, take(own_ref, row))
    for row in range(2):
        put_beside(row, across_ref, near_ref, row)
        put_beside(4 + row, near_ref, across_ref, row)
    for pair in (0, 2):
        grads = to_channels(w_out, wide, pair, channels) * slope_ref[step, pair // 2]
        for half in range(2):
            row = grads[:, half * width : (half + 1) * width]
            row = jnp.where(inside(pair + half - 1), row, 0.0)
            put_twice(hid, pair + half, hidden, 0, split(row))
    moved = from_channels(w_in, hid, 0, hidden, channels)
    for row in range(2):
        total = take(own_ref, row) + moved[row]
        for extra in added:
            total = total + take(extra, row)
        out_ref[row * channels : (row + 1) * channels, :] = total
    if known_ref:
        last = 2 * channels
        out_ref[last:, :] = known_ref[0][...]


def backward(step, own, near, across, slopes, w_out, w_in, *added):
    count, width = own.shape
    channels = (count - slab_count) // 2
    hidden = w_out[0].shape[0]
    vmem = pl.BlockSpec(memory_space=pltpu.VMEM)
    return pl.pallas_call(
        functools.partial(backward_kernel, step),
        in_specs=[vmem] * (8 + len(added)),
        out_shape=jax.ShapeDtypeStruct((count if step else 2 * channels, width), f32),
        scratch_shapes=[pltpu.VMEM((18 * channels, 2 * width), bf16)] * 2
        + [pltpu.VMEM((4 * hidden, 2 * width), bf16)] * 2,
        compiler_params=params,
        name="backward",
    )(own, near, across, slopes, *w_out, *w_in, *added)


def on_device(initial_states, targets, lat_weight, weight_in, weight_out, hidden_bias):
    members = lax.axis_size(MEMBER)
    slabs = lax.axis_size(LAT)
    steps, slab_rows, channels, width = targets.shape
    rows = slabs * slab_rows
    near = [(i, i ^ 1) for i in range(slabs)]
    across = [(i, (i + 1 if i % 2 else i - 1) % slabs) for i in range(slabs)]

    own = initial_states[0]
    beside = lax.ppermute(own, LAT, near)
    crossed = lax.ppermute(own, LAT, across)
    far_crossed = lax.ppermute(beside, LAT, across)
    ready = prepare(weight_in.T, weight_out, hidden_bias[None, :], lat_weight[None, :], width)
    crossed, beside = lax.optimization_barrier((crossed, beside))
    far_beside = lax.ppermute(crossed, LAT, near)
    before, fields = forward(
        own, beside, crossed, far_crossed, far_beside, ready[4], ready[:2], ready[2:4]
    )
    height = steps * slab_rows * channels // members
    chunks = lax.all_to_all(
        fields.reshape(members, height, width), MEMBER, split_axis=0, concat_axis=0, tiled=True
    )
    grads = crps(ready[5], chunks, targets.reshape(members, height, width))
    grads = lax.all_to_all(grads, MEMBER, split_axis=0, concat_axis=0, tiled=True)
    grads, before = lax.optimization_barrier((grads, before))
    *back, slopes = prepare_back(weight_in.T, weight_out, before)
    w_out_back, w_in_back = back[:2], back[2:]
    first_grads, message = collect(grads)

    beside = lax.ppermute(message, LAT, near)
    crossed = lax.ppermute(message, LAT, across)
    known = merge(message, beside, crossed)
    far = lax.ppermute(known, LAT, [(i, i ^ 4) for i in range(slabs)])
    message = backward(1, message, beside, crossed, slopes, w_out_back, w_in_back, first_grads, known)
    message, far = lax.optimization_barrier((message, far))
    beside = lax.ppermute(message, LAT, near)
    crossed = lax.ppermute(message, LAT, across)
    known = merge(message, beside, crossed, far)
    gradient = backward(0, message, beside, crossed, slopes, w_out_back, w_in_back)
    opposite = lax.ppermute(known, LAT, [(i, i ^ 8) for i in range(slabs)])
    total = jnp.sum(jnp.where(known != 0.0, known, opposite))
    loss = total / (members * steps * rows * channels * width)
    return gradient.reshape(initial_states.shape), loss


def solution(mesh):
    torus = Mesh(
        mesh.devices.reshape(4, 2, 2, 4, 2), ("member_0", "member_1", "lat_0", "lat_1", "lat_2")
    )
    placed = (P(MEMBER, LAT, None, None), P(None, LAT, None, None), P(LAT), P(), P(), P())
    return jax.shard_map(
        on_device,
        mesh=torus,
        in_specs=placed,
        out_specs=(P(MEMBER, LAT, None, None), P()),
        check_vma=False,
    )
```

```python
import functools

import jax
import jax.numpy as jnp
from jax import lax
from jax.experimental import pallas as pl
from jax.experimental.pallas import tpu as pltpu
from jax.sharding import Mesh
from jax.sharding import PartitionSpec as P

MEMBER = ("member_0", "member_1")
LAT = ("lat_0", "lat_1", "lat_2")

smooth_width = 0.1
gelu_scale = 0.7978845608028654
gelu_cubic = 0.044715
slab_count = 16

f32 = jnp.float32
bf16 = jnp.bfloat16
params = pltpu.CompilerParams(vmem_limit_bytes=16 * 1024 * 1024)


def split(value):
    high = value.astype(bf16)
    return high, (value - high.astype(f32)).astype(bf16)


def product(left, right):
    dot = functools.partial(jnp.dot, preferred_element_type=f32)
    count = left.shape[0] // 2
    both = dot(left, right[0])
    return both[:count] + (both[count:] + dot(left[:count], right[1]))


def from_left(row):
    lane = lax.broadcasted_iota(jnp.int32, row.shape, 1)
    return jnp.where(lane == 0, 0.0, pltpu.roll(row, 1, 1))


def from_right(row):
    lane = lax.broadcasted_iota(jnp.int32, row.shape, 1)
    return jnp.where(lane == row.shape[1] - 1, 0.0, pltpu.roll(row, row.shape[1] - 1, 1))


def put_twice(refs, index, height, part, values):
    width = values[0].shape[1]
    size = values[0].shape[0]
    for ref, value in zip(refs, values):
        base = index * height + part * size
        if base + size <= ref.shape[0]:
            ref[base : base + size, :width] = value
        if index:
            ref[base - height : base - height + size, width:] = value


def put_windows(refs, index, row):
    height = 3 * row.shape[0]
    for part, shifted in enumerate((from_left(row), row, from_right(row))):
        put_twice(refs, index, height, part, split(shifted))


def read(refs, start, size):
    return tuple(ref[start : start + size, :] for ref in refs)


def to_channels(weights, windows, pair, channels):
    return product(weights, read(windows, pair * 3 * channels, 9 * channels))


def from_channels(weights, hidden, pair, channels, outer):
    mixed = product(weights, read(hidden, pair * channels, 3 * channels))
    width = mixed.shape[1] // 2
    rows = []
    for half in range(2):
        part = mixed[:, half * width : (half + 1) * width]
        rows.append(
            from_left(part[:outer])
            + part[outer : 2 * outer]
            + from_right(part[2 * outer :])
        )
    return rows


def gelu(x):
    return 0.5 * x * (1.0 + jnp.tanh(gelu_scale * (x + gelu_cubic * x * x * x)))


def gelu_slope(x):
    t = jnp.tanh(gelu_scale * (x + gelu_cubic * x * x * x))
    inner = gelu_scale * (1.0 + 3.0 * gelu_cubic * x * x)
    return 0.5 * (1.0 + t) + 0.5 * x * (1.0 - t * t) * inner


def fetch(pairs, arrived):
    copies = [pltpu.make_async_copy(*pair, arrived.at[i]) for i, pair in enumerate(pairs)]
    for copy in copies:
        copy.start()
    for copy in copies:
        copy.wait()


def prepare_kernel(win_hbm, wout_hbm, bias_hbm, lat_hbm, in_ref, out_ref, wide_bias_ref, wide_lat_ref,
                   win_ref, wout_ref, bias_ref, lat_ref, arrived):
    fetch(((win_hbm, win_ref), (wout_hbm, wout_ref), (bias_hbm, bias_ref), (lat_hbm, lat_ref)), arrived)
    outer, width = wout_ref.shape
    hidden = width // 9
    in_ref[:hidden, :], in_ref[hidden:, :] = split(win_ref[...].T)
    for a in range(3):
        for b in range(3):
            tap = 3 * a + b
            high, low = split(wout_ref[:, tap * hidden : (tap + 1) * hidden])
            out_ref[b * outer : (b + 1) * outer, a * hidden : (a + 1) * hidden] = high
            out_ref[(3 + b) * outer : (4 + b) * outer, a * hidden : (a + 1) * hidden] = low
    wide_bias_ref[...] = jnp.broadcast_to(bias_ref[...], wide_bias_ref.shape[::-1]).T
    for row in range(2):
        one = jnp.broadcast_to(lat_ref[:, row : row + 1], (8, wide_lat_ref.shape[1]))
        wide_lat_ref[8 * row : 8 * (row + 1), :] = one


def prepare(weight_in, weight_out, bias, lat_weight, width):
    taps_in, hidden = weight_in.shape
    outer = weight_out.shape[0]
    arrays = (weight_in, weight_out, bias, lat_weight)
    shapes = [(2 * hidden, taps_in), (6 * outer, 3 * hidden)]
    return pl.pallas_call(
        prepare_kernel,
        out_shape=[jax.ShapeDtypeStruct(shape, bf16) for shape in shapes]
        + [jax.ShapeDtypeStruct((hidden, width), f32), jax.ShapeDtypeStruct((16, width), f32)],
        in_specs=[pl.BlockSpec(memory_space=pltpu.HBM)] * 4,
        scratch_shapes=[pltpu.VMEM(array.shape, f32) for array in arrays] + [pltpu.SemaphoreType.DMA((4,))],
        compiler_params=params,
        name="prepare",
    )(*(pltpu.with_memory_space_constraint(array, pltpu.HBM) for array in arrays))


def prepare_back_kernel(win_hbm, wout_hbm, before_ref, outb_ref, inb_ref, slope_ref,
                        stack, win_ref, wout_ref, arrived):
    pairs = ((win_hbm, win_ref), (wout_hbm, wout_ref))
    copies = [pltpu.make_async_copy(*pair, arrived.at[i]) for i, pair in enumerate(pairs)]
    for copy in copies:
        copy.start()
    for step in range(2):
        for pair in range(2):
            slope_ref[step, pair] = gelu_slope(before_ref[step, pair])
    for copy in copies:
        copy.wait()
    outer, width = wout_ref.shape
    hidden = width // 9
    inner = win_ref.shape[0] // 9
    for a in range(3):
        for b in range(3):
            tap = 3 * a + b
            stack[(8 - tap) * outer : (9 - tap) * outer, :] = wout_ref[:, tap * hidden : (tap + 1) * hidden]
            high, low = split(win_ref[tap * inner : (tap + 1) * inner, :])
            j, k = 2 - a, 2 - b
            inb_ref[k * inner : (k + 1) * inner, j * hidden : (j + 1) * hidden] = high
            inb_ref[(3 + k) * inner : (4 + k) * inner, j * hidden : (j + 1) * hidden] = low
    outb_ref[:hidden, :], outb_ref[hidden:, :] = split(stack[...].T)


def prepare_back(weight_in, weight_out, before):
    taps_in, hidden = weight_in.shape
    outer = weight_out.shape[0]
    inner = taps_in // 9
    arrays = (weight_in, weight_out)
    shapes = [(2 * hidden, 9 * outer), (6 * inner, 3 * hidden)]
    hbm = pl.BlockSpec(memory_space=pltpu.HBM)
    return pl.pallas_call(
        prepare_back_kernel,
        out_shape=[jax.ShapeDtypeStruct(shape, bf16) for shape in shapes]
        + [jax.ShapeDtypeStruct(before.shape, f32)],
        in_specs=[hbm, hbm, pl.BlockSpec(memory_space=pltpu.VMEM)],
        scratch_shapes=[pltpu.VMEM((9 * outer, hidden), f32)]
        + [pltpu.VMEM(array.shape, f32) for array in arrays]
        + [pltpu.SemaphoreType.DMA((2,))],
        compiler_params=params,
        name="prepare_back",
    )(*(pltpu.with_memory_space_constraint(array, pltpu.HBM) for array in arrays), before)


def inside(row):
    index = lax.axis_index(LAT) * 2 + row
    return (index >= 0) & (index < 2 * slab_count)


def is_even():
    return lax.rem(lax.axis_index(LAT), 2) == 0


def forward_kernel(own_ref, near_ref, across_ref, far_across_ref, far_near_ref, bias_ref,
                   in_ref, out_ref, before_ref, fields_ref, wide_hi, wide_lo, hid_hi, hid_lo):
    channels, width = own_ref.shape[1:]
    hidden = in_ref.shape[0] // 2
    even = is_even()
    wide = (wide_hi, wide_lo)
    hid = (hid_hi, hid_lo)
    w_in = in_ref[...]
    w_out = out_ref[...]
    bias = jnp.concatenate([bias_ref[...]] * 2, axis=1)

    def initial(index):
        slab, row = index // 2, index % 2
        if slab == 2:
            return own_ref[row]
        first, second = {
            0: (far_across_ref, far_near_ref),
            1: (across_ref, near_ref),
            3: (near_ref, across_ref),
            4: (far_near_ref, far_across_ref),
        }[slab]
        value = jnp.where(even, first[row], second[row])
        return jnp.where(inside(index - 4), value, 0.0)

    def advance(field, first, count, keep, step):
        for index in range(count):
            put_windows(wide, index, field(index))
        for pair in range(0, count - 2, 2):
            before = to_channels(w_in, wide, pair, channels) + bias
            if pair in keep:
                before_ref[step, keep.index(pair)] = before
            active = gelu(before)
            for half in range(2):
                row = active[:, half * width : (half + 1) * width]
                row = jnp.where(inside(first + 1 + pair + half), row, 0.0)
                put_twice(hid, pair + half, hidden, 0, split(row))
        result = []
        for pair in range(0, count - 4, 2):
            moved = from_channels(w_out, hid, pair, hidden, channels)
            for half in range(2):
                row = field(pair + 2 + half) + moved[half]
                result.append(jnp.where(inside(first + 2 + pair + half), row, 0.0))
        return result

    first = advance(initial, -4, 10, (2, 4), 0)
    for half in range(2):
        fields_ref[half * channels : (half + 1) * channels, :] = first[2 + half]
    second = advance(lambda index: first[index], -2, 6, (0, 2), 1)
    for half in range(2):
        fields_ref[(2 + half) * channels : (3 + half) * channels, :] = second[half]


def forward(own, near, across, far_across, far_near, bias, w_in, w_out):
    channels, width = own.shape[1:]
    hidden = w_in.shape[0] // 2
    vmem = pl.BlockSpec(memory_space=pltpu.VMEM)
    return pl.pallas_call(
        forward_kernel,
        in_specs=[vmem] * 8,
        out_shape=[
            jax.ShapeDtypeStruct((2, 2, hidden, 2 * width), f32),
            jax.ShapeDtypeStruct((4 * channels, width), f32),
        ],
        scratch_shapes=[pltpu.VMEM((30 * channels, 2 * width), bf16)] * 2
        + [pltpu.VMEM((8 * hidden, 2 * width), bf16)] * 2,
        compiler_params=params,
        name="forward",
    )(own, near, across, far_across, far_near, bias, w_in, w_out)


def crps_kernel(weight_ref, fields_ref, targets_ref, out_ref):
    members, height, width = fields_ref.shape
    mine = lax.axis_index(MEMBER)
    weight = jnp.where(lax.rem(lax.div(mine, 2), 2) == 0, weight_ref[:8, :], weight_ref[8:, :])
    softness = smooth_width * smooth_width
    loss = jnp.zeros((8, width), f32)
    for tile in range(0, height, 8):
        values = [fields_ref[m, tile : tile + 8, :] for m in range(members)]
        truth = targets_ref[mine, tile : tile + 8, :]
        direct = jnp.zeros((8, width), f32)
        pairs = jnp.full((8, width), members * smooth_width, f32)
        slopes = [jnp.zeros((8, width), f32) for m in range(members)]
        grads = []
        for m in range(members):
            error = values[m] - truth
            square = error * error + softness
            inverse = lax.rsqrt(square)
            direct = direct + square * inverse
            grads.append(error * inverse)
            for other in range(m + 1, members):
                gap = values[m] - values[other]
                square = gap * gap + softness
                inverse = lax.rsqrt(square)
                pairs = pairs + 2.0 * square * inverse
                slope = gap * inverse
                slopes[m] = slopes[m] + slope
                slopes[other] = slopes[other] - slope
        loss = loss + weight * (direct - pairs / (2.0 * (members - 1)))
        for m in range(members):
            out_ref[m, tile : tile + 8, :] = weight * (grads[m] - slopes[m] / (members - 1))
    for m in range(members):
        out_ref[m, height : height + 8, :] = loss


def crps(weights, fields, targets):
    members, height, width = fields.shape
    return pl.pallas_call(
        crps_kernel,
        out_shape=jax.ShapeDtypeStruct((members, height + 8, width), f32),
        compiler_params=params,
        name="crps",
    )(weights, fields, targets)


def collect_kernel(grads_ref, first_ref, second_ref, known_ref):
    chunks, height, width = grads_ref.shape
    height = height - 8
    half = chunks // 2
    total = grads_ref[0, height : height + 8, :]
    for chunk in range(1, chunks):
        total = total + grads_ref[chunk, height : height + 8, :]
    for chunk in range(half):
        first_ref[chunk * height : (chunk + 1) * height, :] = grads_ref[chunk, :height, :]
        second_ref[chunk * height : (chunk + 1) * height, :] = grads_ref[half + chunk, :height, :]
    known = jnp.broadcast_to(jnp.sum(total, axis=0, keepdims=True), (slab_count, width))
    slab = lax.broadcasted_iota(jnp.int32, known.shape, 0)
    known = jnp.where(slab == lax.axis_index(LAT), known, 0.0)
    second_ref[half * height :, :] = known
    known_ref[...] = known


def collect(grads):
    chunks, height, width = grads.shape
    count = chunks // 2 * (height - 8)
    return pl.pallas_call(
        collect_kernel,
        out_shape=[
            jax.ShapeDtypeStruct((count, width), f32),
            jax.ShapeDtypeStruct((count + slab_count, width), f32),
            jax.ShapeDtypeStruct((slab_count, width), f32),
        ],
        compiler_params=params,
        name="collect",
    )(grads)


def merged(*known):
    result = known[0]
    for other in known[1:]:
        result = jnp.where(result != 0.0, result, other)
    return result


def table_of(*refs):
    return merged(*(ref[ref.shape[0] - slab_count :, :] for ref in refs))


def merge_kernel(*refs):
    refs[-1][...] = table_of(*refs[:-1])


def merge(*messages):
    return pl.pallas_call(
        merge_kernel,
        out_shape=jax.ShapeDtypeStruct((slab_count, messages[0].shape[1]), f32),
        compiler_params=params,
        name="merge",
    )(*messages)


def finish_kernel(count, gradient_ref, known_ref, opposite_ref, out_hbm, loss_ref, done):
    copy = pltpu.make_async_copy(gradient_ref, out_hbm, done)
    copy.start()
    total = jnp.sum(table_of(known_ref, opposite_ref), axis=0, keepdims=True)
    loss_ref[...] = jnp.sum(total, axis=1, keepdims=True) / count
    copy.wait()


def finish(gradient, known, opposite, count):
    vmem = pl.BlockSpec(memory_space=pltpu.VMEM)
    return pl.pallas_call(
        functools.partial(finish_kernel, count),
        out_shape=[
            jax.ShapeDtypeStruct(gradient.shape, f32),
            jax.ShapeDtypeStruct((1, 1), f32),
        ],
        in_specs=[vmem] * 3,
        out_specs=[pl.BlockSpec(memory_space=pltpu.HBM), vmem],
        scratch_shapes=[pltpu.SemaphoreType.DMA(())],
        compiler_params=params,
        name="finish",
    )(gradient, known, opposite)


def backward_kernel(step, own_ref, near_ref, across_ref, slope_ref, outb_ref, inb_ref,
                    *rest):
    added, far_ref = rest[:-5][:1], rest[:-5][1:]
    out_ref, wide_hi, wide_lo, hid_hi, hid_lo = rest[-5:]
    width = own_ref.shape[1]
    channels = (own_ref.shape[0] - slab_count) // 2
    hidden = outb_ref.shape[0] // 2
    even = is_even()
    wide = (wide_hi, wide_lo)
    hid = (hid_hi, hid_lo)
    w_out = outb_ref[...]
    w_in = inb_ref[...]

    def take(ref, row):
        return ref[row * channels : (row + 1) * channels, :]

    def put_beside(index, first, second, row):
        value = jnp.where(even, take(first, row), take(second, row))
        value = jnp.where(inside(index - 2), value, 0.0)
        put_windows(wide, index, value)

    for row in range(2):
        put_windows(wide, 2 + row, take(own_ref, row))
    for row in range(2):
        put_beside(row, across_ref, near_ref, row)
        put_beside(4 + row, near_ref, across_ref, row)
    for pair in (0, 2):
        grads = to_channels(w_out, wide, pair, channels) * slope_ref[step, pair // 2]
        for half in range(2):
            row = grads[:, half * width : (half + 1) * width]
            row = jnp.where(inside(pair + half - 1), row, 0.0)
            put_twice(hid, pair + half, hidden, 0, split(row))
    moved = from_channels(w_in, hid, 0, hidden, channels)
    for row in range(2):
        total = take(own_ref, row) + moved[row]
        for extra in added:
            total = total + take(extra, row)
        out_ref[row * channels : (row + 1) * channels, :] = total
    if far_ref:
        out_ref[2 * channels :, :] = table_of(own_ref, near_ref, across_ref, *far_ref)


def backward(step, own, near, across, slopes, w_out, w_in, *added):
    count, width = own.shape
    channels = (count - slab_count) // 2
    hidden = w_out.shape[0] // 2
    vmem = pl.BlockSpec(memory_space=pltpu.VMEM)
    return pl.pallas_call(
        functools.partial(backward_kernel, step),
        in_specs=[vmem] * (6 + len(added)),
        out_shape=jax.ShapeDtypeStruct((count if step else 2 * channels, width), f32),
        scratch_shapes=[pltpu.VMEM((18 * channels, 2 * width), bf16)] * 2
        + [pltpu.VMEM((4 * hidden, 2 * width), bf16)] * 2,
        compiler_params=params,
        name="backward",
    )(own, near, across, slopes, w_out, w_in, *added)


def on_device(initial_states, targets, lat_weight, weight_in, weight_out, hidden_bias):
    members = lax.axis_size(MEMBER)
    slabs = lax.axis_size(LAT)
    steps, slab_rows, channels, width = targets.shape
    rows = slabs * slab_rows
    near = [(i, i ^ 1) for i in range(slabs)]
    across = [(i, (i + 1 if i % 2 else i - 1) % slabs) for i in range(slabs)]

    own = initial_states[0]
    beside = lax.ppermute(own, LAT, near)
    crossed = lax.ppermute(own, LAT, across)
    far_crossed = lax.ppermute(beside, LAT, across)
    ready = prepare(weight_in.T, weight_out, hidden_bias[None, :], lat_weight[None, :], width)
    crossed, beside = lax.optimization_barrier((crossed, beside))
    far_beside = lax.ppermute(crossed, LAT, near)
    before, fields = forward(
        own, beside, crossed, far_crossed, far_beside, ready[2], ready[0], ready[1]
    )
    height = steps * slab_rows * channels // members
    chunks = lax.all_to_all(
        fields.reshape(members, height, width), MEMBER, split_axis=0, concat_axis=0, tiled=True
    )
    grads = crps(ready[3], chunks, targets.reshape(members, height, width))
    grads = lax.all_to_all(grads, MEMBER, split_axis=0, concat_axis=0, tiled=True)
    grads, before = lax.optimization_barrier((grads, before))
    w_out_back, w_in_back, slopes = prepare_back(weight_in.T, weight_out, before)
    first_grads, message, known = collect(grads)

    beside = lax.ppermute(message, LAT, near)
    crossed = lax.ppermute(message, LAT, across)
    far = lax.ppermute(known, LAT, [(i, i ^ 4) for i in range(slabs)])
    beside, crossed, far, slopes = lax.optimization_barrier((beside, crossed, far, slopes))
    message = backward(
        1, message, beside, crossed, slopes, w_out_back, w_in_back, first_grads, far
    )
    beside = lax.ppermute(message, LAT, near)
    crossed = lax.ppermute(message, LAT, across)
    known = merge(message, beside, crossed)
    gradient = backward(0, message, beside, crossed, slopes, w_out_back, w_in_back)
    opposite = lax.ppermute(known, LAT, [(i, i ^ 8) for i in range(slabs)])
    gradient, loss = finish(
        gradient, known, opposite, members * steps * rows * channels * width
    )
    loss = loss.reshape(())
    return gradient.reshape(initial_states.shape), loss


def solution(mesh):
    torus = Mesh(
        mesh.devices.reshape(4, 2, 2, 4, 2), ("member_0", "member_1", "lat_0", "lat_1", "lat_2")
    )
    placed = (P(MEMBER, LAT, None, None), P(None, LAT, None, None), P(LAT), P(), P(), P())
    return jax.shard_map(
        on_device,
        mesh=torus,
        in_specs=placed,
        out_specs=(P(MEMBER, LAT, None, None), P()),
        check_vma=False,
    )
```

```python
import functools

import jax
import jax.numpy as jnp
from jax import lax
from jax.experimental import pallas as pl
from jax.experimental.pallas import tpu as pltpu
from jax.sharding import Mesh
from jax.sharding import PartitionSpec as P

MEMBER = ("member_0", "member_1")
LAT = ("lat_0", "lat_1", "lat_2")

smooth_width = 0.1
gelu_scale = 0.7978845608028654
gelu_cubic = 0.044715
slab_count = 16

f32 = jnp.float32
bf16 = jnp.bfloat16
params = pltpu.CompilerParams(vmem_limit_bytes=16 * 1024 * 1024)


def split(value):
    high = value.astype(bf16)
    return high, (value - high.astype(f32)).astype(bf16)


def product(left, right):
    dot = functools.partial(jnp.dot, preferred_element_type=f32)
    count = left.shape[0] // 2
    both = dot(left, right[0])
    return both[:count] + (both[count:] + dot(left[:count], right[1]))


def from_left(row):
    lane = lax.broadcasted_iota(jnp.int32, row.shape, 1)
    return jnp.where(lane == 0, 0.0, pltpu.roll(row, 1, 1))


def from_right(row):
    lane = lax.broadcasted_iota(jnp.int32, row.shape, 1)
    return jnp.where(lane == row.shape[1] - 1, 0.0, pltpu.roll(row, row.shape[1] - 1, 1))


def put_twice(refs, index, height, part, values):
    width = values[0].shape[1]
    size = values[0].shape[0]
    for ref, value in zip(refs, values):
        base = index * height + part * size
        if base + size <= ref.shape[0]:
            ref[base : base + size, :width] = value
        if index:
            ref[base - height : base - height + size, width:] = value


def put_windows(refs, index, row):
    height = 3 * row.shape[0]
    for part, shifted in enumerate((from_left(row), row, from_right(row))):
        put_twice(refs, index, height, part, split(shifted))


def read(refs, start, size):
    return tuple(ref[start : start + size, :] for ref in refs)


def to_channels(weights, windows, pair, channels):
    return product(weights, read(windows, pair * 3 * channels, 9 * channels))


def from_channels(weights, hidden, pair, channels, outer):
    mixed = product(weights, read(hidden, pair * channels, 3 * channels))
    width = mixed.shape[1] // 2
    rows = []
    for half in range(2):
        part = mixed[:, half * width : (half + 1) * width]
        rows.append(
            from_left(part[:outer])
            + part[outer : 2 * outer]
            + from_right(part[2 * outer :])
        )
    return rows


def gelu(x):
    return 0.5 * x * (1.0 + jnp.tanh(gelu_scale * (x + gelu_cubic * x * x * x)))


def gelu_slope(x):
    t = jnp.tanh(gelu_scale * (x + gelu_cubic * x * x * x))
    inner = gelu_scale * (1.0 + 3.0 * gelu_cubic * x * x)
    return 0.5 * (1.0 + t) + 0.5 * x * (1.0 - t * t) * inner


def fetch(pairs, arrived):
    copies = [pltpu.make_async_copy(*pair, arrived.at[i]) for i, pair in enumerate(pairs)]
    for copy in copies:
        copy.start()
    for copy in copies:
        copy.wait()


def prepare_kernel(win_hbm, wout_hbm, bias_hbm, lat_hbm, in_ref, out_ref, wide_bias_ref, wide_lat_ref,
                   win_ref, wout_ref, bias_ref, lat_ref, arrived):
    fetch(((win_hbm, win_ref), (wout_hbm, wout_ref), (bias_hbm, bias_ref), (lat_hbm, lat_ref)), arrived)
    outer, width = wout_ref.shape
    hidden = width // 9
    in_ref[:hidden, :], in_ref[hidden:, :] = split(win_ref[...].T)
    for a in range(3):
        for b in range(3):
            tap = 3 * a + b
            high, low = split(wout_ref[:, tap * hidden : (tap + 1) * hidden])
            out_ref[b * outer : (b + 1) * outer, a * hidden : (a + 1) * hidden] = high
            out_ref[(3 + b) * outer : (4 + b) * outer, a * hidden : (a + 1) * hidden] = low
    wide_bias_ref[...] = jnp.broadcast_to(bias_ref[...], wide_bias_ref.shape[::-1]).T
    for row in range(2):
        one = jnp.broadcast_to(lat_ref[:, row : row + 1], (8, wide_lat_ref.shape[1]))
        wide_lat_ref[8 * row : 8 * (row + 1), :] = one


def prepare(weight_in, weight_out, bias, lat_weight, width):
    taps_in, hidden = weight_in.shape
    outer = weight_out.shape[0]
    arrays = (weight_in, weight_out, bias, lat_weight)
    shapes = [(2 * hidden, taps_in), (6 * outer, 3 * hidden)]
    return pl.pallas_call(
        prepare_kernel,
        out_shape=[jax.ShapeDtypeStruct(shape, bf16) for shape in shapes]
        + [jax.ShapeDtypeStruct((hidden, width), f32), jax.ShapeDtypeStruct((16, width), f32)],
        in_specs=[pl.BlockSpec(memory_space=pltpu.HBM)] * 4,
        scratch_shapes=[pltpu.VMEM(array.shape, f32) for array in arrays] + [pltpu.SemaphoreType.DMA((4,))],
        compiler_params=params,
        name="prepare",
    )(*(pltpu.with_memory_space_constraint(array, pltpu.HBM) for array in arrays))


def prepare_back_kernel(win_hbm, wout_hbm, first_ref, second_ref, outb_ref, inb_ref, slope_ref,
                        stack, win_ref, wout_ref, arrived):
    pairs = ((win_hbm, win_ref), (wout_hbm, wout_ref))
    copies = [pltpu.make_async_copy(*pair, arrived.at[i]) for i, pair in enumerate(pairs)]
    for copy in copies:
        copy.start()
    for step, before_ref in enumerate((first_ref, second_ref)):
        for pair in range(2):
            slope_ref[step, pair] = gelu_slope(before_ref[pair])
    for copy in copies:
        copy.wait()
    outer, width = wout_ref.shape
    hidden = width // 9
    inner = win_ref.shape[0] // 9
    for a in range(3):
        for b in range(3):
            tap = 3 * a + b
            stack[(8 - tap) * outer : (9 - tap) * outer, :] = wout_ref[:, tap * hidden : (tap + 1) * hidden]
            high, low = split(win_ref[tap * inner : (tap + 1) * inner, :])
            j, k = 2 - a, 2 - b
            inb_ref[k * inner : (k + 1) * inner, j * hidden : (j + 1) * hidden] = high
            inb_ref[(3 + k) * inner : (4 + k) * inner, j * hidden : (j + 1) * hidden] = low
    outb_ref[:hidden, :], outb_ref[hidden:, :] = split(stack[...].T)


def prepare_back(weight_in, weight_out, first, second):
    taps_in, hidden = weight_in.shape
    outer = weight_out.shape[0]
    inner = taps_in // 9
    arrays = (weight_in, weight_out)
    shapes = [(2 * hidden, 9 * outer), (6 * inner, 3 * hidden)]
    hbm = pl.BlockSpec(memory_space=pltpu.HBM)
    return pl.pallas_call(
        prepare_back_kernel,
        out_shape=[jax.ShapeDtypeStruct(shape, bf16) for shape in shapes]
        + [jax.ShapeDtypeStruct((2, *first.shape), f32)],
        in_specs=[hbm, hbm] + [pl.BlockSpec(memory_space=pltpu.VMEM)] * 2,
        scratch_shapes=[pltpu.VMEM((9 * outer, hidden), f32)]
        + [pltpu.VMEM(array.shape, f32) for array in arrays]
        + [pltpu.SemaphoreType.DMA((2,))],
        compiler_params=params,
        name="prepare_back",
    )(*(pltpu.with_memory_space_constraint(array, pltpu.HBM) for array in arrays), first, second)


def inside(row):
    index = lax.axis_index(LAT) * 2 + row
    return (index >= 0) & (index < 2 * slab_count)


def is_even():
    return lax.rem(lax.axis_index(LAT), 2) == 0


def either(first, second):
    return lambda row: jnp.where(is_even(), first[row], second[row])


def activate(before, first, hid, index, hidden, width):
    active = gelu(before)
    for half in range(2):
        row = active[:, half * width : (half + 1) * width]
        row = jnp.where(inside(first + half), row, 0.0)
        put_twice(hid, index + half, hidden, 0, split(row))


def inner_kernel(own_ref, near_ref, across_ref, bias_ref, in_ref, out_ref, before_ref, field_ref, hid_hi, hid_lo,
                 wide_hi, wide_lo):
    channels, width = own_ref.shape[1:]
    hidden = in_ref.shape[0] // 2
    wide = (wide_hi, wide_lo)
    hid = (hid_hi, hid_lo)
    bias = jnp.concatenate([bias_ref[...]] * 2, axis=1)
    slabs = (either(across_ref, near_ref), lambda row: own_ref[row], either(near_ref, across_ref))
    for index in range(6):
        row = slabs[index // 2](index % 2)
        if index // 2 != 1:
            row = jnp.where(inside(index - 2), row, 0.0)
        put_windows(wide, index, row)
    w_in = in_ref[...]
    for pair in (0, 2):
        before = to_channels(w_in, wide, pair, channels) + bias
        before_ref[pair // 2] = before
        activate(before, pair - 1, hid, pair, hidden, width)
    moved = from_channels(out_ref[...], hid, 0, hidden, channels)
    for row in range(2):
        field_ref[row * channels : (row + 1) * channels, :] = own_ref[row] + moved[row]


def inner(own, near, across, bias, w_in, w_out):
    channels, width = own.shape[1:]
    hidden = w_in.shape[0] // 2
    return pl.pallas_call(
        inner_kernel,
        out_shape=[
            jax.ShapeDtypeStruct((2, hidden, 2 * width), f32),
            jax.ShapeDtypeStruct((2 * channels, width), f32),
        ]
        + [jax.ShapeDtypeStruct((4 * hidden, 2 * width), bf16)] * 2,
        scratch_shapes=[pltpu.VMEM((18 * channels, 2 * width), bf16)] * 2,
        compiler_params=params,
        name="inner",
    )(own, near, across, bias, w_in, w_out)


def outer_kernel(near_ref, across_ref, far_across_ref, far_near_ref, field_ref, hid_hi, hid_lo, bias_ref, in_ref,
                 out_ref, before_ref, fields_ref, wide_hi, wide_lo, side_hi, side_lo):
    channels, width = near_ref.shape[1:]
    hidden = in_ref.shape[0] // 2
    wide = (wide_hi, wide_lo)
    side = (side_hi, side_lo)
    bias = jnp.concatenate([bias_ref[...]] * 2, axis=1)
    w_in = in_ref[...]
    w_out = out_ref[...]
    fields = [None, None] + [field_ref[row * channels : (row + 1) * channels, :] for row in range(2)] + [None, None]
    count = 2 * hidden
    for after in range(2):
        if after:
            slabs = (either(near_ref, across_ref), either(far_near_ref, far_across_ref))
        else:
            slabs = (either(far_across_ref, far_near_ref), either(across_ref, near_ref))
        first = 2 if after else -4
        base = 4 * after
        rows = []
        for index in range(4):
            row = jnp.where(inside(first + index), slabs[index // 2](index % 2), 0.0)
            rows.append(row)
            put_windows(wide, base + index, row)
        before = to_channels(w_in, wide, base, channels) + bias
        if after:
            for ref, known in zip(side, (hid_hi, hid_lo)):
                ref[4 * hidden : 5 * hidden, :] = known[count : count + hidden, :]
                ref[5 * hidden : 6 * hidden, :width] = known[count : count + hidden, width:]
            activate(before, 3, side, 6, hidden, width)
        else:
            for ref, known in zip(side, (hid_hi, hid_lo)):
                ref[count : count + hidden, :] = known[:hidden, :]
                ref[hidden:count, width:] = known[:hidden, :width]
            activate(before, -3, side, 0, hidden, width)
        moved = from_channels(w_out, side, base, hidden, channels)
        for row in range(2):
            at = 4 * after + row
            value = rows[(0 if after else 2) + row] + moved[row]
            fields[at] = jnp.where(inside(at - 2), value, 0.0)
    for index in range(6):
        put_windows(wide, index, fields[index])
    for pair in (0, 2):
        before = to_channels(w_in, wide, pair, channels) + bias
        before_ref[pair // 2] = before
        activate(before, pair - 1, side, pair, hidden, width)
    moved = from_channels(w_out, side, 0, hidden, channels)
    for row in range(2):
        fields_ref[row * channels : (row + 1) * channels, :] = fields[2 + row]
        fields_ref[(2 + row) * channels : (3 + row) * channels, :] = fields[2 + row] + moved[row]


def outer(near, across, far_across, far_near, field, hid, bias, w_in, w_out):
    channels, width = near.shape[1:]
    hidden = w_in.shape[0] // 2
    return pl.pallas_call(
        outer_kernel,
        out_shape=[
            jax.ShapeDtypeStruct((2, hidden, 2 * width), f32),
            jax.ShapeDtypeStruct((4 * channels, width), f32),
        ],
        scratch_shapes=[pltpu.VMEM((24 * channels, 2 * width), bf16)] * 2
        + [pltpu.VMEM((8 * hidden, 2 * width), bf16)] * 2,
        compiler_params=params,
        name="outer",
    )(near, across, far_across, far_near, field, *hid, bias, w_in, w_out)


def crps_kernel(weight_ref, fields_ref, targets_ref, out_ref):
    members, height, width = fields_ref.shape
    mine = lax.axis_index(MEMBER)
    weight = jnp.where(lax.rem(lax.div(mine, 2), 2) == 0, weight_ref[:8, :], weight_ref[8:, :])
    softness = smooth_width * smooth_width
    loss = jnp.zeros((8, width), f32)
    for tile in range(0, height, 8):
        values = [fields_ref[m, tile : tile + 8, :] for m in range(members)]
        truth = targets_ref[mine, tile : tile + 8, :]
        direct = jnp.zeros((8, width), f32)
        pairs = jnp.full((8, width), members * smooth_width, f32)
        slopes = [jnp.zeros((8, width), f32) for m in range(members)]
        grads = []
        for m in range(members):
            error = values[m] - truth
            square = error * error + softness
            inverse = lax.rsqrt(square)
            direct = direct + square * inverse
            grads.append(error * inverse)
            for other in range(m + 1, members):
                gap = values[m] - values[other]
                square = gap * gap + softness
                inverse = lax.rsqrt(square)
                pairs = pairs + 2.0 * square * inverse
                slope = gap * inverse
                slopes[m] = slopes[m] + slope
                slopes[other] = slopes[other] - slope
        loss = loss + weight * (direct - pairs / (2.0 * (members - 1)))
        for m in range(members):
            out_ref[m, tile : tile + 8, :] = weight * (grads[m] - slopes[m] / (members - 1))
    for m in range(members):
        out_ref[m, height : height + 8, :] = loss


def crps(weights, fields, targets):
    members, height, width = fields.shape
    return pl.pallas_call(
        crps_kernel,
        out_shape=jax.ShapeDtypeStruct((members, height + 8, width), f32),
        compiler_params=params,
        name="crps",
    )(weights, fields, targets)


def collect_kernel(grads_ref, first_ref, second_ref, known_ref):
    chunks, height, width = grads_ref.shape
    height = height - 8
    half = chunks // 2
    total = grads_ref[0, height : height + 8, :]
    for chunk in range(1, chunks):
        total = total + grads_ref[chunk, height : height + 8, :]
    for chunk in range(half):
        first_ref[chunk * height : (chunk + 1) * height, :] = grads_ref[chunk, :height, :]
        second_ref[chunk * height : (chunk + 1) * height, :] = grads_ref[half + chunk, :height, :]
    known = jnp.broadcast_to(jnp.sum(total, axis=0, keepdims=True), (slab_count, width))
    slab = lax.broadcasted_iota(jnp.int32, known.shape, 0)
    known = jnp.where(slab == lax.axis_index(LAT), known, 0.0)
    second_ref[half * height :, :] = known
    known_ref[...] = known


def collect(grads):
    chunks, height, width = grads.shape
    count = chunks // 2 * (height - 8)
    return pl.pallas_call(
        collect_kernel,
        out_shape=[
            jax.ShapeDtypeStruct((count, width), f32),
            jax.ShapeDtypeStruct((count + slab_count, width), f32),
            jax.ShapeDtypeStruct((slab_count, width), f32),
        ],
        compiler_params=params,
        name="collect",
    )(grads)


def merged(*known):
    result = known[0]
    for other in known[1:]:
        result = jnp.where(result != 0.0, result, other)
    return result


def table_of(*refs):
    return merged(*(ref[ref.shape[0] - slab_count :, :] for ref in refs))


def merge_kernel(*refs):
    refs[-1][...] = table_of(*refs[:-1])


def merge(*messages):
    return pl.pallas_call(
        merge_kernel,
        out_shape=jax.ShapeDtypeStruct((slab_count, messages[0].shape[1]), f32),
        compiler_params=params,
        name="merge",
    )(*messages)


def finish_kernel(count, gradient_ref, known_ref, opposite_ref, out_hbm, loss_hbm, loss_ref, done):
    copy = pltpu.make_async_copy(gradient_ref, out_hbm, done.at[0])
    copy.start()
    total = jnp.sum(table_of(known_ref, opposite_ref), axis=0, keepdims=True)
    loss_ref[...] = jnp.sum(total, axis=1, keepdims=True) / count
    second = pltpu.make_async_copy(loss_ref, loss_hbm, done.at[1])
    second.start()
    copy.wait()
    second.wait()


def finish(gradient, known, opposite, count):
    vmem = pl.BlockSpec(memory_space=pltpu.VMEM)
    return pl.pallas_call(
        functools.partial(finish_kernel, count),
        out_shape=[
            jax.ShapeDtypeStruct(gradient.shape, f32),
            jax.ShapeDtypeStruct((1, 1), f32),
        ],
        in_specs=[vmem] * 3,
        out_specs=[pl.BlockSpec(memory_space=pltpu.HBM)] * 2,
        scratch_shapes=[pltpu.VMEM((1, 1), f32), pltpu.SemaphoreType.DMA((2,))],
        compiler_params=params,
        name="finish",
    )(gradient, known, opposite)


def hidden_grads(step, near_side, beside_ref, own_ref, slope_ref, weight_ref, wide):
    width = own_ref.shape[1]
    channels = (own_ref.shape[0] - slab_count) // 2
    even = is_even()
    below = even if near_side else jnp.logical_not(even)

    def take(ref, row):
        return ref[row * channels : (row + 1) * channels, :]

    first = jnp.where(below, 0, -2)
    for index in range(4):
        own, beside = take(own_ref, index % 2), take(beside_ref, index % 2)
        row = jnp.where(below, own, beside) if index < 2 else jnp.where(below, beside, own)
        put_windows(wide, index, jnp.where(inside(first + index), row, 0.0))
    grads = to_channels(weight_ref[...], wide, 0, channels) * slope_ref[step, jnp.where(below, 1, 0)]
    rows = []
    for half in range(2):
        row = grads[:, half * width : (half + 1) * width]
        rows.append(split(jnp.where(inside(first + 1 + half), row, 0.0)))
    return rows


def backward_near_kernel(step, own_ref, near_ref, slope_ref, outb_ref, high_ref, low_ref, wide_hi, wide_lo):
    rows = hidden_grads(step, True, near_ref, own_ref, slope_ref, outb_ref, (wide_hi, wide_lo))
    for half in range(2):
        high_ref[half], low_ref[half] = rows[half]


def backward_near(step, own, near, slopes, w_out):
    count, width = own.shape
    channels = (count - slab_count) // 2
    hidden = w_out.shape[0] // 2
    return pl.pallas_call(
        functools.partial(backward_near_kernel, step),
        out_shape=[jax.ShapeDtypeStruct((2, hidden, width), bf16)] * 2,
        scratch_shapes=[pltpu.VMEM((12 * channels, 2 * width), bf16)] * 2,
        compiler_params=params,
        name="backward_near",
    )(own, near, slopes, w_out)


def backward_kernel(step, own_ref, across_ref, slope_ref, high_ref, low_ref, outb_ref, inb_ref, *rest):
    added, tables = rest[:-5][:1], rest[:-5][1:]
    out_ref, wide_hi, wide_lo, hid_hi, hid_lo = rest[-5:]
    channels = (own_ref.shape[0] - slab_count) // 2
    hidden = outb_ref.shape[0] // 2
    hid = (hid_hi, hid_lo)
    even = is_even()
    rows = hidden_grads(step, False, across_ref, own_ref, slope_ref, outb_ref, (wide_hi, wide_lo))
    for half in range(2):
        known = (high_ref[half], low_ref[half])
        pairs = list(zip(rows[half], known))
        put_twice(hid, half, hidden, 0, [jnp.where(even, far, close) for far, close in pairs])
        put_twice(hid, 2 + half, hidden, 0, [jnp.where(even, close, far) for far, close in pairs])
    moved = from_channels(inb_ref[...], hid, 0, hidden, channels)
    for row in range(2):
        part = slice(row * channels, (row + 1) * channels)
        total = own_ref[part, :] + moved[row]
        for extra in added:
            total = total + extra[part, :]
        out_ref[part, :] = total
    if tables:
        out_ref[2 * channels :, :] = table_of(own_ref, across_ref, *tables)


def backward(step, own, across, slopes, close, w_out, w_in, *added):
    count, width = own.shape
    channels = (count - slab_count) // 2
    hidden = w_out.shape[0] // 2
    return pl.pallas_call(
        functools.partial(backward_kernel, step),
        out_shape=jax.ShapeDtypeStruct((count if step else 2 * channels, width), f32),
        scratch_shapes=[pltpu.VMEM((12 * channels, 2 * width), bf16)] * 2
        + [pltpu.VMEM((4 * hidden, 2 * width), bf16)] * 2,
        compiler_params=params,
        name="backward",
    )(own, across, slopes, *close, w_out, w_in, *added)


def on_device(initial_states, targets, lat_weight, weight_in, weight_out, hidden_bias):
    members = lax.axis_size(MEMBER)
    slabs = lax.axis_size(LAT)
    steps, slab_rows, channels, width = targets.shape
    rows = slabs * slab_rows
    near = [(i, i ^ 1) for i in range(slabs)]
    across = [(i, (i + 1 if i % 2 else i - 1) % slabs) for i in range(slabs)]

    own = initial_states[0]
    beside = lax.ppermute(own, LAT, near)
    crossed = lax.ppermute(own, LAT, across)
    ready = prepare(weight_in.T, weight_out, hidden_bias[None, :], lat_weight[None, :], width)
    crossed, beside, ready = lax.optimization_barrier((crossed, beside, ready))
    far_crossed = lax.ppermute(beside, LAT, across)
    far_beside = lax.ppermute(crossed, LAT, near)
    w_in, w_out, bias, lat_weights = ready
    before_first, field, *hid = inner(own, beside, crossed, bias, w_in, w_out)
    before_second, fields = outer(
        beside, crossed, far_crossed, far_beside, field, hid, bias, w_in, w_out
    )
    height = steps * slab_rows * channels // members
    chunks = lax.all_to_all(
        fields.reshape(members, height, width), MEMBER, split_axis=0, concat_axis=0, tiled=True
    )
    grads = crps(lat_weights, chunks, targets.reshape(members, height, width))
    grads = lax.all_to_all(grads, MEMBER, split_axis=0, concat_axis=0, tiled=True)
    grads, before_first = lax.optimization_barrier((grads, before_first))
    back = prepare_back(weight_in.T, weight_out, before_first, before_second)
    w_out_back, w_in_back, slopes = back
    first_grads, message, known = collect(grads)

    beside = lax.ppermute(message, LAT, near)
    crossed = lax.ppermute(message, LAT, across)
    far = lax.ppermute(known, LAT, [(i, i ^ 4) for i in range(slabs)])
    close = backward_near(1, message, beside, slopes, w_out_back)
    message = backward(
        1, message, crossed, slopes, close, w_out_back, w_in_back, first_grads, beside, far
    )
    beside = lax.ppermute(message, LAT, near)
    crossed = lax.ppermute(message, LAT, across)
    close = backward_near(0, message, beside, slopes, w_out_back)
    crossed, close = lax.optimization_barrier((crossed, close))
    known = merge(message, beside, crossed)
    gradient = backward(0, message, crossed, slopes, close, w_out_back, w_in_back)
    opposite = lax.ppermute(known, LAT, [(i, i ^ 8) for i in range(slabs)])
    gradient, loss = finish(
        gradient, known, opposite, members * steps * rows * channels * width
    )
    loss = loss.reshape(())
    return gradient.reshape(initial_states.shape), loss


def solution(mesh):
    torus = Mesh(
        mesh.devices.reshape(4, 2, 2, 4, 2), ("member_0", "member_1", "lat_0", "lat_1", "lat_2")
    )
    placed = (P(MEMBER, LAT, None, None), P(None, LAT, None, None), P(LAT), P(), P(), P())
    return jax.shard_map(
        on_device,
        mesh=torus,
        in_specs=placed,
        out_specs=(P(MEMBER, LAT, None, None), P()),
        check_vma=False,
    )
```

```python
import functools

import jax
import jax.numpy as jnp
from jax import lax
from jax.experimental import pallas as pl
from jax.experimental.pallas import tpu as pltpu
from jax.sharding import Mesh
from jax.sharding import PartitionSpec as P

MEMBER = ("member_0", "member_1")
LAT = ("lat_0", "lat_1", "lat_2")

smooth_width = 0.1
gelu_scale = 0.7978845608028654
gelu_cubic = 0.044715
slab_count = 16

f32 = jnp.float32
bf16 = jnp.bfloat16
params = pltpu.CompilerParams(vmem_limit_bytes=16 * 1024 * 1024)


def split(value):
    high = value.astype(bf16)
    return high, (value - high.astype(f32)).astype(bf16)


def product(left, right):
    dot = functools.partial(jnp.dot, preferred_element_type=f32)
    count = left.shape[0] // 2
    both = dot(left, right[0])
    return both[:count] + (both[count:] + dot(left[:count], right[1]))


def from_left(row):
    lane = lax.broadcasted_iota(jnp.int32, row.shape, 1)
    return jnp.where(lane == 0, 0.0, pltpu.roll(row, 1, 1))


def from_right(row):
    lane = lax.broadcasted_iota(jnp.int32, row.shape, 1)
    return jnp.where(lane == row.shape[1] - 1, 0.0, pltpu.roll(row, row.shape[1] - 1, 1))


def put(refs, start, values):
    for ref, value in zip(refs, values):
        ref[start : start + value.shape[0], :] = value


def put_windows(refs, index, row):
    channels = row.shape[0]
    for part, shifted in enumerate((from_left(row), row, from_right(row))):
        put(refs, (3 * index + part) * channels, split(shifted))


def read(refs, start, size, height):
    parts = [(ref[start : start + size, :], ref[start + height : start + height + size, :]) for ref in refs]
    return tuple(jnp.concatenate(part, axis=1) for part in parts)


def to_channels(weights, windows, pair, channels):
    return product(weights, read(windows, pair * 3 * channels, 9 * channels, 3 * channels))


def from_channels(weights, hidden, pair, channels, outer):
    mixed = product(weights, read(hidden, pair * channels, 3 * channels, channels))
    width = mixed.shape[1] // 2
    rows = []
    for half in range(2):
        part = mixed[:, half * width : (half + 1) * width]
        rows.append(
            from_left(part[:outer])
            + part[outer : 2 * outer]
            + from_right(part[2 * outer :])
        )
    return rows


def gelu(x, half):
    t = jnp.tanh(x * (gelu_scale + (gelu_scale * gelu_cubic) * (x * x)))
    h = half * x
    return h + h * t


def gelu_slope(x):
    t = jnp.tanh(gelu_scale * (x + gelu_cubic * x * x * x))
    inner = gelu_scale * (1.0 + 3.0 * gelu_cubic * x * x)
    return 0.5 * (1.0 + t) + 0.5 * x * (1.0 - t * t) * inner


def fetch(pairs, arrived):
    copies = [pltpu.make_async_copy(*pair, arrived.at[i]) for i, pair in enumerate(pairs)]
    for copy in copies:
        copy.start()
    for copy in copies:
        copy.wait()


def prepare_kernel(win_hbm, wout_hbm, bias_hbm, lat_hbm, in_ref, out_ref, wide_bias_ref, wide_lat_ref,
                   win_ref, wout_ref, bias_ref, lat_ref, arrived):
    fetch(((win_hbm, win_ref), (wout_hbm, wout_ref), (bias_hbm, bias_ref), (lat_hbm, lat_ref)), arrived)
    outer, width = wout_ref.shape
    hidden = width // 9
    in_ref[:hidden, :], in_ref[hidden:, :] = split(win_ref[...].T)
    for a in range(3):
        for b in range(3):
            tap = 3 * a + b
            high, low = split(wout_ref[:, tap * hidden : (tap + 1) * hidden])
            out_ref[b * outer : (b + 1) * outer, a * hidden : (a + 1) * hidden] = high
            out_ref[(3 + b) * outer : (4 + b) * outer, a * hidden : (a + 1) * hidden] = low
    wide_bias_ref[...] = jnp.broadcast_to(bias_ref[...], wide_bias_ref.shape[::-1]).T
    for row in range(2):
        one = jnp.broadcast_to(lat_ref[:, row : row + 1], (8, wide_lat_ref.shape[1]))
        wide_lat_ref[8 * row : 8 * (row + 1), :] = one


def prepare(weight_in, weight_out, bias, lat_weight, width):
    taps_in, hidden = weight_in.shape
    outer = weight_out.shape[0]
    arrays = (weight_in, weight_out, bias, lat_weight)
    shapes = [(2 * hidden, taps_in), (6 * outer, 3 * hidden)]
    return pl.pallas_call(
        prepare_kernel,
        out_shape=[jax.ShapeDtypeStruct(shape, bf16) for shape in shapes]
        + [jax.ShapeDtypeStruct((hidden, width), f32), jax.ShapeDtypeStruct((16, width), f32)],
        in_specs=[pl.BlockSpec(memory_space=pltpu.HBM)] * 4,
        scratch_shapes=[pltpu.VMEM(array.shape, f32) for array in arrays] + [pltpu.SemaphoreType.DMA((4,))],
        compiler_params=params,
        name="prepare",
    )(*(pltpu.with_memory_space_constraint(array, pltpu.HBM) for array in arrays))


def prepare_back_kernel(win_hbm, wout_hbm, first_ref, second_ref, outb_ref, inb_ref, slope_ref,
                        stack, win_ref, wout_ref, arrived):
    pairs = ((win_hbm, win_ref), (wout_hbm, wout_ref))
    copies = [pltpu.make_async_copy(*pair, arrived.at[i]) for i, pair in enumerate(pairs)]
    for copy in copies:
        copy.start()
    for step, before_ref in enumerate((first_ref, second_ref)):
        for pair in range(2):
            slope = gelu_slope(before_ref[pair])
            width = slope.shape[1] // 2
            for half in range(2):
                part = slope[:, half * width : (half + 1) * width]
                if pair != half:
                    slope_ref[step, pair, :, half * width : (half + 1) * width] = part
                else:
                    part = jnp.where(inside(3 * pair - 1), part, 0.0)
                    slope_ref[step, pair, :, half * width : (half + 1) * width] = part
    for copy in copies:
        copy.wait()
    outer, width = wout_ref.shape
    hidden = width // 9
    inner = win_ref.shape[0] // 9
    for a in range(3):
        for b in range(3):
            tap = 3 * a + b
            stack[(8 - tap) * outer : (9 - tap) * outer, :] = wout_ref[:, tap * hidden : (tap + 1) * hidden]
            high, low = split(win_ref[tap * inner : (tap + 1) * inner, :])
            j, k = 2 - a, 2 - b
            inb_ref[k * inner : (k + 1) * inner, j * hidden : (j + 1) * hidden] = high
            inb_ref[(3 + k) * inner : (4 + k) * inner, j * hidden : (j + 1) * hidden] = low
    outb_ref[:hidden, :], outb_ref[hidden:, :] = split(stack[...].T)


def prepare_back(weight_in, weight_out, first, second):
    taps_in, hidden = weight_in.shape
    outer = weight_out.shape[0]
    inner = taps_in // 9
    arrays = (weight_in, weight_out)
    shapes = [(2 * hidden, 9 * outer), (6 * inner, 3 * hidden)]
    hbm = pl.BlockSpec(memory_space=pltpu.HBM)
    return pl.pallas_call(
        prepare_back_kernel,
        out_shape=[jax.ShapeDtypeStruct(shape, bf16) for shape in shapes]
        + [jax.ShapeDtypeStruct((2, *first.shape), f32)],
        in_specs=[hbm, hbm] + [pl.BlockSpec(memory_space=pltpu.VMEM)] * 2,
        scratch_shapes=[pltpu.VMEM((9 * outer, hidden), f32)]
        + [pltpu.VMEM(array.shape, f32) for array in arrays]
        + [pltpu.SemaphoreType.DMA((2,))],
        compiler_params=params,
        name="prepare_back",
    )(*(pltpu.with_memory_space_constraint(array, pltpu.HBM) for array in arrays), first, second)


def inside(row):
    index = lax.axis_index(LAT) * 2 + row
    return (index >= 0) & (index < 2 * slab_count)


def is_even():
    return lax.rem(lax.axis_index(LAT), 2) == 0


def either(first, second):
    return lambda row: jnp.where(is_even(), first[row], second[row])


def activate(before, first, hid, index, hidden, width):
    for half in range(2):
        row = first + half
        scale = 0.5 if row in (0, 1) else jnp.where(inside(row), 0.5, 0.0)
        active = gelu(before[:, half * width : (half + 1) * width], scale)
        put(hid, (index + half) * hidden, split(active))


def inner_kernel(own_ref, near_ref, across_ref, bias_ref, in_ref, out_ref, before_ref, field_ref, hid_hi, hid_lo,
                 wide_hi, wide_lo):
    channels, width = own_ref.shape[1:]
    hidden = in_ref.shape[0] // 2
    wide = (wide_hi, wide_lo)
    hid = (hid_hi, hid_lo)
    bias = jnp.concatenate([bias_ref[...]] * 2, axis=1)
    slabs = (either(across_ref, near_ref), lambda row: own_ref[row], either(near_ref, across_ref))
    for index in range(6):
        row = slabs[index // 2](index % 2)
        if index // 2 != 1:
            row = jnp.where(inside(index - 2), row, 0.0)
        put_windows(wide, index, row)
    for pair in (0, 2):
        before = to_channels(in_ref[...], wide, pair, channels) + bias
        before_ref[pair // 2] = before
        activate(before, pair - 1, hid, pair, hidden, width)
    moved = from_channels(out_ref[...], hid, 0, hidden, channels)
    for row in range(2):
        field_ref[row * channels : (row + 1) * channels, :] = own_ref[row] + moved[row]


def inner(own, near, across, bias, w_in, w_out):
    channels, width = own.shape[1:]
    hidden = w_in.shape[0] // 2
    return pl.pallas_call(
        inner_kernel,
        out_shape=[
            jax.ShapeDtypeStruct((2, hidden, 2 * width), f32),
            jax.ShapeDtypeStruct((2 * channels, width), f32),
        ]
        + [jax.ShapeDtypeStruct((4 * hidden, width), bf16)] * 2,
        scratch_shapes=[pltpu.VMEM((18 * channels, width), bf16)] * 2,
        compiler_params=params,
        name="inner",
    )(own, near, across, bias, w_in, w_out)


def outer_kernel(near_ref, across_ref, far_across_ref, far_near_ref, field_ref, hid_hi, hid_lo, bias_ref, in_ref,
                 out_ref, before_ref, fields_ref, wide_hi, wide_lo, side_hi, side_lo):
    channels, width = near_ref.shape[1:]
    hidden = in_ref.shape[0] // 2
    wide = (wide_hi, wide_lo)
    side = (side_hi, side_lo)
    bias = jnp.concatenate([bias_ref[...]] * 2, axis=1)
    fields = [None, None] + [field_ref[row * channels : (row + 1) * channels, :] for row in range(2)] + [None, None]
    sides = (
        (-4, (either(far_across_ref, far_near_ref), either(across_ref, near_ref))),
        (2, (either(near_ref, across_ref), either(far_near_ref, far_across_ref))),
    )
    rows = []
    for after, (first, slabs) in enumerate(sides):
        for index in range(4):
            row = jnp.where(inside(first + index), slabs[index // 2](index % 2), 0.0)
            rows.append(row)
            put_windows(wide, 4 * after + index, row)
        for ref, known in zip(side, (hid_hi, hid_lo)):
            ref[(2 + 2 * after) * hidden : (4 + 2 * after) * hidden, :] = known[
                2 * after * hidden : 2 * (after + 1) * hidden, :
            ]
    before = [to_channels(in_ref[...], wide, 4 * after, channels) + bias for after in range(2)]
    activate(before[0], -3, side, 0, hidden, width)
    activate(before[1], 3, side, 6, hidden, width)
    for after in range(2):
        moved = from_channels(out_ref[...], side, 4 * after, hidden, channels)
        for row in range(2):
            at = 4 * after + row
            value = rows[2 + 2 * after + row] + moved[row]
            fields[at] = jnp.where(inside(at - 2), value, 0.0)
    for index in range(6):
        put_windows(wide, index, fields[index])
    for pair in (0, 2):
        before = to_channels(in_ref[...], wide, pair, channels) + bias
        before_ref[pair // 2] = before
        activate(before, pair - 1, side, pair, hidden, width)
    moved = from_channels(out_ref[...], side, 0, hidden, channels)
    for row in range(2):
        fields_ref[row * channels : (row + 1) * channels, :] = fields[2 + row]
        fields_ref[(2 + row) * channels : (3 + row) * channels, :] = fields[2 + row] + moved[row]


def outer(near, across, far_across, far_near, field, hid, bias, w_in, w_out):
    channels, width = near.shape[1:]
    hidden = w_in.shape[0] // 2
    return pl.pallas_call(
        outer_kernel,
        out_shape=[
            jax.ShapeDtypeStruct((2, hidden, 2 * width), f32),
            jax.ShapeDtypeStruct((4 * channels, width), f32),
        ],
        scratch_shapes=[pltpu.VMEM((24 * channels, width), bf16)] * 2
        + [pltpu.VMEM((8 * hidden, width), bf16)] * 2,
        compiler_params=params,
        name="outer",
    )(near, across, far_across, far_near, field, *hid, bias, w_in, w_out)


def crps_kernel(weight_ref, fields_ref, targets_ref, out_ref):
    members, height, width = fields_ref.shape
    mine = lax.axis_index(MEMBER)
    weight = jnp.where(lax.rem(lax.div(mine, 2), 2) == 0, weight_ref[:8, :], weight_ref[8:, :])
    softness = smooth_width * smooth_width
    loss = jnp.zeros((8, width), f32)
    for tile in range(0, height, 8):
        values = [fields_ref[m, tile : tile + 8, :] for m in range(members)]
        truth = targets_ref[mine, tile : tile + 8, :]
        direct = jnp.zeros((8, width), f32)
        pairs = jnp.full((8, width), members * smooth_width, f32)
        slopes = [jnp.zeros((8, width), f32) for m in range(members)]
        grads = []
        for m in range(members):
            error = values[m] - truth
            square = error * error + softness
            inverse = lax.rsqrt(square)
            direct = direct + square * inverse
            grads.append(error * inverse)
            for other in range(m + 1, members):
                gap = values[m] - values[other]
                square = gap * gap + softness
                inverse = lax.rsqrt(square)
                pairs = pairs + 2.0 * square * inverse
                slope = gap * inverse
                slopes[m] = slopes[m] + slope
                slopes[other] = slopes[other] - slope
        loss = loss + weight * (direct - pairs / (2.0 * (members - 1)))
        for m in range(members):
            out_ref[m, tile : tile + 8, :] = weight * (grads[m] - slopes[m] / (members - 1))
    for m in range(members):
        out_ref[m, height : height + 8, :] = loss


def crps(weights, fields, targets):
    members, height, width = fields.shape
    return pl.pallas_call(
        crps_kernel,
        out_shape=jax.ShapeDtypeStruct((members, height + 8, width), f32),
        compiler_params=params,
        name="crps",
    )(weights, fields, targets)


def collect_kernel(grads_ref, first_ref, second_ref, known_ref):
    chunks, height, width = grads_ref.shape
    height = height - 8
    half = chunks // 2
    total = grads_ref[0, height : height + 8, :]
    for chunk in range(1, chunks):
        total = total + grads_ref[chunk, height : height + 8, :]
    for chunk in range(half):
        first_ref[chunk * height : (chunk + 1) * height, :] = grads_ref[chunk, :height, :]
        second_ref[chunk * height : (chunk + 1) * height, :] = grads_ref[half + chunk, :height, :]
    known = jnp.broadcast_to(jnp.sum(total, axis=0, keepdims=True), (slab_count, width))
    slab = lax.broadcasted_iota(jnp.int32, known.shape, 0)
    known = jnp.where(slab == lax.axis_index(LAT), known, 0.0)
    second_ref[half * height :, :] = known
    known_ref[...] = known


def collect(grads):
    chunks, height, width = grads.shape
    count = chunks // 2 * (height - 8)
    return pl.pallas_call(
        collect_kernel,
        out_shape=[
            jax.ShapeDtypeStruct((count, width), f32),
            jax.ShapeDtypeStruct((count + slab_count, width), f32),
            jax.ShapeDtypeStruct((slab_count, width), f32),
        ],
        compiler_params=params,
        name="collect",
    )(grads)


def merged(*known):
    result = known[0]
    for other in known[1:]:
        result = jnp.where(result != 0.0, result, other)
    return result


def table_of(*refs):
    return merged(*(ref[ref.shape[0] - slab_count :, :] for ref in refs))


def merge_kernel(*refs):
    refs[-1][...] = table_of(*refs[:-1])


def merge(*messages):
    return pl.pallas_call(
        merge_kernel,
        out_shape=jax.ShapeDtypeStruct((slab_count, messages[0].shape[1]), f32),
        compiler_params=params,
        name="merge",
    )(*messages)


def finish_kernel(count, gradient_ref, known_ref, opposite_ref, out_hbm, loss_hbm, loss_ref, done):
    copy = pltpu.make_async_copy(gradient_ref, out_hbm, done.at[0])
    copy.start()
    total = jnp.sum(table_of(known_ref, opposite_ref), axis=0, keepdims=True)
    loss_ref[...] = jnp.sum(total, axis=1, keepdims=True) / count
    second = pltpu.make_async_copy(loss_ref, loss_hbm, done.at[1])
    second.start()
    copy.wait()
    second.wait()


def finish(gradient, known, opposite, count):
    vmem = pl.BlockSpec(memory_space=pltpu.VMEM)
    return pl.pallas_call(
        functools.partial(finish_kernel, count),
        out_shape=[
            jax.ShapeDtypeStruct(gradient.shape, f32),
            jax.ShapeDtypeStruct((1, 1), f32),
        ],
        in_specs=[vmem] * 3,
        out_specs=[pl.BlockSpec(memory_space=pltpu.HBM)] * 2,
        scratch_shapes=[pltpu.VMEM((1, 1), f32), pltpu.SemaphoreType.DMA((2,))],
        compiler_params=params,
        name="finish",
    )(gradient, known, opposite)


def hidden_grads(step, near_side, beside_ref, own_ref, slope_ref, weight_ref, wide):
    width = own_ref.shape[1]
    channels = (own_ref.shape[0] - slab_count) // 2
    even = is_even()
    below = even if near_side else jnp.logical_not(even)

    def take(ref, row):
        return ref[row * channels : (row + 1) * channels, :]

    first = jnp.where(below, 0, -2)
    for index in range(4):
        own, beside = take(own_ref, index % 2), take(beside_ref, index % 2)
        row = jnp.where(below, own, beside) if index < 2 else jnp.where(below, beside, own)
        put_windows(wide, index, jnp.where(inside(first + index), row, 0.0))
    grads = to_channels(weight_ref[...], wide, 0, channels) * slope_ref[step, jnp.where(below, 1, 0)]
    rows = []
    for half in range(2):
        row = grads[:, half * width : (half + 1) * width]
        rows.append(split(row))
    return rows


def backward_side_kernel(step, near_side, own_ref, beside_ref, slope_ref, outb_ref, high_ref, low_ref, wide_hi,
                         wide_lo):
    rows = hidden_grads(step, near_side, beside_ref, own_ref, slope_ref, outb_ref, (wide_hi, wide_lo))
    for half in range(2):
        high_ref[half], low_ref[half] = rows[half]


def backward_side(step, near_side, own, beside, slopes, w_out):
    count, width = own.shape
    channels = (count - slab_count) // 2
    hidden = w_out.shape[0] // 2
    return pl.pallas_call(
        functools.partial(backward_side_kernel, step, near_side),
        out_shape=[jax.ShapeDtypeStruct((2, hidden, width), bf16)] * 2,
        scratch_shapes=[pltpu.VMEM((12 * channels, width), bf16)] * 2,
        compiler_params=params,
        name="backward_near" if near_side else "backward_across",
    )(own, beside, slopes, w_out)


def join_kernel(own_ref, close_hi, close_lo, far_hi, far_lo, inb_ref, *rest):
    added, tables = rest[:-3][:1], rest[:-3][1:]
    out_ref, hid_hi, hid_lo = rest[-3:]
    channels = (own_ref.shape[0] - slab_count) // 2
    hidden = close_hi.shape[1]
    even = is_even()
    for half in range(2):
        far = pl.multiple_of(jnp.where(even, half, 2 + half) * hidden, hidden)
        close = pl.multiple_of(jnp.where(even, 2 + half, half) * hidden, hidden)
        for ref, far_ref, close_ref in ((hid_hi, far_hi, close_hi), (hid_lo, far_lo, close_lo)):
            ref[pl.ds(far, hidden), :] = far_ref[half]
            ref[pl.ds(close, hidden), :] = close_ref[half]
    moved = from_channels(inb_ref[...], (hid_hi, hid_lo), 0, hidden, channels)
    for row in range(2):
        part = slice(row * channels, (row + 1) * channels)
        total = own_ref[part, :] + moved[row]
        for extra in added:
            total = total + extra[part, :]
        out_ref[part, :] = total
    if tables:
        out_ref[2 * channels :, :] = table_of(own_ref, *tables)


def join(own, close, far, w_in, *added):
    count, width = own.shape
    channels = (count - slab_count) // 2
    hidden = close[0].shape[1]
    return pl.pallas_call(
        join_kernel,
        out_shape=jax.ShapeDtypeStruct((count if added else 2 * channels, width), f32),
        scratch_shapes=[pltpu.VMEM((4 * hidden, width), bf16)] * 2,
        compiler_params=params,
        name="join",
    )(own, *close, *far, w_in, *added)


def on_device(initial_states, targets, lat_weight, weight_in, weight_out, hidden_bias):
    members = lax.axis_size(MEMBER)
    slabs = lax.axis_size(LAT)
    steps, slab_rows, channels, width = targets.shape
    rows = slabs * slab_rows
    near = [(i, i ^ 1) for i in range(slabs)]
    across = [(i, (i + 1 if i % 2 else i - 1) % slabs) for i in range(slabs)]

    own = initial_states[0]
    beside = lax.ppermute(own, LAT, near)
    crossed = lax.ppermute(own, LAT, across)
    ready = prepare(weight_in.T, weight_out, hidden_bias[None, :], lat_weight[None, :], width)
    crossed, beside, ready = lax.optimization_barrier((crossed, beside, ready))
    far_crossed = lax.ppermute(beside, LAT, across)
    far_beside = lax.ppermute(crossed, LAT, near)
    w_in, w_out, bias, lat_weights = ready
    before_first, field, *hid = inner(own, beside, crossed, bias, w_in, w_out)
    before_second, fields = outer(
        beside, crossed, far_crossed, far_beside, field, hid, bias, w_in, w_out
    )
    height = steps * slab_rows * channels // members
    chunks = lax.all_to_all(
        fields.reshape(members, height, width), MEMBER, split_axis=0, concat_axis=0, tiled=True
    )
    grads = crps(lat_weights, chunks, targets.reshape(members, height, width))
    grads = lax.all_to_all(grads, MEMBER, split_axis=0, concat_axis=0, tiled=True)
    back = prepare_back(weight_in.T, weight_out, before_first, before_second)
    w_out_back, w_in_back, slopes = back
    first_grads, message, known = collect(grads)

    beside = lax.ppermute(message, LAT, near)
    crossed = lax.ppermute(message, LAT, across)
    far = lax.ppermute(known, LAT, [(i, i ^ 4) for i in range(slabs)])
    close = backward_side(1, True, message, beside, slopes, w_out_back)
    crossed, close = lax.optimization_barrier((crossed, close))
    distant = backward_side(1, False, message, crossed, slopes, w_out_back)
    message = join(message, close, distant, w_in_back, first_grads, beside, crossed, far)
    beside = lax.ppermute(message, LAT, near)
    crossed = lax.ppermute(message, LAT, across)
    close = backward_side(0, True, message, beside, slopes, w_out_back)
    crossed, close = lax.optimization_barrier((crossed, close))
    known = merge(message, beside, crossed)
    distant = backward_side(0, False, message, crossed, slopes, w_out_back)
    gradient = join(message, close, distant, w_in_back)
    opposite = lax.ppermute(known, LAT, [(i, i ^ 8) for i in range(slabs)])
    gradient, loss = finish(
        gradient, known, opposite, members * steps * rows * channels * width
    )
    loss = loss.reshape(())
    return gradient.reshape(initial_states.shape), loss


def solution(mesh):
    torus = Mesh(
        mesh.devices.reshape(4, 2, 2, 4, 2), ("member_0", "member_1", "lat_0", "lat_1", "lat_2")
    )
    placed = (P(MEMBER, LAT, None, None), P(None, LAT, None, None), P(LAT), P(), P(), P())
    return jax.shard_map(
        on_device,
        mesh=torus,
        in_specs=placed,
        out_specs=(P(MEMBER, LAT, None, None), P()),
        check_vma=False,
    )
```

```python
import functools

import jax
import jax.numpy as jnp
from jax import lax
from jax.experimental import pallas as pl
from jax.experimental.pallas import tpu as pltpu
from jax.sharding import Mesh
from jax.sharding import PartitionSpec as P

MEMBER = ("member_0", "member_1")
LAT = ("lat_0", "lat_1", "lat_2")

smooth_width = 0.1
gelu_scale = 0.7978845608028654
gelu_cubic = 0.044715
slab_count = 16

f32 = jnp.float32
bf16 = jnp.bfloat16
params = pltpu.CompilerParams(vmem_limit_bytes=16 * 1024 * 1024)


def split(value):
    high = value.astype(bf16)
    return high, (value - high.astype(f32)).astype(bf16)


def product(left, right):
    dot = functools.partial(jnp.dot, preferred_element_type=f32)
    count = left.shape[0] // 2
    both = dot(left, right[0])
    return both[:count] + (both[count:] + dot(left[:count], right[1]))


def from_left(row):
    lane = lax.broadcasted_iota(jnp.int32, row.shape, 1)
    return jnp.where(lane == 0, 0.0, pltpu.roll(row, 1, 1))


def from_right(row):
    lane = lax.broadcasted_iota(jnp.int32, row.shape, 1)
    return jnp.where(lane == row.shape[1] - 1, 0.0, pltpu.roll(row, row.shape[1] - 1, 1))


def put(refs, start, values):
    for ref, value in zip(refs, values):
        ref[start : start + value.shape[0], :] = value


def put_windows(refs, index, row):
    channels = row.shape[0]
    for part, shifted in enumerate((from_left(row), row, from_right(row))):
        put(refs, (3 * index + part) * channels, split(shifted))


def read(refs, start, size, height):
    parts = [(ref[start : start + size, :], ref[start + height : start + height + size, :]) for ref in refs]
    return tuple(jnp.concatenate(part, axis=1) for part in parts)


def to_channels(weights, windows, pair, channels):
    return product(weights, read(windows, pair * 3 * channels, 9 * channels, 3 * channels))


def from_channels(weights, hidden, pair, channels, outer):
    mixed = product(weights, read(hidden, pair * channels, 3 * channels, channels))
    width = mixed.shape[1] // 2
    rows = []
    for half in range(2):
        part = mixed[:, half * width : (half + 1) * width]
        rows.append(
            from_left(part[:outer])
            + part[outer : 2 * outer]
            + from_right(part[2 * outer :])
        )
    return rows


def gelu(x, half):
    t = jnp.tanh(x * (gelu_scale + (gelu_scale * gelu_cubic) * (x * x)))
    h = half * x
    return h + h * t


def gelu_slope(x):
    t = jnp.tanh(gelu_scale * (x + gelu_cubic * x * x * x))
    inner = gelu_scale * (1.0 + 3.0 * gelu_cubic * x * x)
    return 0.5 * (1.0 + t) + 0.5 * x * (1.0 - t * t) * inner


def fetch(pairs, arrived):
    copies = [pltpu.make_async_copy(*pair, arrived.at[i]) for i, pair in enumerate(pairs)]
    for copy in copies:
        copy.start()
    for copy in copies:
        copy.wait()


def prepare_kernel(win_hbm, wout_hbm, bias_hbm, lat_hbm, in_ref, out_ref, wide_bias_ref, wide_lat_ref,
                   win_ref, wout_ref, bias_ref, lat_ref, arrived):
    fetch(((win_hbm, win_ref), (wout_hbm, wout_ref), (bias_hbm, bias_ref), (lat_hbm, lat_ref)), arrived)
    outer, width = wout_ref.shape
    hidden = width // 9
    in_ref[:hidden, :], in_ref[hidden:, :] = split(win_ref[...].T)
    for a in range(3):
        for b in range(3):
            tap = 3 * a + b
            high, low = split(wout_ref[:, tap * hidden : (tap + 1) * hidden])
            out_ref[b * outer : (b + 1) * outer, a * hidden : (a + 1) * hidden] = high
            out_ref[(3 + b) * outer : (4 + b) * outer, a * hidden : (a + 1) * hidden] = low
    wide_bias_ref[...] = jnp.broadcast_to(bias_ref[...], wide_bias_ref.shape[::-1]).T
    for row in range(2):
        one = jnp.broadcast_to(lat_ref[:, row : row + 1], (8, wide_lat_ref.shape[1]))
        wide_lat_ref[8 * row : 8 * (row + 1), :] = one


def prepare(weight_in, weight_out, bias, lat_weight, width):
    taps_in, hidden = weight_in.shape
    outer = weight_out.shape[0]
    arrays = (weight_in, weight_out, bias, lat_weight)
    shapes = [(2 * hidden, taps_in), (6 * outer, 3 * hidden)]
    return pl.pallas_call(
        prepare_kernel,
        out_shape=[jax.ShapeDtypeStruct(shape, bf16) for shape in shapes]
        + [jax.ShapeDtypeStruct((hidden, width), f32), jax.ShapeDtypeStruct((16, width), f32)],
        in_specs=[pl.BlockSpec(memory_space=pltpu.HBM)] * 4,
        scratch_shapes=[pltpu.VMEM(array.shape, f32) for array in arrays] + [pltpu.SemaphoreType.DMA((4,))],
        compiler_params=params,
        name="prepare",
    )(*(pltpu.with_memory_space_constraint(array, pltpu.HBM) for array in arrays))


def prepare_back_kernel(win_hbm, wout_hbm, first_ref, second_ref, outb_ref, inb_ref, slope_ref,
                        stack, win_ref, wout_ref, arrived):
    pairs = ((win_hbm, win_ref), (wout_hbm, wout_ref))
    copies = [pltpu.make_async_copy(*pair, arrived.at[i]) for i, pair in enumerate(pairs)]
    for copy in copies:
        copy.start()
    for step, before_ref in enumerate((first_ref, second_ref)):
        for pair in range(2):
            slope = gelu_slope(before_ref[pair])
            width = slope.shape[1] // 2
            for half in range(2):
                part = slope[:, half * width : (half + 1) * width]
                if pair != half:
                    slope_ref[step, pair, :, half * width : (half + 1) * width] = part
                else:
                    part = jnp.where(inside(3 * pair - 1), part, 0.0)
                    slope_ref[step, pair, :, half * width : (half + 1) * width] = part
    for copy in copies:
        copy.wait()
    outer, width = wout_ref.shape
    hidden = width // 9
    inner = win_ref.shape[0] // 9
    for a in range(3):
        for b in range(3):
            tap = 3 * a + b
            stack[(8 - tap) * outer : (9 - tap) * outer, :] = wout_ref[:, tap * hidden : (tap + 1) * hidden]
            high, low = split(win_ref[tap * inner : (tap + 1) * inner, :])
            j, k = 2 - a, 2 - b
            inb_ref[k * inner : (k + 1) * inner, j * hidden : (j + 1) * hidden] = high
            inb_ref[(3 + k) * inner : (4 + k) * inner, j * hidden : (j + 1) * hidden] = low
    outb_ref[:hidden, :], outb_ref[hidden:, :] = split(stack[...].T)


def prepare_back(weight_in, weight_out, first, second):
    taps_in, hidden = weight_in.shape
    outer = weight_out.shape[0]
    inner = taps_in // 9
    arrays = (weight_in, weight_out)
    shapes = [(2 * hidden, 9 * outer), (6 * inner, 3 * hidden)]
    hbm = pl.BlockSpec(memory_space=pltpu.HBM)
    return pl.pallas_call(
        prepare_back_kernel,
        out_shape=[jax.ShapeDtypeStruct(shape, bf16) for shape in shapes]
        + [jax.ShapeDtypeStruct((2, *first.shape), f32)],
        in_specs=[hbm, hbm] + [pl.BlockSpec(memory_space=pltpu.VMEM)] * 2,
        scratch_shapes=[pltpu.VMEM((9 * outer, hidden), f32)]
        + [pltpu.VMEM(array.shape, f32) for array in arrays]
        + [pltpu.SemaphoreType.DMA((2,))],
        compiler_params=params,
        name="prepare_back",
    )(*(pltpu.with_memory_space_constraint(array, pltpu.HBM) for array in arrays), first, second)


def inside(row):
    index = lax.axis_index(LAT) * 2 + row
    return (index >= 0) & (index < 2 * slab_count)


def is_even():
    return lax.rem(lax.axis_index(LAT), 2) == 0


def either(first, second):
    return lambda row: jnp.where(is_even(), first[row], second[row])


def activate(before, first, hid, index, hidden, width):
    for half in range(2):
        row = first + half
        scale = 0.5 if row in (0, 1) else jnp.where(inside(row), 0.5, 0.0)
        active = gelu(before[:, half * width : (half + 1) * width], scale)
        put(hid, (index + half) * hidden, split(active))


def inner_kernel(own_ref, near_ref, across_ref, bias_ref, in_ref, out_ref, before_ref, field_ref, hid_hi, hid_lo,
                 wide_hi, wide_lo):
    channels, width = own_ref.shape[1:]
    hidden = in_ref.shape[0] // 2
    wide = (wide_hi, wide_lo)
    hid = (hid_hi, hid_lo)
    bias = jnp.concatenate([bias_ref[...]] * 2, axis=1)
    slabs = (either(across_ref, near_ref), lambda row: own_ref[row], either(near_ref, across_ref))
    for index in range(6):
        row = slabs[index // 2](index % 2)
        if index // 2 != 1:
            row = jnp.where(inside(index - 2), row, 0.0)
        put_windows(wide, index, row)
    for pair in (0, 2):
        before = to_channels(in_ref[...], wide, pair, channels) + bias
        before_ref[pair // 2] = before
        activate(before, pair - 1, hid, pair, hidden, width)
    moved = from_channels(out_ref[...], hid, 0, hidden, channels)
    for row in range(2):
        field_ref[row * channels : (row + 1) * channels, :] = own_ref[row] + moved[row]


def inner(own, near, across, bias, w_in, w_out):
    channels, width = own.shape[1:]
    hidden = w_in.shape[0] // 2
    return pl.pallas_call(
        inner_kernel,
        out_shape=[
            jax.ShapeDtypeStruct((2, hidden, 2 * width), f32),
            jax.ShapeDtypeStruct((2 * channels, width), f32),
        ]
        + [jax.ShapeDtypeStruct((4 * hidden, width), bf16)] * 2,
        scratch_shapes=[pltpu.VMEM((18 * channels, width), bf16)] * 2,
        compiler_params=params,
        name="inner",
    )(own, near, across, bias, w_in, w_out)


def outer_kernel(near_ref, across_ref, far_across_ref, far_near_ref, field_ref, hid_hi, hid_lo, bias_ref, in_ref,
                 out_ref, before_ref, fields_ref, wide_hi, wide_lo, side_hi, side_lo):
    channels, width = near_ref.shape[1:]
    hidden = in_ref.shape[0] // 2
    wide = (wide_hi, wide_lo)
    side = (side_hi, side_lo)
    bias = jnp.concatenate([bias_ref[...]] * 2, axis=1)
    fields = [None, None] + [field_ref[row * channels : (row + 1) * channels, :] for row in range(2)] + [None, None]
    sides = (
        (-4, (either(far_across_ref, far_near_ref), either(across_ref, near_ref))),
        (2, (either(near_ref, across_ref), either(far_near_ref, far_across_ref))),
    )
    rows = []
    for after, (first, slabs) in enumerate(sides):
        for index in range(4):
            row = jnp.where(inside(first + index), slabs[index // 2](index % 2), 0.0)
            rows.append(row)
            put_windows(wide, 4 * after + index, row)
        for ref, known in zip(side, (hid_hi, hid_lo)):
            ref[(2 + 2 * after) * hidden : (4 + 2 * after) * hidden, :] = known[
                2 * after * hidden : 2 * (after + 1) * hidden, :
            ]
    before = [to_channels(in_ref[...], wide, 4 * after, channels) + bias for after in range(2)]
    activate(before[0], -3, side, 0, hidden, width)
    activate(before[1], 3, side, 6, hidden, width)
    for after in range(2):
        moved = from_channels(out_ref[...], side, 4 * after, hidden, channels)
        for row in range(2):
            at = 4 * after + row
            value = rows[2 + 2 * after + row] + moved[row]
            fields[at] = jnp.where(inside(at - 2), value, 0.0)
    for index in range(6):
        put_windows(wide, index, fields[index])
    for pair in (0, 2):
        before = to_channels(in_ref[...], wide, pair, channels) + bias
        before_ref[pair // 2] = before
        activate(before, pair - 1, side, pair, hidden, width)
    moved = from_channels(out_ref[...], side, 0, hidden, channels)
    for row in range(2):
        fields_ref[row * channels : (row + 1) * channels, :] = fields[2 + row]
        fields_ref[(2 + row) * channels : (3 + row) * channels, :] = fields[2 + row] + moved[row]


def outer(near, across, far_across, far_near, field, hid, bias, w_in, w_out):
    channels, width = near.shape[1:]
    hidden = w_in.shape[0] // 2
    return pl.pallas_call(
        outer_kernel,
        out_shape=[
            jax.ShapeDtypeStruct((2, hidden, 2 * width), f32),
            jax.ShapeDtypeStruct((4 * channels, width), f32),
        ],
        scratch_shapes=[pltpu.VMEM((24 * channels, width), bf16)] * 2
        + [pltpu.VMEM((8 * hidden, width), bf16)] * 2,
        compiler_params=params,
        name="outer",
    )(near, across, far_across, far_near, field, *hid, bias, w_in, w_out)


def crps_kernel(weight_ref, fields_ref, targets_ref, out_ref):
    members, height, width = fields_ref.shape
    mine = lax.axis_index(MEMBER)
    weight = jnp.where(lax.rem(lax.div(mine, 2), 2) == 0, weight_ref[:8, :], weight_ref[8:, :])
    softness = smooth_width * smooth_width
    loss = jnp.zeros((8, width), f32)
    for tile in range(0, height, 8):
        values = [fields_ref[m, tile : tile + 8, :] for m in range(members)]
        truth = targets_ref[mine, tile : tile + 8, :]
        direct = jnp.zeros((8, width), f32)
        pairs = jnp.full((8, width), members * smooth_width, f32)
        slopes = [jnp.zeros((8, width), f32) for m in range(members)]
        grads = []
        for m in range(members):
            error = values[m] - truth
            square = error * error + softness
            inverse = lax.rsqrt(square)
            direct = direct + square * inverse
            grads.append(error * inverse)
            for other in range(m + 1, members):
                gap = values[m] - values[other]
                square = gap * gap + softness
                inverse = lax.rsqrt(square)
                pairs = pairs + 2.0 * square * inverse
                slope = gap * inverse
                slopes[m] = slopes[m] + slope
                slopes[other] = slopes[other] - slope
        loss = loss + weight * (direct - pairs / (2.0 * (members - 1)))
        for m in range(members):
            out_ref[m, tile : tile + 8, :] = weight * (grads[m] - slopes[m] / (members - 1))
    for m in range(members):
        out_ref[m, height : height + 8, :] = loss


def crps(weights, fields, targets):
    members, height, width = fields.shape
    return pl.pallas_call(
        crps_kernel,
        out_shape=jax.ShapeDtypeStruct((members, height + 8, width), f32),
        compiler_params=params,
        name="crps",
    )(weights, fields, targets)


def collect_kernel(grads_ref, first_ref, second_ref, known_ref):
    chunks, height, width = grads_ref.shape
    height = height - 8
    half = chunks // 2
    total = grads_ref[0, height : height + 8, :]
    for chunk in range(1, chunks):
        total = total + grads_ref[chunk, height : height + 8, :]
    for chunk in range(half):
        first_ref[chunk * height : (chunk + 1) * height, :] = grads_ref[chunk, :height, :]
        second_ref[chunk * height : (chunk + 1) * height, :] = grads_ref[half + chunk, :height, :]
    known = jnp.broadcast_to(jnp.sum(total, axis=0, keepdims=True), (slab_count, width))
    slab = lax.broadcasted_iota(jnp.int32, known.shape, 0)
    known = jnp.where(slab == lax.axis_index(LAT), known, 0.0)
    second_ref[half * height :, :] = known
    known_ref[...] = known


def collect(grads):
    chunks, height, width = grads.shape
    count = chunks // 2 * (height - 8)
    return pl.pallas_call(
        collect_kernel,
        out_shape=[
            jax.ShapeDtypeStruct((count, width), f32),
            jax.ShapeDtypeStruct((count + slab_count, width), f32),
            jax.ShapeDtypeStruct((slab_count, width), f32),
        ],
        compiler_params=params,
        name="collect",
    )(grads)


def merged(*known):
    result = known[0]
    for other in known[1:]:
        result = jnp.where(result != 0.0, result, other)
    return result


def table_of(*refs):
    return merged(*(ref[ref.shape[0] - slab_count :, :] for ref in refs))


def hidden_grads(step, near_side, beside_ref, own_ref, slope_ref, weight_ref, wide):
    width = own_ref.shape[1]
    channels = (own_ref.shape[0] - slab_count) // 2
    even = is_even()
    below = even if near_side else jnp.logical_not(even)

    def take(ref, row):
        return ref[row * channels : (row + 1) * channels, :]

    first = jnp.where(below, 0, -2)
    for index in range(4):
        own, beside = take(own_ref, index % 2), take(beside_ref, index % 2)
        row = jnp.where(below, own, beside) if index < 2 else jnp.where(below, beside, own)
        put_windows(wide, index, jnp.where(inside(first + index), row, 0.0))
    grads = to_channels(weight_ref[...], wide, 0, channels) * slope_ref[step, jnp.where(below, 1, 0)]
    rows = []
    for half in range(2):
        row = grads[:, half * width : (half + 1) * width]
        rows.append(split(row))
    return rows


def backward_side_kernel(step, near_side, own_ref, beside_ref, slope_ref, outb_ref, high_ref, low_ref, wide_hi,
                         wide_lo):
    rows = hidden_grads(step, near_side, beside_ref, own_ref, slope_ref, outb_ref, (wide_hi, wide_lo))
    for half in range(2):
        high_ref[half], low_ref[half] = rows[half]


def backward_side(step, near_side, own, beside, slopes, w_out):
    count, width = own.shape
    channels = (count - slab_count) // 2
    hidden = w_out.shape[0] // 2
    return pl.pallas_call(
        functools.partial(backward_side_kernel, step, near_side),
        out_shape=[jax.ShapeDtypeStruct((2, hidden, width), bf16)] * 2,
        scratch_shapes=[pltpu.VMEM((12 * channels, width), bf16)] * 2,
        compiler_params=params,
        name="backward_near" if near_side else "backward_across",
    )(own, beside, slopes, w_out)


def gather_hidden(hid, close, far):
    hidden = close[0].shape[1]
    even = is_even()
    for half in range(2):
        far_at = pl.multiple_of(jnp.where(even, half, 2 + half) * hidden, hidden)
        close_at = pl.multiple_of(jnp.where(even, 2 + half, half) * hidden, hidden)
        for ref, far_ref, close_ref in zip(hid, far, close):
            ref[pl.ds(far_at, hidden), :] = far_ref[half]
            ref[pl.ds(close_at, hidden), :] = close_ref[half]


def join_kernel(own_ref, close_hi, close_lo, far_hi, far_lo, inb_ref, added_ref, *rest):
    *tables, out_ref, known_ref, hid_hi, hid_lo = rest
    channels = (own_ref.shape[0] - slab_count) // 2
    gather_hidden((hid_hi, hid_lo), (close_hi, close_lo), (far_hi, far_lo))
    moved = from_channels(inb_ref[...], (hid_hi, hid_lo), 0, close_hi.shape[1], channels)
    for row in range(2):
        part = slice(row * channels, (row + 1) * channels)
        out_ref[part, :] = own_ref[part, :] + moved[row] + added_ref[part, :]
    known = table_of(own_ref, *tables)
    out_ref[2 * channels :, :] = known
    known_ref[...] = known


def join(own, close, far, w_in, added, *tables):
    hidden, width = close[0].shape[1:]
    return pl.pallas_call(
        join_kernel,
        out_shape=[
            jax.ShapeDtypeStruct(own.shape, f32),
            jax.ShapeDtypeStruct((slab_count, width), f32),
        ],
        scratch_shapes=[pltpu.VMEM((4 * hidden, width), bf16)] * 2,
        compiler_params=params,
        name="join",
    )(own, *close, *far, w_in, added, *tables)


def finish_kernel(count, own_ref, close_hi, close_lo, far_hi, far_lo, inb_ref, *rest):
    *tables, out_hbm, loss_hbm, out_ref, loss_ref, hid_hi, hid_lo, done = rest
    channels = (own_ref.shape[0] - slab_count) // 2
    total = jnp.sum(table_of(own_ref, *tables), axis=0, keepdims=True)
    loss_ref[...] = jnp.sum(total, axis=1, keepdims=True) / count
    copies = [pltpu.make_async_copy(loss_ref, loss_hbm, done.at[0])]
    copies[0].start()
    gather_hidden((hid_hi, hid_lo), (close_hi, close_lo), (far_hi, far_lo))
    moved = from_channels(inb_ref[...], (hid_hi, hid_lo), 0, close_hi.shape[1], channels)
    for row in range(2):
        part = pl.ds(row * channels, channels)
        out_ref[part, :] = own_ref[part, :] + moved[row]
        copies.append(pltpu.make_async_copy(out_ref.at[part, :], out_hbm.at[part, :], done.at[1 + row]))
        copies[-1].start()
    for copy in copies:
        copy.wait()


def finish(count, own, close, far, w_in, *tables):
    hidden, width = close[0].shape[1:]
    lines = own.shape[0] - slab_count
    vmem = pl.BlockSpec(memory_space=pltpu.VMEM)
    return pl.pallas_call(
        functools.partial(finish_kernel, count),
        out_shape=[
            jax.ShapeDtypeStruct((lines, width), f32),
            jax.ShapeDtypeStruct((1, 1), f32),
        ],
        in_specs=[vmem] * (6 + len(tables)),
        out_specs=[pl.BlockSpec(memory_space=pltpu.HBM)] * 2,
        scratch_shapes=[pltpu.VMEM((lines, width), f32), pltpu.VMEM((1, 1), f32)]
        + [pltpu.VMEM((4 * hidden, width), bf16)] * 2
        + [pltpu.SemaphoreType.DMA((3,))],
        compiler_params=params,
        name="finish",
    )(own, *close, *far, w_in, *tables)


def on_device(initial_states, targets, lat_weight, weight_in, weight_out, hidden_bias):
    members = lax.axis_size(MEMBER)
    slabs = lax.axis_size(LAT)
    steps, slab_rows, channels, width = targets.shape
    rows = slabs * slab_rows
    near = [(i, i ^ 1) for i in range(slabs)]
    across = [(i, (i + 1 if i % 2 else i - 1) % slabs) for i in range(slabs)]

    own = initial_states[0]
    beside = lax.ppermute(own, LAT, near)
    crossed = lax.ppermute(own, LAT, across)
    ready = prepare(weight_in.T, weight_out, hidden_bias[None, :], lat_weight[None, :], width)
    crossed, beside, ready = lax.optimization_barrier((crossed, beside, ready))
    far_crossed = lax.ppermute(beside, LAT, across)
    far_beside = lax.ppermute(crossed, LAT, near)
    w_in, w_out, bias, lat_weights = ready
    before_first, field, *hid = inner(own, beside, crossed, bias, w_in, w_out)
    before_second, fields = outer(
        beside, crossed, far_crossed, far_beside, field, hid, bias, w_in, w_out
    )
    height = steps * slab_rows * channels // members
    chunks = lax.all_to_all(
        fields.reshape(members, height, width), MEMBER, split_axis=0, concat_axis=0, tiled=True
    )
    grads = crps(lat_weights, chunks, targets.reshape(members, height, width))
    grads = lax.all_to_all(grads, MEMBER, split_axis=0, concat_axis=0, tiled=True)
    back = prepare_back(weight_in.T, weight_out, before_first, before_second)
    w_out_back, w_in_back, slopes = back
    first_grads, message, known = collect(grads)

    beside = lax.ppermute(message, LAT, near)
    crossed = lax.ppermute(message, LAT, across)
    opposite = [(i, i ^ 8) for i in range(slabs)]
    ahead = [(i, (i + 5 if i % 2 == 0 else i - 5) % slabs) for i in range(slabs)]
    behind = [(i, (i - 5 if i % 2 == 0 else i + 5) % slabs) for i in range(slabs)]
    distant_tables = [lax.ppermute(known, LAT, pairs) for pairs in (ahead, behind)]
    close = backward_side(1, True, message, beside, slopes, w_out_back)
    crossed, close = lax.optimization_barrier((crossed, close))
    distant = backward_side(1, False, message, crossed, slopes, w_out_back)
    message, known = join(
        message, close, distant, w_in_back, first_grads, beside, crossed, *distant_tables
    )
    beside = lax.ppermute(message, LAT, near)
    crossed = lax.ppermute(message, LAT, across)
    distant_tables = [lax.ppermute(known, LAT, pairs) for pairs in (opposite,)]
    close = backward_side(0, True, message, beside, slopes, w_out_back)
    crossed, close = lax.optimization_barrier((crossed, close))
    distant = backward_side(0, False, message, crossed, slopes, w_out_back)
    count = members * steps * rows * channels * width
    gradient, loss = finish(
        count, message, close, distant, w_in_back, beside, crossed, *distant_tables
    )
    loss = loss.reshape(())
    return gradient.reshape(initial_states.shape), loss


def solution(mesh):
    torus = Mesh(
        mesh.devices.reshape(4, 2, 2, 4, 2), ("member_0", "member_1", "lat_0", "lat_1", "lat_2")
    )
    placed = (P(MEMBER, LAT, None, None), P(None, LAT, None, None), P(LAT), P(), P(), P())
    return jax.shard_map(
        on_device,
        mesh=torus,
        in_specs=placed,
        out_specs=(P(MEMBER, LAT, None, None), P()),
        check_vma=False,
    )
```

```python
import functools

import jax
import jax.numpy as jnp
from jax import lax
from jax.experimental import pallas as pl
from jax.experimental.pallas import tpu as pltpu
from jax.sharding import Mesh
from jax.sharding import PartitionSpec as P

MEMBER = ("member_0", "member_1")
LAT = ("lat_0", "lat_1", "lat_2")

smooth_width = 0.1
gelu_scale = 0.7978845608028654
gelu_cubic = 0.044715
slab_count = 16

f32 = jnp.float32
bf16 = jnp.bfloat16
params = pltpu.CompilerParams(vmem_limit_bytes=16 * 1024 * 1024)


def split(value):
    high = value.astype(bf16)
    return high, (value - high.astype(f32)).astype(bf16)


def product(left, right):
    dot = functools.partial(jnp.dot, preferred_element_type=f32)
    count = left.shape[0] // 2
    both = dot(left, right[0])
    return both[:count] + (both[count:] + dot(left[:count], right[1]))


def from_left(row):
    lane = lax.broadcasted_iota(jnp.int32, row.shape, 1)
    return jnp.where(lane == 0, 0.0, pltpu.roll(row, 1, 1))


def from_right(row):
    lane = lax.broadcasted_iota(jnp.int32, row.shape, 1)
    return jnp.where(lane == row.shape[1] - 1, 0.0, pltpu.roll(row, row.shape[1] - 1, 1))


def put(refs, start, values):
    for ref, value in zip(refs, values):
        ref[start : start + value.shape[0], :] = value


def put_windows(refs, index, row):
    channels = row.shape[0]
    for part, shifted in enumerate((from_left(row), row, from_right(row))):
        put(refs, (3 * index + part) * channels, split(shifted))


def read(refs, start, size, height):
    parts = [(ref[start : start + size, :], ref[start + height : start + height + size, :]) for ref in refs]
    return tuple(jnp.concatenate(part, axis=1) for part in parts)


def to_channels(weights, windows, pair, channels):
    return product(weights, read(windows, pair * 3 * channels, 9 * channels, 3 * channels))


def from_channels(weights, hidden, pair, channels, outer):
    mixed = product(weights, read(hidden, pair * channels, 3 * channels, channels))
    width = mixed.shape[1] // 2
    rows = []
    for half in range(2):
        part = mixed[:, half * width : (half + 1) * width]
        rows.append(
            from_left(part[:outer])
            + part[outer : 2 * outer]
            + from_right(part[2 * outer :])
        )
    return rows


def gelu(x, half):
    t = jnp.tanh(x * (gelu_scale + (gelu_scale * gelu_cubic) * (x * x)))
    h = half * x
    return h + h * t


def gelu_slope(x):
    t = jnp.tanh(gelu_scale * (x + gelu_cubic * x * x * x))
    inner = gelu_scale * (1.0 + 3.0 * gelu_cubic * x * x)
    return 0.5 * (1.0 + t) + 0.5 * x * (1.0 - t * t) * inner


def fetch(pairs, arrived):
    copies = [pltpu.make_async_copy(*pair, arrived.at[i]) for i, pair in enumerate(pairs)]
    for copy in copies:
        copy.start()
    for copy in copies:
        copy.wait()


def prepare_kernel(win_hbm, wout_hbm, bias_hbm, lat_hbm, in_ref, out_ref, wide_bias_ref, wide_lat_ref,
                   win_ref, wout_ref, bias_ref, lat_ref, arrived):
    fetch(((win_hbm, win_ref), (wout_hbm, wout_ref), (bias_hbm, bias_ref), (lat_hbm, lat_ref)), arrived)
    outer, width = wout_ref.shape
    hidden = width // 9
    in_ref[:hidden, :], in_ref[hidden:, :] = split(win_ref[...].T)
    for a in range(3):
        for b in range(3):
            tap = 3 * a + b
            high, low = split(wout_ref[:, tap * hidden : (tap + 1) * hidden])
            out_ref[b * outer : (b + 1) * outer, a * hidden : (a + 1) * hidden] = high
            out_ref[(3 + b) * outer : (4 + b) * outer, a * hidden : (a + 1) * hidden] = low
    wide_bias_ref[...] = jnp.broadcast_to(bias_ref[...], wide_bias_ref.shape[::-1]).T
    for row in range(2):
        one = jnp.broadcast_to(lat_ref[:, row : row + 1], (8, wide_lat_ref.shape[1]))
        wide_lat_ref[8 * row : 8 * (row + 1), :] = one


def prepare(weight_in, weight_out, bias, lat_weight, width):
    taps_in, hidden = weight_in.shape
    outer = weight_out.shape[0]
    arrays = (weight_in, weight_out, bias, lat_weight)
    shapes = [(2 * hidden, taps_in), (6 * outer, 3 * hidden)]
    return pl.pallas_call(
        prepare_kernel,
        out_shape=[jax.ShapeDtypeStruct(shape, bf16) for shape in shapes]
        + [jax.ShapeDtypeStruct((hidden, width), f32), jax.ShapeDtypeStruct((16, width), f32)]
        + [jax.ShapeDtypeStruct(array.shape, f32) for array in arrays[:2]],
        in_specs=[pl.BlockSpec(memory_space=pltpu.HBM)] * 4,
        scratch_shapes=[pltpu.VMEM(array.shape, f32) for array in arrays[2:]] + [pltpu.SemaphoreType.DMA((4,))],
        compiler_params=params,
        name="prepare",
    )(*(pltpu.with_memory_space_constraint(array, pltpu.HBM) for array in arrays))


def prepare_back_kernel(win_ref, wout_ref, *rest):
    before_refs, (outb_ref, inb_ref, slope_ref, stack) = rest[:4], rest[4:]
    for side in range(2):
        below = is_even() if side == 0 else jnp.logical_not(is_even())
        first = jnp.where(below, 0, -2)
        for step, before_ref in enumerate(before_refs[side::2]):
            slope = gelu_slope(before_ref[...])
            width = slope.shape[1] // 2
            for half in range(2):
                part = slope[:, half * width : (half + 1) * width]
                part = jnp.where(inside(first + 1 + half), part, 0.0)
                slope_ref[step, side, :, half * width : (half + 1) * width] = part
    outer, width = wout_ref.shape
    hidden = width // 9
    inner = win_ref.shape[0] // 9
    for a in range(3):
        for b in range(3):
            tap = 3 * a + b
            stack[(8 - tap) * outer : (9 - tap) * outer, :] = wout_ref[:, tap * hidden : (tap + 1) * hidden]
            high, low = split(win_ref[tap * inner : (tap + 1) * inner, :])
            j, k = 2 - a, 2 - b
            inb_ref[k * inner : (k + 1) * inner, j * hidden : (j + 1) * hidden] = high
            inb_ref[(3 + k) * inner : (4 + k) * inner, j * hidden : (j + 1) * hidden] = low
    outb_ref[:hidden, :], outb_ref[hidden:, :] = split(stack[...].T)


def prepare_back(weight_in, weight_out, *before):
    taps_in, hidden = weight_in.shape
    outer = weight_out.shape[0]
    inner = taps_in // 9
    shapes = [(2 * hidden, 9 * outer), (6 * inner, 3 * hidden)]
    return pl.pallas_call(
        prepare_back_kernel,
        out_shape=[jax.ShapeDtypeStruct(shape, bf16) for shape in shapes]
        + [jax.ShapeDtypeStruct((2, 2, *before[0].shape), f32)],
        scratch_shapes=[pltpu.VMEM((9 * outer, hidden), f32)],
        compiler_params=params,
        name="prepare_back",
    )(weight_in, weight_out, *before)


def inside(row):
    index = lax.axis_index(LAT) * 2 + row
    return (index >= 0) & (index < 2 * slab_count)


def is_even():
    return lax.rem(lax.axis_index(LAT), 2) == 0


def side_windows(near_side, own, beside, wide):
    even = is_even()
    below = even if near_side else jnp.logical_not(even)
    first = jnp.where(below, 0, -2)
    for index in range(4):
        mine, other = own(index % 2), beside(index % 2)
        row = jnp.where(below, mine, other) if index < 2 else jnp.where(below, other, mine)
        put_windows(wide, index, jnp.where(inside(first + index), row, 0.0))
    return first


def forward_side_kernel(near_side, own_ref, beside_ref, bias_ref, in_ref, before_ref, high_ref, low_ref, wide_hi,
                        wide_lo):
    channels, width = own_ref.shape[1:]
    wide = (wide_hi, wide_lo)
    first = side_windows(near_side, lambda row: own_ref[row], lambda row: beside_ref[row], wide)
    before = to_channels(in_ref[...], wide, 0, channels) + jnp.concatenate([bias_ref[...]] * 2, axis=1)
    before_ref[...] = before
    for half in range(2):
        scale = jnp.where(inside(first + 1 + half), 0.5, 0.0)
        active = gelu(before[:, half * width : (half + 1) * width], scale)
        high_ref[half], low_ref[half] = split(active)


def forward_side(near_side, own, beside, bias, w_in):
    channels, width = own.shape[1:]
    hidden = w_in.shape[0] // 2
    return pl.pallas_call(
        functools.partial(forward_side_kernel, near_side),
        out_shape=[jax.ShapeDtypeStruct((hidden, 2 * width), f32)]
        + [jax.ShapeDtypeStruct((2, hidden, width), bf16)] * 2,
        scratch_shapes=[pltpu.VMEM((12 * channels, width), bf16)] * 2,
        compiler_params=params,
        name="forward_near" if near_side else "forward_across",
    )(own, beside, bias, w_in)


def move_kernel(keep, field_ref, close_hi, close_lo, far_hi, far_lo, out_ref, moved_ref, hid_hi, hid_lo):
    rows, channels, width = field_ref.shape
    gather_hidden((hid_hi, hid_lo), (close_hi, close_lo), (far_hi, far_lo))
    moved = from_channels(out_ref[...], (hid_hi, hid_lo), 0, close_hi.shape[1], channels)
    for row in range(rows):
        if keep:
            moved_ref[row] = field_ref[row]
        moved_ref[rows * keep + row] = field_ref[row] + moved[row]


def move(keep, field, close, far, w_out):
    rows, channels, width = field.shape
    hidden = close[0].shape[1]
    return pl.pallas_call(
        functools.partial(move_kernel, keep),
        out_shape=jax.ShapeDtypeStruct(((1 + keep) * rows, channels, width), f32),
        scratch_shapes=[pltpu.VMEM((4 * hidden, width), bf16)] * 2,
        compiler_params=params,
        name="move",
    )(field, *close, *far, w_out)


def crps_kernel(weight_ref, fields_ref, targets_ref, out_ref):
    members, height, width = fields_ref.shape
    mine = lax.axis_index(MEMBER)
    weight = jnp.where(lax.rem(lax.div(mine, 2), 2) == 0, weight_ref[:8, :], weight_ref[8:, :])
    softness = smooth_width * smooth_width
    loss = jnp.zeros((8, width), f32)
    for tile in range(0, height, 8):
        values = [fields_ref[m, tile : tile + 8, :] for m in range(members)]
        truth = targets_ref[mine, tile : tile + 8, :]
        direct = jnp.zeros((8, width), f32)
        pairs = jnp.full((8, width), members * smooth_width, f32)
        slopes = [jnp.zeros((8, width), f32) for m in range(members)]
        grads = []
        for m in range(members):
            error = values[m] - truth
            square = error * error + softness
            inverse = lax.rsqrt(square)
            direct = direct + square * inverse
            grads.append(error * inverse)
            for other in range(m + 1, members):
                gap = values[m] - values[other]
                square = gap * gap + softness
                inverse = lax.rsqrt(square)
                pairs = pairs + 2.0 * square * inverse
                slope = gap * inverse
                slopes[m] = slopes[m] + slope
                slopes[other] = slopes[other] - slope
        loss = loss + weight * (direct - pairs / (2.0 * (members - 1)))
        for m in range(members):
            out_ref[m, tile : tile + 8, :] = weight * (grads[m] - slopes[m] / (members - 1))
    for m in range(members):
        out_ref[m, height : height + 8, :] = loss


def crps(weights, fields, targets):
    members, height, width = fields.shape
    return pl.pallas_call(
        crps_kernel,
        out_shape=jax.ShapeDtypeStruct((members, height + 8, width), f32),
        compiler_params=params,
        name="crps",
    )(weights, fields, targets)


def collect_kernel(grads_ref, first_ref, second_ref, known_ref):
    chunks, height, width = grads_ref.shape
    height = height - 8
    half = chunks // 2
    total = grads_ref[0, height : height + 8, :]
    for chunk in range(1, chunks):
        total = total + grads_ref[chunk, height : height + 8, :]
    for chunk in range(half):
        first_ref[chunk * height : (chunk + 1) * height, :] = grads_ref[chunk, :height, :]
        second_ref[chunk * height : (chunk + 1) * height, :] = grads_ref[half + chunk, :height, :]
    known = jnp.broadcast_to(jnp.sum(total, axis=0, keepdims=True), (slab_count, width))
    slab = lax.broadcasted_iota(jnp.int32, known.shape, 0)
    known = jnp.where(slab == lax.axis_index(LAT), known, 0.0)
    second_ref[half * height :, :] = known
    known_ref[...] = known


def collect(grads):
    chunks, height, width = grads.shape
    count = chunks // 2 * (height - 8)
    return pl.pallas_call(
        collect_kernel,
        out_shape=[
            jax.ShapeDtypeStruct((count, width), f32),
            jax.ShapeDtypeStruct((count + slab_count, width), f32),
            jax.ShapeDtypeStruct((slab_count, width), f32),
        ],
        compiler_params=params,
        name="collect",
    )(grads)


def merged(*known):
    result = known[0]
    for other in known[1:]:
        result = jnp.where(result != 0.0, result, other)
    return result


def table_of(*refs):
    return merged(*(ref[ref.shape[0] - slab_count :, :] for ref in refs))


def hidden_grads(step, near_side, beside_ref, own_ref, slope_ref, weight_ref, wide):
    width = own_ref.shape[1]
    channels = (own_ref.shape[0] - slab_count) // 2

    def rows_of(ref):
        return lambda row: ref[row * channels : (row + 1) * channels, :]

    side_windows(near_side, rows_of(own_ref), rows_of(beside_ref), wide)
    grads = to_channels(weight_ref[...], wide, 0, channels) * slope_ref[step, 0 if near_side else 1]
    return [split(grads[:, half * width : (half + 1) * width]) for half in range(2)]


def backward_side_kernel(step, near_side, own_ref, beside_ref, slope_ref, outb_ref, high_ref, low_ref, wide_hi,
                         wide_lo):
    rows = hidden_grads(step, near_side, beside_ref, own_ref, slope_ref, outb_ref, (wide_hi, wide_lo))
    for half in range(2):
        high_ref[half], low_ref[half] = rows[half]


def backward_side(step, near_side, own, beside, slopes, w_out):
    count, width = own.shape
    channels = (count - slab_count) // 2
    hidden = w_out.shape[0] // 2
    return pl.pallas_call(
        functools.partial(backward_side_kernel, step, near_side),
        out_shape=[jax.ShapeDtypeStruct((2, hidden, width), bf16)] * 2,
        scratch_shapes=[pltpu.VMEM((12 * channels, width), bf16)] * 2,
        compiler_params=params,
        name="backward_near" if near_side else "backward_across",
    )(own, beside, slopes, w_out)


def gather_hidden(hid, close, far):
    hidden = close[0].shape[1]
    even = is_even()
    for half in range(2):
        far_at = pl.multiple_of(jnp.where(even, half, 2 + half) * hidden, hidden)
        close_at = pl.multiple_of(jnp.where(even, 2 + half, half) * hidden, hidden)
        for ref, far_ref, close_ref in zip(hid, far, close):
            ref[pl.ds(far_at, hidden), :] = far_ref[half]
            ref[pl.ds(close_at, hidden), :] = close_ref[half]


def join_kernel(own_ref, close_hi, close_lo, far_hi, far_lo, inb_ref, added_ref, *rest):
    *tables, out_ref, known_ref, hid_hi, hid_lo = rest
    channels = (own_ref.shape[0] - slab_count) // 2
    gather_hidden((hid_hi, hid_lo), (close_hi, close_lo), (far_hi, far_lo))
    moved = from_channels(inb_ref[...], (hid_hi, hid_lo), 0, close_hi.shape[1], channels)
    for row in range(2):
        part = slice(row * channels, (row + 1) * channels)
        out_ref[part, :] = own_ref[part, :] + moved[row] + added_ref[part, :]
    known = table_of(own_ref, *tables)
    out_ref[2 * channels :, :] = known
    known_ref[...] = known


def join(own, close, far, w_in, added, *tables):
    hidden, width = close[0].shape[1:]
    return pl.pallas_call(
        join_kernel,
        out_shape=[
            jax.ShapeDtypeStruct(own.shape, f32),
            jax.ShapeDtypeStruct((slab_count, width), f32),
        ],
        scratch_shapes=[pltpu.VMEM((4 * hidden, width), bf16)] * 2,
        compiler_params=params,
        name="join",
    )(own, *close, *far, w_in, added, *tables)


def finish_kernel(count, own_ref, close_hi, close_lo, far_hi, far_lo, inb_ref, *rest):
    *tables, out_hbm, loss_hbm, out_ref, loss_ref, hid_hi, hid_lo, done = rest
    channels = (own_ref.shape[0] - slab_count) // 2
    total = jnp.sum(table_of(own_ref, *tables), axis=0, keepdims=True)
    loss_ref[...] = jnp.sum(total, axis=1, keepdims=True) / count
    copies = [pltpu.make_async_copy(loss_ref, loss_hbm, done.at[0])]
    copies[0].start()
    gather_hidden((hid_hi, hid_lo), (close_hi, close_lo), (far_hi, far_lo))
    moved = from_channels(inb_ref[...], (hid_hi, hid_lo), 0, close_hi.shape[1], channels)
    for row in range(2):
        part = pl.ds(row * channels, channels)
        out_ref[part, :] = own_ref[part, :] + moved[row]
        copies.append(pltpu.make_async_copy(out_ref.at[part, :], out_hbm.at[part, :], done.at[1 + row]))
        copies[-1].start()
    for copy in copies:
        copy.wait()


def finish(count, own, close, far, w_in, *tables):
    hidden, width = close[0].shape[1:]
    lines = own.shape[0] - slab_count
    vmem = pl.BlockSpec(memory_space=pltpu.VMEM)
    return pl.pallas_call(
        functools.partial(finish_kernel, count),
        out_shape=[
            jax.ShapeDtypeStruct((lines, width), f32),
            jax.ShapeDtypeStruct((1, 1), f32),
        ],
        in_specs=[vmem] * (6 + len(tables)),
        out_specs=[pl.BlockSpec(memory_space=pltpu.HBM)] * 2,
        scratch_shapes=[pltpu.VMEM((lines, width), f32), pltpu.VMEM((1, 1), f32)]
        + [pltpu.VMEM((4 * hidden, width), bf16)] * 2
        + [pltpu.SemaphoreType.DMA((3,))],
        compiler_params=params,
        name="finish",
    )(own, *close, *far, w_in, *tables)


def on_device(initial_states, targets, lat_weight, weight_in, weight_out, hidden_bias):
    members = lax.axis_size(MEMBER)
    slabs = lax.axis_size(LAT)
    steps, slab_rows, channels, width = targets.shape
    rows = slabs * slab_rows
    near = [(i, i ^ 1) for i in range(slabs)]
    across = [(i, (i + 1 if i % 2 else i - 1) % slabs) for i in range(slabs)]

    own = initial_states[0]
    beside = lax.ppermute(own, LAT, near)
    crossed = lax.ppermute(own, LAT, across)
    ready = prepare(weight_in.T, weight_out, hidden_bias[None, :], lat_weight[None, :], width)
    w_in, w_out, bias, lat_weights, *raw = ready
    before_near, *close = forward_side(True, own, beside, bias, w_in)
    crossed, close = lax.optimization_barrier((crossed, close))
    before_across, *distant = forward_side(False, own, crossed, bias, w_in)
    before_first = (before_near, before_across)
    field = move(0, own, close, distant, w_out)
    beside = lax.ppermute(field, LAT, near)
    crossed = lax.ppermute(field, LAT, across)
    before_near, *close = forward_side(True, field, beside, bias, w_in)
    crossed, close = lax.optimization_barrier((crossed, close))
    before_across, *distant = forward_side(False, field, crossed, bias, w_in)
    before_second = (before_near, before_across)
    fields = move(1, field, close, distant, w_out)
    height = steps * slab_rows * channels // members
    chunks = lax.all_to_all(
        fields.reshape(members, height, width), MEMBER, split_axis=0, concat_axis=0, tiled=True
    )
    grads = crps(lat_weights, chunks, targets.reshape(members, height, width))
    grads = lax.all_to_all(grads, MEMBER, split_axis=0, concat_axis=0, tiled=True)
    back = prepare_back(*raw, *before_first, *before_second)
    w_out_back, w_in_back, slopes = back
    first_grads, message, known = collect(grads)

    beside = lax.ppermute(message, LAT, near)
    crossed = lax.ppermute(message, LAT, across)
    opposite = [(i, i ^ 8) for i in range(slabs)]
    ahead = [(i, (i + 5 if i % 2 == 0 else i - 5) % slabs) for i in range(slabs)]
    behind = [(i, (i - 5 if i % 2 == 0 else i + 5) % slabs) for i in range(slabs)]
    distant_tables = [lax.ppermute(known, LAT, pairs) for pairs in (ahead, behind)]
    close = backward_side(1, True, message, beside, slopes, w_out_back)
    crossed, close = lax.optimization_barrier((crossed, close))
    distant = backward_side(1, False, message, crossed, slopes, w_out_back)
    message, known = join(
        message, close, distant, w_in_back, first_grads, beside, crossed, *distant_tables
    )
    beside = lax.ppermute(message, LAT, near)
    crossed = lax.ppermute(message, LAT, across)
    distant_tables = [lax.ppermute(known, LAT, pairs) for pairs in (opposite,)]
    close = backward_side(0, True, message, beside, slopes, w_out_back)
    crossed, close = lax.optimization_barrier((crossed, close))
    distant = backward_side(0, False, message, crossed, slopes, w_out_back)
    count = members * steps * rows * channels * width
    gradient, loss = finish(
        count, message, close, distant, w_in_back, beside, crossed, *distant_tables
    )
    loss = loss.reshape(())
    return gradient.reshape(initial_states.shape), loss


def solution(mesh):
    torus = Mesh(
        mesh.devices.reshape(4, 2, 2, 4, 2), ("member_0", "member_1", "lat_0", "lat_1", "lat_2")
    )
    placed = (P(MEMBER, LAT, None, None), P(None, LAT, None, None), P(LAT), P(), P(), P())
    return jax.shard_map(
        on_device,
        mesh=torus,
        in_specs=placed,
        out_specs=(P(MEMBER, LAT, None, None), P()),
        check_vma=False,
    )
```

```python
import functools

import jax
import jax.numpy as jnp
from jax import lax
from jax.experimental import pallas as pl
from jax.experimental.pallas import tpu as pltpu
from jax.sharding import Mesh
from jax.sharding import PartitionSpec as P

MEMBER = ("member_0", "member_1")
LAT = ("lat_0", "lat_1", "lat_2")

smooth_width = 0.1
gelu_scale = 0.7978845608028654
gelu_cubic = 0.044715
slab_count = 16

f32 = jnp.float32
bf16 = jnp.bfloat16
params = pltpu.CompilerParams(vmem_limit_bytes=16 * 1024 * 1024)


def split(value):
    high = value.astype(bf16)
    return high, (value - high.astype(f32)).astype(bf16)


def product(left, right):
    dot = functools.partial(jnp.dot, preferred_element_type=f32)
    count = left.shape[0] // 2
    both = dot(left, right[0])
    return both[:count] + (both[count:] + dot(left[:count], right[1]))


def from_left(row):
    lane = lax.broadcasted_iota(jnp.int32, row.shape, 1)
    return jnp.where(lane == 0, 0.0, pltpu.roll(row, 1, 1))


def from_right(row):
    lane = lax.broadcasted_iota(jnp.int32, row.shape, 1)
    return jnp.where(lane == row.shape[1] - 1, 0.0, pltpu.roll(row, row.shape[1] - 1, 1))


def put(refs, start, values):
    for ref, value in zip(refs, values):
        ref[start : start + value.shape[0], :] = value


def put_windows(refs, index, row):
    channels = row.shape[0]
    for part, shifted in enumerate((from_left(row), row, from_right(row))):
        put(refs, (3 * index + part) * channels, split(shifted))


def read(refs, start, size, height):
    parts = [(ref[start : start + size, :], ref[start + height : start + height + size, :]) for ref in refs]
    return tuple(jnp.concatenate(part, axis=1) for part in parts)


def to_channels(weights, windows, pair, channels):
    return product(weights, read(windows, pair * 3 * channels, 9 * channels, 3 * channels))


def from_channels(weights, hidden, pair, channels, outer):
    mixed = product(weights, read(hidden, pair * channels, 3 * channels, channels))
    width = mixed.shape[1] // 2
    rows = []
    for half in range(2):
        part = mixed[:, half * width : (half + 1) * width]
        rows.append(
            from_left(part[:outer])
            + part[outer : 2 * outer]
            + from_right(part[2 * outer :])
        )
    return rows


def gelu(x, half):
    t = jnp.tanh(x * (gelu_scale + (gelu_scale * gelu_cubic) * (x * x)))
    h = half * x
    return h + h * t


def gelu_slope(x):
    t = jnp.tanh(gelu_scale * (x + gelu_cubic * x * x * x))
    inner = gelu_scale * (1.0 + 3.0 * gelu_cubic * x * x)
    return 0.5 * (1.0 + t) + 0.5 * x * (1.0 - t * t) * inner


def fetch(pairs, arrived):
    copies = [pltpu.make_async_copy(*pair, arrived.at[i]) for i, pair in enumerate(pairs)]
    for copy in copies:
        copy.start()
    for copy in copies:
        copy.wait()


def prepare_kernel(win_hbm, wout_hbm, bias_hbm, lat_hbm, in_ref, out_ref, wide_bias_ref, wide_lat_ref,
                   win_ref, wout_ref, bias_ref, lat_ref, arrived):
    fetch(((win_hbm, win_ref), (wout_hbm, wout_ref), (bias_hbm, bias_ref), (lat_hbm, lat_ref)), arrived)
    outer, width = wout_ref.shape
    hidden = width // 9
    in_ref[:hidden, :], in_ref[hidden:, :] = split(win_ref[...].T)
    for a in range(3):
        for b in range(3):
            tap = 3 * a + b
            high, low = split(wout_ref[:, tap * hidden : (tap + 1) * hidden])
            out_ref[b * outer : (b + 1) * outer, a * hidden : (a + 1) * hidden] = high
            out_ref[(3 + b) * outer : (4 + b) * outer, a * hidden : (a + 1) * hidden] = low
    wide_bias_ref[...] = jnp.broadcast_to(bias_ref[...], wide_bias_ref.shape[::-1]).T
    for row in range(2):
        one = jnp.broadcast_to(lat_ref[:, row : row + 1], (8, wide_lat_ref.shape[1]))
        wide_lat_ref[8 * row : 8 * (row + 1), :] = one


def prepare(weight_in, weight_out, bias, lat_weight, width):
    taps_in, hidden = weight_in.shape
    outer = weight_out.shape[0]
    arrays = (weight_in, weight_out, bias, lat_weight)
    shapes = [(2 * hidden, taps_in), (6 * outer, 3 * hidden)]
    return pl.pallas_call(
        prepare_kernel,
        out_shape=[jax.ShapeDtypeStruct(shape, bf16) for shape in shapes]
        + [jax.ShapeDtypeStruct((hidden, width), f32), jax.ShapeDtypeStruct((16, width), f32)]
        + [jax.ShapeDtypeStruct(array.shape, f32) for array in arrays[:2]],
        in_specs=[pl.BlockSpec(memory_space=pltpu.HBM)] * 4,
        scratch_shapes=[pltpu.VMEM(array.shape, f32) for array in arrays[2:]] + [pltpu.SemaphoreType.DMA((4,))],
        compiler_params=params,
        name="prepare",
    )(*(pltpu.with_memory_space_constraint(array, pltpu.HBM) for array in arrays))


def prepare_back_kernel(win_ref, wout_ref, outb_ref, inb_ref, stack):
    outer, width = wout_ref.shape
    hidden = width // 9
    inner = win_ref.shape[0] // 9
    for a in range(3):
        for b in range(3):
            tap = 3 * a + b
            stack[(8 - tap) * outer : (9 - tap) * outer, :] = wout_ref[:, tap * hidden : (tap + 1) * hidden]
            high, low = split(win_ref[tap * inner : (tap + 1) * inner, :])
            j, k = 2 - a, 2 - b
            inb_ref[k * inner : (k + 1) * inner, j * hidden : (j + 1) * hidden] = high
            inb_ref[(3 + k) * inner : (4 + k) * inner, j * hidden : (j + 1) * hidden] = low
    outb_ref[:hidden, :], outb_ref[hidden:, :] = split(stack[...].T)


def prepare_back(weight_in, weight_out):
    taps_in, hidden = weight_in.shape
    outer = weight_out.shape[0]
    shapes = [(2 * hidden, 9 * outer), (6 * (taps_in // 9), 3 * hidden)]
    return pl.pallas_call(
        prepare_back_kernel,
        out_shape=[jax.ShapeDtypeStruct(shape, bf16) for shape in shapes],
        scratch_shapes=[pltpu.VMEM((9 * outer, hidden), f32)],
        compiler_params=params,
        name="prepare_back",
    )(weight_in, weight_out)


def slopes_kernel(*refs):
    *before_refs, slope_ref = refs
    for side, before_ref in enumerate(before_refs):
        below = is_even() if side == 0 else jnp.logical_not(is_even())
        first = jnp.where(below, 0, -2)
        slope = gelu_slope(before_ref[...])
        width = slope.shape[1] // 2
        for half in range(2):
            part = slope[:, half * width : (half + 1) * width]
            part = jnp.where(inside(first + 1 + half), part, 0.0)
            slope_ref[side, :, half * width : (half + 1) * width] = part


def slopes_of(*before):
    return pl.pallas_call(
        slopes_kernel,
        out_shape=jax.ShapeDtypeStruct((2, *before[0].shape), f32),
        compiler_params=params,
        name="slopes",
    )(*before)


def inside(row):
    index = lax.axis_index(LAT) * 2 + row
    return (index >= 0) & (index < 2 * slab_count)


def is_even():
    return lax.rem(lax.axis_index(LAT), 2) == 0


def side_windows(near_side, own, beside, wide):
    even = is_even()
    below = even if near_side else jnp.logical_not(even)
    first = jnp.where(below, 0, -2)
    for index in range(4):
        mine, other = own(index % 2), beside(index % 2)
        row = jnp.where(below, mine, other) if index < 2 else jnp.where(below, other, mine)
        put_windows(wide, index, jnp.where(inside(first + index), row, 0.0))
    return first


def forward_side_kernel(near_side, own_ref, beside_ref, bias_ref, in_ref, before_ref, high_ref, low_ref, wide_hi,
                        wide_lo):
    channels, width = own_ref.shape[1:]
    wide = (wide_hi, wide_lo)
    first = side_windows(near_side, lambda row: own_ref[row], lambda row: beside_ref[row], wide)
    before = to_channels(in_ref[...], wide, 0, channels) + jnp.concatenate([bias_ref[...]] * 2, axis=1)
    before_ref[...] = before
    for half in range(2):
        scale = jnp.where(inside(first + 1 + half), 0.5, 0.0)
        active = gelu(before[:, half * width : (half + 1) * width], scale)
        high_ref[half], low_ref[half] = split(active)


def forward_side(near_side, own, beside, bias, w_in):
    channels, width = own.shape[1:]
    hidden = w_in.shape[0] // 2
    return pl.pallas_call(
        functools.partial(forward_side_kernel, near_side),
        out_shape=[jax.ShapeDtypeStruct((hidden, 2 * width), f32)]
        + [jax.ShapeDtypeStruct((2, hidden, width), bf16)] * 2,
        scratch_shapes=[pltpu.VMEM((12 * channels, width), bf16)] * 2,
        compiler_params=params,
        name="forward_near" if near_side else "forward_across",
    )(own, beside, bias, w_in)


def move_kernel(keep, field_ref, close_hi, close_lo, far_hi, far_lo, out_ref, moved_ref, hid_hi, hid_lo):
    rows, channels, width = field_ref.shape
    gather_hidden((hid_hi, hid_lo), (close_hi, close_lo), (far_hi, far_lo))
    moved = from_channels(out_ref[...], (hid_hi, hid_lo), 0, close_hi.shape[1], channels)
    for row in range(rows):
        if keep:
            moved_ref[row] = field_ref[row]
        moved_ref[rows * keep + row] = field_ref[row] + moved[row]


def move(keep, field, close, far, w_out):
    rows, channels, width = field.shape
    hidden = close[0].shape[1]
    return pl.pallas_call(
        functools.partial(move_kernel, keep),
        out_shape=jax.ShapeDtypeStruct(((1 + keep) * rows, channels, width), f32),
        scratch_shapes=[pltpu.VMEM((4 * hidden, width), bf16)] * 2,
        compiler_params=params,
        name="move",
    )(field, *close, *far, w_out)


def crps_kernel(weight_ref, fields_ref, targets_ref, out_ref):
    members, height, width = fields_ref.shape
    mine = lax.axis_index(MEMBER)
    weight = jnp.where(lax.rem(lax.div(mine, 2), 2) == 0, weight_ref[:8, :], weight_ref[8:, :])
    softness = smooth_width * smooth_width
    loss = jnp.zeros((8, width), f32)
    for tile in range(0, height, 8):
        values = [fields_ref[m, tile : tile + 8, :] for m in range(members)]
        truth = targets_ref[mine, tile : tile + 8, :]
        direct = jnp.zeros((8, width), f32)
        pairs = jnp.full((8, width), members * smooth_width, f32)
        slopes = [jnp.zeros((8, width), f32) for m in range(members)]
        grads = []
        for m in range(members):
            error = values[m] - truth
            square = error * error + softness
            inverse = lax.rsqrt(square)
            direct = direct + square * inverse
            grads.append(error * inverse)
            for other in range(m + 1, members):
                gap = values[m] - values[other]
                square = gap * gap + softness
                inverse = lax.rsqrt(square)
                pairs = pairs + 2.0 * square * inverse
                slope = gap * inverse
                slopes[m] = slopes[m] + slope
                slopes[other] = slopes[other] - slope
        loss = loss + weight * (direct - pairs / (2.0 * (members - 1)))
        for m in range(members):
            out_ref[m, tile : tile + 8, :] = weight * (grads[m] - slopes[m] / (members - 1))
    for m in range(members):
        out_ref[m, height : height + 8, :] = loss


def crps(weights, fields, targets):
    members, height, width = fields.shape
    return pl.pallas_call(
        crps_kernel,
        out_shape=jax.ShapeDtypeStruct((members, height + 8, width), f32),
        compiler_params=params,
        name="crps",
    )(weights, fields, targets)


def collect_kernel(grads_ref, first_ref, second_ref, known_ref):
    chunks, height, width = grads_ref.shape
    height = height - 8
    half = chunks // 2
    total = grads_ref[0, height : height + 8, :]
    for chunk in range(1, chunks):
        total = total + grads_ref[chunk, height : height + 8, :]
    for chunk in range(half):
        first_ref[chunk * height : (chunk + 1) * height, :] = grads_ref[chunk, :height, :]
        second_ref[chunk * height : (chunk + 1) * height, :] = grads_ref[half + chunk, :height, :]
    known = jnp.broadcast_to(jnp.sum(total, axis=0, keepdims=True), (slab_count, width))
    slab = lax.broadcasted_iota(jnp.int32, known.shape, 0)
    known = jnp.where(slab == lax.axis_index(LAT), known, 0.0)
    second_ref[half * height :, :] = known
    known_ref[...] = known


def collect(grads):
    chunks, height, width = grads.shape
    count = chunks // 2 * (height - 8)
    return pl.pallas_call(
        collect_kernel,
        out_shape=[
            jax.ShapeDtypeStruct((count, width), f32),
            jax.ShapeDtypeStruct((count + slab_count, width), f32),
            jax.ShapeDtypeStruct((slab_count, width), f32),
        ],
        compiler_params=params,
        name="collect",
    )(grads)


def merged(*known):
    result = known[0]
    for other in known[1:]:
        result = jnp.where(result != 0.0, result, other)
    return result


def table_of(*refs):
    return merged(*(ref[ref.shape[0] - slab_count :, :] for ref in refs))


def hidden_grads(step, near_side, beside_ref, own_ref, slope_ref, weight_ref, wide):
    width = own_ref.shape[1]
    channels = (own_ref.shape[0] - slab_count) // 2

    def rows_of(ref):
        return lambda row: ref[row * channels : (row + 1) * channels, :]

    side_windows(near_side, rows_of(own_ref), rows_of(beside_ref), wide)
    grads = to_channels(weight_ref[...], wide, 0, channels) * slope_ref[0 if near_side else 1]
    return [split(grads[:, half * width : (half + 1) * width]) for half in range(2)]


def backward_side_kernel(step, near_side, own_ref, beside_ref, slope_ref, outb_ref, high_ref, low_ref, wide_hi,
                         wide_lo):
    rows = hidden_grads(step, near_side, beside_ref, own_ref, slope_ref, outb_ref, (wide_hi, wide_lo))
    for half in range(2):
        high_ref[half], low_ref[half] = rows[half]


def backward_side(step, near_side, own, beside, slopes, w_out):
    count, width = own.shape
    channels = (count - slab_count) // 2
    hidden = w_out.shape[0] // 2
    return pl.pallas_call(
        functools.partial(backward_side_kernel, step, near_side),
        out_shape=[jax.ShapeDtypeStruct((2, hidden, width), bf16)] * 2,
        scratch_shapes=[pltpu.VMEM((12 * channels, width), bf16)] * 2,
        compiler_params=params,
        name="backward_near" if near_side else "backward_across",
    )(own, beside, slopes, w_out)


def gather_hidden(hid, close, far):
    hidden = close[0].shape[1]
    even = is_even()
    for half in range(2):
        far_at = pl.multiple_of(jnp.where(even, half, 2 + half) * hidden, hidden)
        close_at = pl.multiple_of(jnp.where(even, 2 + half, half) * hidden, hidden)
        for ref, far_ref, close_ref in zip(hid, far, close):
            ref[pl.ds(far_at, hidden), :] = far_ref[half]
            ref[pl.ds(close_at, hidden), :] = close_ref[half]


def join_kernel(own_ref, close_hi, close_lo, far_hi, far_lo, inb_ref, added_ref, *rest):
    *tables, out_ref, known_ref, hid_hi, hid_lo = rest
    channels = (own_ref.shape[0] - slab_count) // 2
    gather_hidden((hid_hi, hid_lo), (close_hi, close_lo), (far_hi, far_lo))
    moved = from_channels(inb_ref[...], (hid_hi, hid_lo), 0, close_hi.shape[1], channels)
    for row in range(2):
        part = slice(row * channels, (row + 1) * channels)
        out_ref[part, :] = own_ref[part, :] + moved[row] + added_ref[part, :]
    known = table_of(own_ref, *tables)
    out_ref[2 * channels :, :] = known
    known_ref[...] = known


def join(own, close, far, w_in, added, *tables):
    hidden, width = close[0].shape[1:]
    return pl.pallas_call(
        join_kernel,
        out_shape=[
            jax.ShapeDtypeStruct(own.shape, f32),
            jax.ShapeDtypeStruct((slab_count, width), f32),
        ],
        scratch_shapes=[pltpu.VMEM((4 * hidden, width), bf16)] * 2,
        compiler_params=params,
        name="join",
    )(own, *close, *far, w_in, added, *tables)


def finish_kernel(count, own_ref, close_hi, close_lo, far_hi, far_lo, inb_ref, *rest):
    *tables, out_hbm, loss_hbm, out_ref, loss_ref, hid_hi, hid_lo, done = rest
    channels = (own_ref.shape[0] - slab_count) // 2
    total = jnp.sum(table_of(own_ref, *tables), axis=0, keepdims=True)
    loss_ref[...] = jnp.sum(total, axis=1, keepdims=True) / count
    copies = [pltpu.make_async_copy(loss_ref, loss_hbm, done.at[0])]
    copies[0].start()
    gather_hidden((hid_hi, hid_lo), (close_hi, close_lo), (far_hi, far_lo))
    moved = from_channels(inb_ref[...], (hid_hi, hid_lo), 0, close_hi.shape[1], channels)
    for row in range(2):
        part = pl.ds(row * channels, channels)
        out_ref[part, :] = own_ref[part, :] + moved[row]
        copies.append(pltpu.make_async_copy(out_ref.at[part, :], out_hbm.at[part, :], done.at[1 + row]))
        copies[-1].start()
    for copy in copies:
        copy.wait()


def finish(count, own, close, far, w_in, *tables):
    hidden, width = close[0].shape[1:]
    lines = own.shape[0] - slab_count
    vmem = pl.BlockSpec(memory_space=pltpu.VMEM)
    return pl.pallas_call(
        functools.partial(finish_kernel, count),
        out_shape=[
            jax.ShapeDtypeStruct((lines, width), f32),
            jax.ShapeDtypeStruct((1, 1), f32),
        ],
        in_specs=[vmem] * (6 + len(tables)),
        out_specs=[pl.BlockSpec(memory_space=pltpu.HBM)] * 2,
        scratch_shapes=[pltpu.VMEM((lines, width), f32), pltpu.VMEM((1, 1), f32)]
        + [pltpu.VMEM((4 * hidden, width), bf16)] * 2
        + [pltpu.SemaphoreType.DMA((3,))],
        compiler_params=params,
        name="finish",
    )(own, *close, *far, w_in, *tables)


def on_device(initial_states, targets, lat_weight, weight_in, weight_out, hidden_bias):
    members = lax.axis_size(MEMBER)
    slabs = lax.axis_size(LAT)
    steps, slab_rows, channels, width = targets.shape
    rows = slabs * slab_rows
    near = [(i, i ^ 1) for i in range(slabs)]
    across = [(i, (i + 1 if i % 2 else i - 1) % slabs) for i in range(slabs)]

    own = initial_states[0]
    beside = lax.ppermute(own, LAT, near)
    crossed = lax.ppermute(own, LAT, across)
    ready = prepare(weight_in.T, weight_out, hidden_bias[None, :], lat_weight[None, :], width)
    w_in, w_out, bias, lat_weights, *raw = ready
    before_near, *close = forward_side(True, own, beside, bias, w_in)
    crossed, close = lax.optimization_barrier((crossed, close))
    before_across, *distant = forward_side(False, own, crossed, bias, w_in)
    before_first = (before_near, before_across)
    field = move(0, own, close, distant, w_out)
    beside = lax.ppermute(field, LAT, near)
    crossed = lax.ppermute(field, LAT, across)
    before_near, *close = forward_side(True, field, beside, bias, w_in)
    raw, close = lax.optimization_barrier((raw, close))
    back = prepare_back(*raw)
    crossed, close, back = lax.optimization_barrier((crossed, close, back))
    w_out_back, w_in_back = back
    before_across, *distant = forward_side(False, field, crossed, bias, w_in)
    before_second = (before_near, before_across)
    fields = move(1, field, close, distant, w_out)
    height = steps * slab_rows * channels // members
    chunks = lax.all_to_all(
        fields.reshape(members, height, width), MEMBER, split_axis=0, concat_axis=0, tiled=True
    )
    grads = crps(lat_weights, chunks, targets.reshape(members, height, width))
    grads = lax.all_to_all(grads, MEMBER, split_axis=0, concat_axis=0, tiled=True)
    slopes = slopes_of(*before_second)
    first_grads, message, known = collect(grads)

    beside = lax.ppermute(message, LAT, near)
    crossed = lax.ppermute(message, LAT, across)
    opposite = [(i, i ^ 8) for i in range(slabs)]
    ahead = [(i, (i + 5 if i % 2 == 0 else i - 5) % slabs) for i in range(slabs)]
    behind = [(i, (i - 5 if i % 2 == 0 else i + 5) % slabs) for i in range(slabs)]
    distant_tables = [lax.ppermute(known, LAT, pairs) for pairs in (ahead, behind)]
    close = backward_side(1, True, message, beside, slopes, w_out_back)
    crossed, close = lax.optimization_barrier((crossed, close))
    distant = backward_side(1, False, message, crossed, slopes, w_out_back)
    message, known = join(
        message, close, distant, w_in_back, first_grads, beside, crossed, *distant_tables
    )
    beside = lax.ppermute(message, LAT, near)
    crossed = lax.ppermute(message, LAT, across)
    distant_tables = [lax.ppermute(known, LAT, pairs) for pairs in (opposite,)]
    message, before_first = lax.optimization_barrier((message, before_first))
    slopes = slopes_of(*before_first)
    close = backward_side(0, True, message, beside, slopes, w_out_back)
    crossed, close = lax.optimization_barrier((crossed, close))
    distant = backward_side(0, False, message, crossed, slopes, w_out_back)
    count = members * steps * rows * channels * width
    gradient, loss = finish(
        count, message, close, distant, w_in_back, beside, crossed, *distant_tables
    )
    loss = loss.reshape(())
    return gradient.reshape(initial_states.shape), loss


def solution(mesh):
    torus = Mesh(
        mesh.devices.reshape(4, 2, 2, 4, 2), ("member_0", "member_1", "lat_0", "lat_1", "lat_2")
    )
    placed = (P(MEMBER, LAT, None, None), P(None, LAT, None, None), P(LAT), P(), P(), P())
    return jax.shard_map(
        on_device,
        mesh=torus,
        in_specs=placed,
        out_specs=(P(MEMBER, LAT, None, None), P()),
        check_vma=False,
    )
```

```python
import functools

import jax
import jax.numpy as jnp
from jax import lax
from jax.experimental import pallas as pl
from jax.experimental.pallas import tpu as pltpu
from jax.sharding import Mesh
from jax.sharding import PartitionSpec as P

MEMBER = ("member_0", "member_1")
LAT = ("lat_0", "lat_1", "lat_2")

smooth_width = 0.1
gelu_scale = 0.7978845608028654
gelu_cubic = 0.044715
slab_count = 16

f32 = jnp.float32
bf16 = jnp.bfloat16
params = pltpu.CompilerParams(vmem_limit_bytes=16 * 1024 * 1024)


def split(value):
    high = value.astype(bf16)
    return high, (value - high.astype(f32)).astype(bf16)


def product(left, right):
    dot = functools.partial(jnp.dot, preferred_element_type=f32)
    count = left.shape[0] // 2
    both = dot(left, right[0])
    return both[:count] + (both[count:] + dot(left[:count], right[1]))


def from_left(row):
    lane = lax.broadcasted_iota(jnp.int32, row.shape, 1)
    return jnp.where(lane == 0, 0.0, pltpu.roll(row, 1, 1))


def from_right(row):
    lane = lax.broadcasted_iota(jnp.int32, row.shape, 1)
    return jnp.where(lane == row.shape[1] - 1, 0.0, pltpu.roll(row, row.shape[1] - 1, 1))


def put(refs, start, values):
    for ref, value in zip(refs, values):
        ref[start : start + value.shape[0], :] = value


def put_windows(refs, index, row):
    channels = row.shape[0]
    for part, shifted in enumerate((from_left(row), row, from_right(row))):
        put(refs, (3 * index + part) * channels, split(shifted))


def read(refs, start, size, height):
    parts = [(ref[start : start + size, :], ref[start + height : start + height + size, :]) for ref in refs]
    return tuple(jnp.concatenate(part, axis=1) for part in parts)


def to_channels(weights, windows, pair, channels):
    return product(weights, read(windows, pair * 3 * channels, 9 * channels, 3 * channels))


def combined(mixed, outer):
    width = mixed.shape[1] // 2
    rows = []
    for half in range(2):
        part = mixed[:, half * width : (half + 1) * width]
        rows.append(
            from_left(part[:outer])
            + part[outer : 2 * outer]
            + from_right(part[2 * outer :])
        )
    return rows


def gelu(x, half):
    t = jnp.tanh(x * (gelu_scale + (gelu_scale * gelu_cubic) * (x * x)))
    h = half * x
    return h + h * t


def gelu_slope(x):
    t = jnp.tanh(gelu_scale * (x + gelu_cubic * x * x * x))
    inner = gelu_scale * (1.0 + 3.0 * gelu_cubic * x * x)
    return 0.5 * (1.0 + t) + 0.5 * x * (1.0 - t * t) * inner


def fetch(pairs, arrived):
    copies = [pltpu.make_async_copy(*pair, arrived.at[i]) for i, pair in enumerate(pairs)]
    for copy in copies:
        copy.start()
    for copy in copies:
        copy.wait()


def prepare_kernel(win_hbm, wout_hbm, bias_hbm, lat_hbm, in_ref, out_ref, wide_bias_ref, wide_lat_ref,
                   win_ref, wout_ref, bias_ref, lat_ref, arrived):
    fetch(((win_hbm, win_ref), (wout_hbm, wout_ref), (bias_hbm, bias_ref), (lat_hbm, lat_ref)), arrived)
    outer, width = wout_ref.shape
    hidden = width // 9
    in_ref[:hidden, :], in_ref[hidden:, :] = split(win_ref[...].T)
    for a in range(3):
        for b in range(3):
            tap = 3 * a + b
            high, low = split(wout_ref[:, tap * hidden : (tap + 1) * hidden])
            out_ref[b * outer : (b + 1) * outer, a * hidden : (a + 1) * hidden] = high
            out_ref[(3 + b) * outer : (4 + b) * outer, a * hidden : (a + 1) * hidden] = low
    wide_bias_ref[...] = jnp.broadcast_to(bias_ref[...], wide_bias_ref.shape[::-1]).T
    for row in range(2):
        one = jnp.broadcast_to(lat_ref[:, row : row + 1], (8, wide_lat_ref.shape[1]))
        wide_lat_ref[8 * row : 8 * (row + 1), :] = one


def prepare(weight_in, weight_out, bias, lat_weight, width):
    taps_in, hidden = weight_in.shape
    outer = weight_out.shape[0]
    arrays = (weight_in, weight_out, bias, lat_weight)
    shapes = [(2 * hidden, taps_in), (6 * outer, 3 * hidden)]
    return pl.pallas_call(
        prepare_kernel,
        out_shape=[jax.ShapeDtypeStruct(shape, bf16) for shape in shapes]
        + [jax.ShapeDtypeStruct((hidden, width), f32), jax.ShapeDtypeStruct((16, width), f32)]
        + [jax.ShapeDtypeStruct(array.shape, f32) for array in arrays[:2]],
        in_specs=[pl.BlockSpec(memory_space=pltpu.HBM)] * 4,
        scratch_shapes=[pltpu.VMEM(array.shape, f32) for array in arrays[2:]] + [pltpu.SemaphoreType.DMA((4,))],
        compiler_params=params,
        name="prepare",
    )(*(pltpu.with_memory_space_constraint(array, pltpu.HBM) for array in arrays))


def prepare_back_kernel(win_ref, wout_ref, *rest):
    before_refs, (outb_ref, inb_ref, slope_ref, stack) = rest[:4], rest[4:]
    for side in range(2):
        below = is_even() if side == 0 else jnp.logical_not(is_even())
        first = jnp.where(below, 0, -2)
        for step, before_ref in enumerate(before_refs[side::2]):
            slope = gelu_slope(before_ref[...])
            width = slope.shape[1] // 2
            for half in range(2):
                part = slope[:, half * width : (half + 1) * width]
                part = jnp.where(inside(first + 1 + half), part, 0.0)
                slope_ref[step, side, :, half * width : (half + 1) * width] = part
    outer, width = wout_ref.shape
    hidden = width // 9
    inner = win_ref.shape[0] // 9
    for a in range(3):
        for b in range(3):
            tap = 3 * a + b
            stack[(8 - tap) * outer : (9 - tap) * outer, :] = wout_ref[:, tap * hidden : (tap + 1) * hidden]
            high, low = split(win_ref[tap * inner : (tap + 1) * inner, :])
            j, k = 2 - a, 2 - b
            inb_ref[k * inner : (k + 1) * inner, j * hidden : (j + 1) * hidden] = high
            inb_ref[(3 + k) * inner : (4 + k) * inner, j * hidden : (j + 1) * hidden] = low
    outb_ref[:hidden, :], outb_ref[hidden:, :] = split(stack[...].T)


def prepare_back(weight_in, weight_out, *before):
    taps_in, hidden = weight_in.shape
    outer = weight_out.shape[0]
    inner = taps_in // 9
    shapes = [(2 * hidden, 9 * outer), (6 * inner, 3 * hidden)]
    return pl.pallas_call(
        prepare_back_kernel,
        out_shape=[jax.ShapeDtypeStruct(shape, bf16) for shape in shapes]
        + [jax.ShapeDtypeStruct((2, 2, *before[0].shape), f32)],
        scratch_shapes=[pltpu.VMEM((9 * outer, hidden), f32)],
        compiler_params=params,
        name="prepare_back",
    )(weight_in, weight_out, *before)


def inside(row):
    index = lax.axis_index(LAT) * 2 + row
    return (index >= 0) & (index < 2 * slab_count)


def is_even():
    return lax.rem(lax.axis_index(LAT), 2) == 0


def side_windows(near_side, own, beside, wide):
    even = is_even()
    below = even if near_side else jnp.logical_not(even)
    first = jnp.where(below, 0, -2)
    for index in range(4):
        mine, other = own(index % 2), beside(index % 2)
        row = jnp.where(below, mine, other) if index < 2 else jnp.where(below, other, mine)
        put_windows(wide, index, jnp.where(inside(first + index), row, 0.0))
    return first


def forward_side_kernel(near_side, own_ref, beside_ref, bias_ref, in_ref, before_ref, high_ref, low_ref, wide_hi,
                        wide_lo):
    channels, width = own_ref.shape[1:]
    wide = (wide_hi, wide_lo)
    first = side_windows(near_side, lambda row: own_ref[row], lambda row: beside_ref[row], wide)
    before = to_channels(in_ref[...], wide, 0, channels) + jnp.concatenate([bias_ref[...]] * 2, axis=1)
    before_ref[...] = before
    for half in range(2):
        scale = jnp.where(inside(first + 1 + half), 0.5, 0.0)
        active = gelu(before[:, half * width : (half + 1) * width], scale)
        high_ref[half], low_ref[half] = split(active)


def forward_side(near_side, own, beside, bias, w_in):
    channels, width = own.shape[1:]
    hidden = w_in.shape[0] // 2
    return pl.pallas_call(
        functools.partial(forward_side_kernel, near_side),
        out_shape=[jax.ShapeDtypeStruct((hidden, 2 * width), f32)]
        + [jax.ShapeDtypeStruct((2, hidden, width), bf16)] * 2,
        scratch_shapes=[pltpu.VMEM((12 * channels, width), bf16)] * 2,
        compiler_params=params,
        name="forward_near" if near_side else "forward_across",
    )(own, beside, bias, w_in)


def move_kernel(keep, field_ref, close_hi, close_lo, far_hi, far_lo, out_ref, moved_ref):
    rows, channels, width = field_ref.shape

    def use(moved):
        for row in range(rows):
            if keep:
                moved_ref[row] = field_ref[row]
            moved_ref[rows * keep + row] = field_ref[row] + moved[row]

    from_sides(out_ref, (close_hi, close_lo), (far_hi, far_lo), channels, use)


def move(keep, field, close, far, w_out):
    rows, channels, width = field.shape
    hidden = close[0].shape[1]
    return pl.pallas_call(
        functools.partial(move_kernel, keep),
        out_shape=jax.ShapeDtypeStruct(((1 + keep) * rows, channels, width), f32),
        compiler_params=params,
        name="move",
    )(field, *close, *far, w_out)


def crps_kernel(weight_ref, fields_ref, targets_ref, out_ref):
    members, height, width = fields_ref.shape
    mine = lax.axis_index(MEMBER)
    weight = jnp.where(lax.rem(lax.div(mine, 2), 2) == 0, weight_ref[:8, :], weight_ref[8:, :])
    softness = smooth_width * smooth_width
    loss = jnp.zeros((8, width), f32)
    for tile in range(0, height, 8):
        values = [fields_ref[m, tile : tile + 8, :] for m in range(members)]
        truth = targets_ref[mine, tile : tile + 8, :]
        direct = jnp.zeros((8, width), f32)
        pairs = jnp.full((8, width), members * smooth_width, f32)
        slopes = [jnp.zeros((8, width), f32) for m in range(members)]
        grads = []
        for m in range(members):
            error = values[m] - truth
            square = error * error + softness
            inverse = lax.rsqrt(square)
            direct = direct + square * inverse
            grads.append(error * inverse)
            for other in range(m + 1, members):
                gap = values[m] - values[other]
                square = gap * gap + softness
                inverse = lax.rsqrt(square)
                pairs = pairs + 2.0 * square * inverse
                slope = gap * inverse
                slopes[m] = slopes[m] + slope
                slopes[other] = slopes[other] - slope
        loss = loss + weight * (direct - pairs / (2.0 * (members - 1)))
        for m in range(members):
            out_ref[m, tile : tile + 8, :] = weight * (grads[m] - slopes[m] / (members - 1))
    for m in range(members):
        out_ref[m, height : height + 8, :] = loss


def crps(weights, fields, targets):
    members, height, width = fields.shape
    return pl.pallas_call(
        crps_kernel,
        out_shape=jax.ShapeDtypeStruct((members, height + 8, width), f32),
        compiler_params=params,
        name="crps",
    )(weights, fields, targets)


def collect_kernel(grads_ref, first_ref, second_ref, known_ref):
    chunks, height, width = grads_ref.shape
    height = height - 8
    half = chunks // 2
    total = grads_ref[0, height : height + 8, :]
    for chunk in range(1, chunks):
        total = total + grads_ref[chunk, height : height + 8, :]
    for chunk in range(half):
        first_ref[chunk * height : (chunk + 1) * height, :] = grads_ref[chunk, :height, :]
        second_ref[chunk * height : (chunk + 1) * height, :] = grads_ref[half + chunk, :height, :]
    known = jnp.broadcast_to(jnp.sum(total, axis=0, keepdims=True), (slab_count, width))
    slab = lax.broadcasted_iota(jnp.int32, known.shape, 0)
    known = jnp.where(slab == lax.axis_index(LAT), known, 0.0)
    second_ref[half * height :, :] = known
    known_ref[...] = known


def collect(grads):
    chunks, height, width = grads.shape
    count = chunks // 2 * (height - 8)
    return pl.pallas_call(
        collect_kernel,
        out_shape=[
            jax.ShapeDtypeStruct((count, width), f32),
            jax.ShapeDtypeStruct((count + slab_count, width), f32),
            jax.ShapeDtypeStruct((slab_count, width), f32),
        ],
        compiler_params=params,
        name="collect",
    )(grads)


def merged(*known):
    result = known[0]
    for other in known[1:]:
        result = jnp.where(result != 0.0, result, other)
    return result


def table_of(*refs):
    return merged(*(ref[ref.shape[0] - slab_count :, :] for ref in refs))


def hidden_grads(step, near_side, beside_ref, own_ref, slope_ref, weight_ref, wide):
    width = own_ref.shape[1]
    channels = (own_ref.shape[0] - slab_count) // 2

    def rows_of(ref):
        return lambda row: ref[row * channels : (row + 1) * channels, :]

    side_windows(near_side, rows_of(own_ref), rows_of(beside_ref), wide)
    grads = to_channels(weight_ref[...], wide, 0, channels) * slope_ref[step, 0 if near_side else 1]
    return [split(grads[:, half * width : (half + 1) * width]) for half in range(2)]


def backward_side_kernel(step, near_side, own_ref, beside_ref, slope_ref, outb_ref, high_ref, low_ref, wide_hi,
                         wide_lo):
    rows = hidden_grads(step, near_side, beside_ref, own_ref, slope_ref, outb_ref, (wide_hi, wide_lo))
    for half in range(2):
        high_ref[half], low_ref[half] = rows[half]


def backward_side(step, near_side, own, beside, slopes, w_out):
    count, width = own.shape
    channels = (count - slab_count) // 2
    hidden = w_out.shape[0] // 2
    return pl.pallas_call(
        functools.partial(backward_side_kernel, step, near_side),
        out_shape=[jax.ShapeDtypeStruct((2, hidden, width), bf16)] * 2,
        scratch_shapes=[pltpu.VMEM((12 * channels, width), bf16)] * 2,
        compiler_params=params,
        name="backward_near" if near_side else "backward_across",
    )(own, beside, slopes, w_out)


def from_sides(weights_ref, close, far, outer, use):
    def run(first, second):
        right = []
        for one, two in zip(first, second):
            rows = [one[0], one[1], two[0], two[1]]
            stacks = [jnp.concatenate(rows[at : at + 3], axis=0) for at in range(2)]
            right.append(jnp.concatenate(stacks, axis=1))
        use(combined(product(weights_ref[...], right), outer))

    pl.when(is_even())(lambda: run(far, close))
    pl.when(jnp.logical_not(is_even()))(lambda: run(close, far))


def join_kernel(own_ref, close_hi, close_lo, far_hi, far_lo, inb_ref, added_ref, *rest):
    *tables, out_ref, known_ref = rest
    channels = (own_ref.shape[0] - slab_count) // 2

    def use(moved):
        for row in range(2):
            part = slice(row * channels, (row + 1) * channels)
            out_ref[part, :] = own_ref[part, :] + moved[row] + added_ref[part, :]

    from_sides(inb_ref, (close_hi, close_lo), (far_hi, far_lo), channels, use)
    known = table_of(own_ref, *tables)
    out_ref[2 * channels :, :] = known
    known_ref[...] = known


def join(own, close, far, w_in, added, *tables):
    hidden, width = close[0].shape[1:]
    return pl.pallas_call(
        join_kernel,
        out_shape=[
            jax.ShapeDtypeStruct(own.shape, f32),
            jax.ShapeDtypeStruct((slab_count, width), f32),
        ],
        compiler_params=params,
        name="join",
    )(own, *close, *far, w_in, added, *tables)


def finish_kernel(count, own_ref, close_hi, close_lo, far_hi, far_lo, inb_ref, *rest):
    *tables, out_hbm, loss_hbm, out_ref, loss_ref, done = rest
    channels = (own_ref.shape[0] - slab_count) // 2
    total = jnp.sum(table_of(own_ref, *tables), axis=0, keepdims=True)
    loss_ref[...] = jnp.sum(total, axis=1, keepdims=True) / count
    copies = [pltpu.make_async_copy(loss_ref, loss_hbm, done.at[0])]
    copies[0].start()

    def use(moved):
        for row in range(2):
            part = slice(row * channels, (row + 1) * channels)
            out_ref[part, :] = own_ref[part, :] + moved[row]

    from_sides(inb_ref, (close_hi, close_lo), (far_hi, far_lo), channels, use)
    copies.append(pltpu.make_async_copy(out_ref, out_hbm, done.at[1]))
    copies[-1].start()
    for copy in copies:
        copy.wait()


def finish(count, own, close, far, w_in, *tables):
    hidden, width = close[0].shape[1:]
    lines = own.shape[0] - slab_count
    vmem = pl.BlockSpec(memory_space=pltpu.VMEM)
    return pl.pallas_call(
        functools.partial(finish_kernel, count),
        out_shape=[
            jax.ShapeDtypeStruct((lines, width), f32),
            jax.ShapeDtypeStruct((1, 1), f32),
        ],
        in_specs=[vmem] * (6 + len(tables)),
        out_specs=[pl.BlockSpec(memory_space=pltpu.HBM)] * 2,
        scratch_shapes=[pltpu.VMEM((lines, width), f32), pltpu.VMEM((1, 1), f32)]
        + [pltpu.SemaphoreType.DMA((2,))],
        compiler_params=params,
        name="finish",
    )(own, *close, *far, w_in, *tables)


def on_device(initial_states, targets, lat_weight, weight_in, weight_out, hidden_bias):
    members = lax.axis_size(MEMBER)
    slabs = lax.axis_size(LAT)
    steps, slab_rows, channels, width = targets.shape
    rows = slabs * slab_rows
    near = [(i, i ^ 1) for i in range(slabs)]
    across = [(i, (i + 1 if i % 2 else i - 1) % slabs) for i in range(slabs)]

    own = initial_states[0]
    beside = lax.ppermute(own, LAT, near)
    crossed = lax.ppermute(own, LAT, across)
    ready = prepare(weight_in.T, weight_out, hidden_bias[None, :], lat_weight[None, :], width)
    w_in, w_out, bias, lat_weights, *raw = ready
    before_near, *close = forward_side(True, own, beside, bias, w_in)
    crossed, close = lax.optimization_barrier((crossed, close))
    before_across, *distant = forward_side(False, own, crossed, bias, w_in)
    before_first = (before_near, before_across)
    field = move(0, own, close, distant, w_out)
    beside = lax.ppermute(field, LAT, near)
    crossed = lax.ppermute(field, LAT, across)
    before_near, *close = forward_side(True, field, beside, bias, w_in)
    crossed, close = lax.optimization_barrier((crossed, close))
    before_across, *distant = forward_side(False, field, crossed, bias, w_in)
    before_second = (before_near, before_across)
    fields = move(1, field, close, distant, w_out)
    height = steps * slab_rows * channels // members
    chunks = lax.all_to_all(
        fields.reshape(members, height, width), MEMBER, split_axis=0, concat_axis=0, tiled=True
    )
    grads = crps(lat_weights, chunks, targets.reshape(members, height, width))
    grads = lax.all_to_all(grads, MEMBER, split_axis=0, concat_axis=0, tiled=True)
    back = prepare_back(*raw, *before_first, *before_second)
    w_out_back, w_in_back, slopes = back
    first_grads, message, known = collect(grads)

    beside = lax.ppermute(message, LAT, near)
    crossed = lax.ppermute(message, LAT, across)
    opposite = [(i, i ^ 8) for i in range(slabs)]
    ahead = [(i, (i + 5 if i % 2 == 0 else i - 5) % slabs) for i in range(slabs)]
    behind = [(i, (i - 5 if i % 2 == 0 else i + 5) % slabs) for i in range(slabs)]
    distant_tables = [lax.ppermute(known, LAT, pairs) for pairs in (ahead, behind)]
    close = backward_side(1, True, message, beside, slopes, w_out_back)
    crossed, close = lax.optimization_barrier((crossed, close))
    distant = backward_side(1, False, message, crossed, slopes, w_out_back)
    message, known = join(
        message, close, distant, w_in_back, first_grads, beside, crossed, *distant_tables
    )
    beside = lax.ppermute(message, LAT, near)
    crossed = lax.ppermute(message, LAT, across)
    distant_tables = [lax.ppermute(known, LAT, pairs) for pairs in (opposite,)]
    close = backward_side(0, True, message, beside, slopes, w_out_back)
    crossed, close = lax.optimization_barrier((crossed, close))
    distant = backward_side(0, False, message, crossed, slopes, w_out_back)
    count = members * steps * rows * channels * width
    gradient, loss = finish(
        count, message, close, distant, w_in_back, beside, crossed, *distant_tables
    )
    loss = loss.reshape(())
    return gradient.reshape(initial_states.shape), loss


def solution(mesh):
    torus = Mesh(
        mesh.devices.reshape(4, 2, 2, 4, 2), ("member_0", "member_1", "lat_0", "lat_1", "lat_2")
    )
    placed = (P(MEMBER, LAT, None, None), P(None, LAT, None, None), P(LAT), P(), P(), P())
    return jax.shard_map(
        on_device,
        mesh=torus,
        in_specs=placed,
        out_specs=(P(MEMBER, LAT, None, None), P()),
        check_vma=False,
    )
```

```python
import functools

import jax
import jax.numpy as jnp
from jax import lax
from jax.experimental import pallas as pl
from jax.experimental.pallas import tpu as pltpu
from jax.sharding import Mesh
from jax.sharding import PartitionSpec as P

MEMBER = ("member_0", "member_1")
LAT = ("lat_0", "lat_1", "lat_2")

smooth_width = 0.1
gelu_scale = 0.7978845608028654
gelu_cubic = 0.044715
slab_count = 16

f32 = jnp.float32
bf16 = jnp.bfloat16
params = pltpu.CompilerParams(vmem_limit_bytes=16 * 1024 * 1024)


def split(value):
    high = value.astype(bf16)
    return high, (value - high.astype(f32)).astype(bf16)


def product(left, right):
    dot = functools.partial(jnp.dot, preferred_element_type=f32)
    count = left.shape[0] // 2
    both = dot(left, right[0])
    return both[:count] + (both[count:] + dot(left[:count], right[1]))


def from_left(row):
    lane = lax.broadcasted_iota(jnp.int32, row.shape, 1)
    return jnp.where(lane == 0, 0.0, pltpu.roll(row, 1, 1))


def from_right(row):
    lane = lax.broadcasted_iota(jnp.int32, row.shape, 1)
    return jnp.where(lane == row.shape[1] - 1, 0.0, pltpu.roll(row, row.shape[1] - 1, 1))


def put(refs, start, values):
    for ref, value in zip(refs, values):
        ref[start : start + value.shape[0], :] = value


def put_windows(refs, index, row):
    channels = row.shape[0]
    for part, shifted in enumerate((from_left(row), row, from_right(row))):
        put(refs, (3 * index + part) * channels, split(shifted))


def read(refs, start, size, height):
    parts = [(ref[start : start + size, :], ref[start + height : start + height + size, :]) for ref in refs]
    return tuple(jnp.concatenate(part, axis=1) for part in parts)


def to_channels(weights, windows, pair, channels):
    return product(weights, read(windows, pair * 3 * channels, 9 * channels, 3 * channels))


def from_channels(weights, hidden, pair, channels, outer):
    mixed = product(weights, read(hidden, pair * channels, 3 * channels, channels))
    width = mixed.shape[1] // 2
    rows = []
    for half in range(2):
        part = mixed[:, half * width : (half + 1) * width]
        rows.append(
            from_left(part[:outer])
            + part[outer : 2 * outer]
            + from_right(part[2 * outer :])
        )
    return rows


def gelu(x, half):
    t = jnp.tanh(x * (gelu_scale + (gelu_scale * gelu_cubic) * (x * x)))
    h = half * x
    return h + h * t


def gelu_slope(x):
    t = jnp.tanh(gelu_scale * (x + gelu_cubic * x * x * x))
    inner = gelu_scale * (1.0 + 3.0 * gelu_cubic * x * x)
    return 0.5 * (1.0 + t) + 0.5 * x * (1.0 - t * t) * inner


def fetch(pairs, arrived):
    copies = [pltpu.make_async_copy(*pair, arrived.at[i]) for i, pair in enumerate(pairs)]
    for copy in copies:
        copy.start()
    for copy in copies:
        copy.wait()


def prepare_kernel(win_hbm, wout_hbm, bias_hbm, lat_hbm, in_ref, out_ref, wide_bias_ref, wide_lat_ref,
                   win_ref, wout_ref, bias_ref, lat_ref, arrived):
    fetch(((win_hbm, win_ref), (wout_hbm, wout_ref), (bias_hbm, bias_ref), (lat_hbm, lat_ref)), arrived)
    outer, width = wout_ref.shape
    hidden = width // 9
    in_ref[:hidden, :], in_ref[hidden:, :] = split(win_ref[...].T)
    for a in range(3):
        for b in range(3):
            tap = 3 * a + b
            high, low = split(wout_ref[:, tap * hidden : (tap + 1) * hidden])
            out_ref[b * outer : (b + 1) * outer, a * hidden : (a + 1) * hidden] = high
            out_ref[(3 + b) * outer : (4 + b) * outer, a * hidden : (a + 1) * hidden] = low
    wide_bias_ref[...] = jnp.broadcast_to(bias_ref[...], wide_bias_ref.shape[::-1]).T
    for row in range(2):
        one = jnp.broadcast_to(lat_ref[:, row : row + 1], (8, wide_lat_ref.shape[1]))
        wide_lat_ref[8 * row : 8 * (row + 1), :] = one


def prepare(weight_in, weight_out, bias, lat_weight, width):
    taps_in, hidden = weight_in.shape
    outer = weight_out.shape[0]
    arrays = (weight_in, weight_out, bias, lat_weight)
    shapes = [(2 * hidden, taps_in), (6 * outer, 3 * hidden)]
    return pl.pallas_call(
        prepare_kernel,
        out_shape=[jax.ShapeDtypeStruct(shape, bf16) for shape in shapes]
        + [jax.ShapeDtypeStruct((hidden, width), f32), jax.ShapeDtypeStruct((16, width), f32)]
        + [jax.ShapeDtypeStruct(array.shape, f32) for array in arrays[:2]],
        in_specs=[pl.BlockSpec(memory_space=pltpu.HBM)] * 4,
        scratch_shapes=[pltpu.VMEM(array.shape, f32) for array in arrays[2:]] + [pltpu.SemaphoreType.DMA((4,))],
        compiler_params=params,
        name="prepare",
    )(*(pltpu.with_memory_space_constraint(array, pltpu.HBM) for array in arrays))


def prepare_back_kernel(win_ref, wout_ref, outb_ref, inb_ref, stack):
    outer, width = wout_ref.shape
    hidden = width // 9
    inner = win_ref.shape[0] // 9
    for a in range(3):
        for b in range(3):
            tap = 3 * a + b
            stack[(8 - tap) * outer : (9 - tap) * outer, :] = wout_ref[:, tap * hidden : (tap + 1) * hidden]
            high, low = split(win_ref[tap * inner : (tap + 1) * inner, :])
            j, k = 2 - a, 2 - b
            inb_ref[k * inner : (k + 1) * inner, j * hidden : (j + 1) * hidden] = high
            inb_ref[(3 + k) * inner : (4 + k) * inner, j * hidden : (j + 1) * hidden] = low
    outb_ref[:hidden, :], outb_ref[hidden:, :] = split(stack[...].T)


def prepare_back(weight_in, weight_out):
    taps_in, hidden = weight_in.shape
    outer = weight_out.shape[0]
    shapes = [(2 * hidden, 9 * outer), (6 * (taps_in // 9), 3 * hidden)]
    return pl.pallas_call(
        prepare_back_kernel,
        out_shape=[jax.ShapeDtypeStruct(shape, bf16) for shape in shapes],
        scratch_shapes=[pltpu.VMEM((9 * outer, hidden), f32)],
        compiler_params=params,
        name="prepare_back",
    )(weight_in, weight_out)


def slopes_kernel(*refs):
    *before_refs, slope_ref = refs
    for side in range(2):
        below = is_even() if side == 0 else jnp.logical_not(is_even())
        first = jnp.where(below, 0, -2)
        for step, before_ref in enumerate(before_refs[side::2]):
            slope = gelu_slope(before_ref[...])
            width = slope.shape[1] // 2
            for half in range(2):
                part = slope[:, half * width : (half + 1) * width]
                part = jnp.where(inside(first + 1 + half), part, 0.0)
                slope_ref[step, side, :, half * width : (half + 1) * width] = part


def slopes_of(*before):
    return pl.pallas_call(
        slopes_kernel,
        out_shape=jax.ShapeDtypeStruct((2, 2, *before[0].shape), f32),
        compiler_params=params,
        name="slopes",
    )(*before)


def inside(row):
    index = lax.axis_index(LAT) * 2 + row
    return (index >= 0) & (index < 2 * slab_count)


def is_even():
    return lax.rem(lax.axis_index(LAT), 2) == 0


def side_windows(near_side, own, beside, wide):
    even = is_even()
    below = even if near_side else jnp.logical_not(even)
    first = jnp.where(below, 0, -2)
    for index in range(4):
        mine, other = own(index % 2), beside(index % 2)
        row = jnp.where(below, mine, other) if index < 2 else jnp.where(below, other, mine)
        put_windows(wide, index, jnp.where(inside(first + index), row, 0.0))
    return first


def forward_side_kernel(near_side, own_ref, beside_ref, bias_ref, in_ref, before_ref, high_ref, low_ref, wide_hi,
                        wide_lo):
    channels, width = own_ref.shape[1:]
    wide = (wide_hi, wide_lo)
    first = side_windows(near_side, lambda row: own_ref[row], lambda row: beside_ref[row], wide)
    before = to_channels(in_ref[...], wide, 0, channels) + jnp.concatenate([bias_ref[...]] * 2, axis=1)
    before_ref[...] = before
    for half in range(2):
        scale = jnp.where(inside(first + 1 + half), 0.5, 0.0)
        active = gelu(before[:, half * width : (half + 1) * width], scale)
        high_ref[half], low_ref[half] = split(active)


def forward_side(near_side, own, beside, bias, w_in):
    channels, width = own.shape[1:]
    hidden = w_in.shape[0] // 2
    return pl.pallas_call(
        functools.partial(forward_side_kernel, near_side),
        out_shape=[jax.ShapeDtypeStruct((hidden, 2 * width), f32)]
        + [jax.ShapeDtypeStruct((2, hidden, width), bf16)] * 2,
        scratch_shapes=[pltpu.VMEM((12 * channels, width), bf16)] * 2,
        compiler_params=params,
        name="forward_near" if near_side else "forward_across",
    )(own, beside, bias, w_in)


def move_kernel(keep, field_ref, close_hi, close_lo, far_hi, far_lo, out_ref, moved_ref, hid_hi, hid_lo):
    rows, channels, width = field_ref.shape
    gather_hidden((hid_hi, hid_lo), (close_hi, close_lo), (far_hi, far_lo))
    moved = from_channels(out_ref[...], (hid_hi, hid_lo), 0, close_hi.shape[1], channels)
    for row in range(rows):
        if keep:
            moved_ref[row] = field_ref[row]
        moved_ref[rows * keep + row] = field_ref[row] + moved[row]


def move(keep, field, close, far, w_out):
    rows, channels, width = field.shape
    hidden = close[0].shape[1]
    return pl.pallas_call(
        functools.partial(move_kernel, keep),
        out_shape=jax.ShapeDtypeStruct(((1 + keep) * rows, channels, width), f32),
        scratch_shapes=[pltpu.VMEM((4 * hidden, width), bf16)] * 2,
        compiler_params=params,
        name="move",
    )(field, *close, *far, w_out)


def crps_kernel(weight_ref, fields_ref, targets_ref, out_ref):
    members, height, width = fields_ref.shape
    mine = lax.axis_index(MEMBER)
    weight = jnp.where(lax.rem(lax.div(mine, 2), 2) == 0, weight_ref[:8, :], weight_ref[8:, :])
    softness = smooth_width * smooth_width
    loss = jnp.zeros((8, width), f32)
    for tile in range(0, height, 8):
        values = [fields_ref[m, tile : tile + 8, :] for m in range(members)]
        truth = targets_ref[mine, tile : tile + 8, :]
        direct = jnp.zeros((8, width), f32)
        pairs = jnp.full((8, width), members * smooth_width, f32)
        slopes = [jnp.zeros((8, width), f32) for m in range(members)]
        grads = []
        for m in range(members):
            error = values[m] - truth
            square = error * error + softness
            inverse = lax.rsqrt(square)
            direct = direct + square * inverse
            grads.append(error * inverse)
            for other in range(m + 1, members):
                gap = values[m] - values[other]
                square = gap * gap + softness
                inverse = lax.rsqrt(square)
                pairs = pairs + 2.0 * square * inverse
                slope = gap * inverse
                slopes[m] = slopes[m] + slope
                slopes[other] = slopes[other] - slope
        loss = loss + weight * (direct - pairs / (2.0 * (members - 1)))
        for m in range(members):
            out_ref[m, tile : tile + 8, :] = weight * (grads[m] - slopes[m] / (members - 1))
    for m in range(members):
        out_ref[m, height : height + 8, :] = loss


def crps(weights, fields, targets):
    members, height, width = fields.shape
    return pl.pallas_call(
        crps_kernel,
        out_shape=jax.ShapeDtypeStruct((members, height + 8, width), f32),
        compiler_params=params,
        name="crps",
    )(weights, fields, targets)


def collect_kernel(grads_ref, first_ref, second_ref, known_ref):
    chunks, height, width = grads_ref.shape
    height = height - 8
    half = chunks // 2
    total = grads_ref[0, height : height + 8, :]
    for chunk in range(1, chunks):
        total = total + grads_ref[chunk, height : height + 8, :]
    for chunk in range(half):
        first_ref[chunk * height : (chunk + 1) * height, :] = grads_ref[chunk, :height, :]
        second_ref[chunk * height : (chunk + 1) * height, :] = grads_ref[half + chunk, :height, :]
    known = jnp.broadcast_to(jnp.sum(total, axis=0, keepdims=True), (slab_count, width))
    slab = lax.broadcasted_iota(jnp.int32, known.shape, 0)
    known = jnp.where(slab == lax.axis_index(LAT), known, 0.0)
    second_ref[half * height :, :] = known
    known_ref[...] = known


def collect(grads):
    chunks, height, width = grads.shape
    count = chunks // 2 * (height - 8)
    return pl.pallas_call(
        collect_kernel,
        out_shape=[
            jax.ShapeDtypeStruct((count, width), f32),
            jax.ShapeDtypeStruct((count + slab_count, width), f32),
            jax.ShapeDtypeStruct((slab_count, width), f32),
        ],
        compiler_params=params,
        name="collect",
    )(grads)


def merged(*known):
    result = known[0]
    for other in known[1:]:
        result = jnp.where(result != 0.0, result, other)
    return result


def table_of(*refs):
    return merged(*(ref[ref.shape[0] - slab_count :, :] for ref in refs))


def hidden_grads(step, near_side, beside_ref, own_ref, slope_ref, weight_ref, wide):
    width = own_ref.shape[1]
    channels = (own_ref.shape[0] - slab_count) // 2

    def rows_of(ref):
        return lambda row: ref[row * channels : (row + 1) * channels, :]

    side_windows(near_side, rows_of(own_ref), rows_of(beside_ref), wide)
    grads = to_channels(weight_ref[...], wide, 0, channels) * slope_ref[step, 0 if near_side else 1]
    return [split(grads[:, half * width : (half + 1) * width]) for half in range(2)]


def backward_side_kernel(step, near_side, own_ref, beside_ref, slope_ref, outb_ref, high_ref, low_ref, wide_hi,
                         wide_lo):
    rows = hidden_grads(step, near_side, beside_ref, own_ref, slope_ref, outb_ref, (wide_hi, wide_lo))
    for half in range(2):
        high_ref[half], low_ref[half] = rows[half]


def backward_side(step, near_side, own, beside, slopes, w_out):
    count, width = own.shape
    channels = (count - slab_count) // 2
    hidden = w_out.shape[0] // 2
    return pl.pallas_call(
        functools.partial(backward_side_kernel, step, near_side),
        out_shape=[jax.ShapeDtypeStruct((2, hidden, width), bf16)] * 2,
        scratch_shapes=[pltpu.VMEM((12 * channels, width), bf16)] * 2,
        compiler_params=params,
        name="backward_near" if near_side else "backward_across",
    )(own, beside, slopes, w_out)


def gather_hidden(hid, close, far):
    hidden = close[0].shape[1]
    even = is_even()
    for half in range(2):
        far_at = pl.multiple_of(jnp.where(even, half, 2 + half) * hidden, hidden)
        close_at = pl.multiple_of(jnp.where(even, 2 + half, half) * hidden, hidden)
        for ref, far_ref, close_ref in zip(hid, far, close):
            ref[pl.ds(far_at, hidden), :] = far_ref[half]
            ref[pl.ds(close_at, hidden), :] = close_ref[half]


def join_kernel(own_ref, close_hi, close_lo, far_hi, far_lo, inb_ref, added_ref, *rest):
    *tables, out_ref, known_ref, hid_hi, hid_lo = rest
    channels = (own_ref.shape[0] - slab_count) // 2
    gather_hidden((hid_hi, hid_lo), (close_hi, close_lo), (far_hi, far_lo))
    moved = from_channels(inb_ref[...], (hid_hi, hid_lo), 0, close_hi.shape[1], channels)
    for row in range(2):
        part = slice(row * channels, (row + 1) * channels)
        out_ref[part, :] = own_ref[part, :] + moved[row] + added_ref[part, :]
    known = table_of(own_ref, *tables)
    out_ref[2 * channels :, :] = known
    known_ref[...] = known


def join(own, close, far, w_in, added, *tables):
    hidden, width = close[0].shape[1:]
    return pl.pallas_call(
        join_kernel,
        out_shape=[
            jax.ShapeDtypeStruct(own.shape, f32),
            jax.ShapeDtypeStruct((slab_count, width), f32),
        ],
        scratch_shapes=[pltpu.VMEM((4 * hidden, width), bf16)] * 2,
        compiler_params=params,
        name="join",
    )(own, *close, *far, w_in, added, *tables)


def finish_kernel(count, own_ref, close_hi, close_lo, far_hi, far_lo, inb_ref, *rest):
    *tables, out_hbm, loss_hbm, out_ref, loss_ref, hid_hi, hid_lo, done = rest
    channels = (own_ref.shape[0] - slab_count) // 2
    total = jnp.sum(table_of(own_ref, *tables), axis=0, keepdims=True)
    loss_ref[...] = jnp.sum(total, axis=1, keepdims=True) / count
    copies = [pltpu.make_async_copy(loss_ref, loss_hbm, done.at[0])]
    copies[0].start()
    gather_hidden((hid_hi, hid_lo), (close_hi, close_lo), (far_hi, far_lo))
    moved = from_channels(inb_ref[...], (hid_hi, hid_lo), 0, close_hi.shape[1], channels)
    for row in range(2):
        part = pl.ds(row * channels, channels)
        out_ref[part, :] = own_ref[part, :] + moved[row]
        copies.append(pltpu.make_async_copy(out_ref.at[part, :], out_hbm.at[part, :], done.at[1 + row]))
        copies[-1].start()
    for copy in copies:
        copy.wait()


def finish(count, own, close, far, w_in, *tables):
    hidden, width = close[0].shape[1:]
    lines = own.shape[0] - slab_count
    vmem = pl.BlockSpec(memory_space=pltpu.VMEM)
    return pl.pallas_call(
        functools.partial(finish_kernel, count),
        out_shape=[
            jax.ShapeDtypeStruct((lines, width), f32),
            jax.ShapeDtypeStruct((1, 1), f32),
        ],
        in_specs=[vmem] * (6 + len(tables)),
        out_specs=[pl.BlockSpec(memory_space=pltpu.HBM)] * 2,
        scratch_shapes=[pltpu.VMEM((lines, width), f32), pltpu.VMEM((1, 1), f32)]
        + [pltpu.VMEM((4 * hidden, width), bf16)] * 2
        + [pltpu.SemaphoreType.DMA((3,))],
        compiler_params=params,
        name="finish",
    )(own, *close, *far, w_in, *tables)


def on_device(initial_states, targets, lat_weight, weight_in, weight_out, hidden_bias):
    members = lax.axis_size(MEMBER)
    slabs = lax.axis_size(LAT)
    steps, slab_rows, channels, width = targets.shape
    rows = slabs * slab_rows
    near = [(i, i ^ 1) for i in range(slabs)]
    across = [(i, (i + 1 if i % 2 else i - 1) % slabs) for i in range(slabs)]

    own = initial_states[0]
    beside = lax.ppermute(own, LAT, near)
    crossed = lax.ppermute(own, LAT, across)
    ready = prepare(weight_in.T, weight_out, hidden_bias[None, :], lat_weight[None, :], width)
    w_in, w_out, bias, lat_weights, *raw = ready
    before_near, *close = forward_side(True, own, beside, bias, w_in)
    crossed, close = lax.optimization_barrier((crossed, close))
    before_across, *distant = forward_side(False, own, crossed, bias, w_in)
    before_first = (before_near, before_across)
    field = move(0, own, close, distant, w_out)
    beside = lax.ppermute(field, LAT, near)
    crossed = lax.ppermute(field, LAT, across)
    before_near, *close = forward_side(True, field, beside, bias, w_in)
    raw, close = lax.optimization_barrier((raw, close))
    back = prepare_back(*raw)
    crossed, close, back = lax.optimization_barrier((crossed, close, back))
    w_out_back, w_in_back = back
    before_across, *distant = forward_side(False, field, crossed, bias, w_in)
    before_second = (before_near, before_across)
    fields = move(1, field, close, distant, w_out)
    height = steps * slab_rows * channels // members
    chunks = lax.all_to_all(
        fields.reshape(members, height, width), MEMBER, split_axis=0, concat_axis=0, tiled=True
    )
    grads = crps(lat_weights, chunks, targets.reshape(members, height, width))
    grads = lax.all_to_all(grads, MEMBER, split_axis=0, concat_axis=0, tiled=True)
    slopes = slopes_of(*before_first, *before_second)
    first_grads, message, known = collect(grads)

    beside = lax.ppermute(message, LAT, near)
    crossed = lax.ppermute(message, LAT, across)
    opposite = [(i, i ^ 8) for i in range(slabs)]
    ahead = [(i, (i + 5 if i % 2 == 0 else i - 5) % slabs) for i in range(slabs)]
    behind = [(i, (i - 5 if i % 2 == 0 else i + 5) % slabs) for i in range(slabs)]
    distant_tables = [lax.ppermute(known, LAT, pairs) for pairs in (ahead, behind)]
    close = backward_side(1, True, message, beside, slopes, w_out_back)
    crossed, close = lax.optimization_barrier((crossed, close))
    distant = backward_side(1, False, message, crossed, slopes, w_out_back)
    message, known = join(
        message, close, distant, w_in_back, first_grads, beside, crossed, *distant_tables
    )
    beside = lax.ppermute(message, LAT, near)
    crossed = lax.ppermute(message, LAT, across)
    distant_tables = [lax.ppermute(known, LAT, pairs) for pairs in (opposite,)]
    close = backward_side(0, True, message, beside, slopes, w_out_back)
    crossed, close = lax.optimization_barrier((crossed, close))
    distant = backward_side(0, False, message, crossed, slopes, w_out_back)
    count = members * steps * rows * channels * width
    gradient, loss = finish(
        count, message, close, distant, w_in_back, beside, crossed, *distant_tables
    )
    loss = loss.reshape(())
    return gradient.reshape(initial_states.shape), loss


def solution(mesh):
    torus = Mesh(
        mesh.devices.reshape(4, 2, 2, 4, 2), ("member_0", "member_1", "lat_0", "lat_1", "lat_2")
    )
    placed = (P(MEMBER, LAT, None, None), P(None, LAT, None, None), P(LAT), P(), P(), P())
    return jax.shard_map(
        on_device,
        mesh=torus,
        in_specs=placed,
        out_specs=(P(MEMBER, LAT, None, None), P()),
        check_vma=False,
    )
```
